128 devices in a mesh: tx: 8 (over x, core), ty: 16 (over z, y).
Axes of the slice: x: 4, y: 4, z: 4, core: 2. Of those that a mesh axis runs over, the one named last changes fastest.
Arguments:
- granule_blocks: bfloat16 [8192, 13, 16, 128], P(('tx', 'ty')), may hold values from -6 to 6
- row_weights: bfloat16 [8192, 8, 16], P(('tx', 'ty')), may hold values from -1.5 to 1.5
- column_bank: bfloat16 [8, 128, 128], replicated, may hold values from -0.5 to 0.5
- destination: int32 [8192], P(('tx', 'ty')), may hold values from 0 to 127, as said below
- window_index: int32 [8192], P(('tx', 'ty')), may hold values from 0 to 31
- bank_index: int32 [8192], P(('tx', 'ty')), may hold values from 0 to 7
- kernel_one: bfloat16 [3, 3, 13, 64], replicated, may hold values from -1 to 1
- reduce_two: bfloat16 [2, 2, 64, 128], replicated, may hold values from -0.5 to 0.5
- kernel_two: bfloat16 [3, 3, 128, 128], replicated, may hold values from -0.25 to 0.25
- reduce_three: bfloat16 [2, 2, 128, 256], replicated, may hold values from -0.375 to 0.375
- kernel_three: bfloat16 [3, 3, 256, 256], replicated, may hold values from -0.1875 to 0.1875
- reduce_four: bfloat16 [2, 2, 256, 512], replicated, may hold values from -0.25 to 0.25
- kernel_four: bfloat16 [3, 3, 512, 512], replicated, may hold values from -0.125 to 0.125
Outputs:
- gridded: bfloat16 [13, 4096, 1024], P(None, 'ty', 'tx')
- bottleneck: bfloat16 [512, 512, 128], P(None, 'ty', 'tx')
The draws below stay inside these ranges and needn't reach their ends.
Inputs may be any that keep to these rules, and one draw needn't show every extreme that they name: At most 2 of the blocks that one device holds name the same destination; in every draw one destination is named by 2 blocks of every device.
All inputs are finite; a program needn't handle non-finite values.
Results may differ from the reference program's by a relative error of at most 0.015.
Values may be sent and summed in bfloat16 or wider, within the bound.
A program may use at most 128 MiB of HBM per device.

```python
import jax
import jax.numpy as jnp
from jax import lax

CH_ONE = 64
CH_TWO = 128
CH_THREE = 256
CH_FOUR = 512
BANDS = 13
SRC_ROWS = 16
SRC_COLS = 128
WIN_ROWS = 8
TILE_COLS = 128
BANK = 8
CAP = 2
BLK_DEV = 64
TILE_ROWS = 256
TILES = 128
BLOCKS = 8192
NWIN = 32
ROWS = 4096
COLS = 1024
N_TX = 8
N_TY = 16


def draw_destination(key, part):
    key_hot, key_tier, key_score = jax.random.split(key, 3)
    slot_total = TILES * CAP
    hottest = jax.random.randint(key_hot, (), 0, TILES)
    tier_level = jax.random.randint(key_tier, (TILES,), 0, 4)
    slot_ids = jnp.arange(slot_total, dtype=jnp.int32)
    owning = slot_ids // CAP
    scores = jax.random.randint(key_score, (TILES, slot_total), 0, 65536)
    scores = scores + ((3 - tier_level[owning]) * 16384)[None, :]
    scores = scores * slot_total + slot_ids[None, :]
    scores = jnp.where((owning == hottest)[None, :], (slot_ids - slot_total)[None, :], scores)
    ranking = jnp.argsort(scores, axis=1, stable=True)
    chosen = ranking[:, :BLK_DEV]
    return (chosen // CAP).astype(jnp.int32).reshape(BLOCKS)


def with_ends(result, key, low, largest):
    shape = result.shape
    spot = [jax.random.randint(jax.random.fold_in(key, axis), (), 0, shape[axis]) for axis in range(len(shape))]
    result = result.at[tuple(spot)].set(low)
    longest = shape.index(max(shape))
    spot[longest] = (spot[longest] + 1) % shape[longest]
    return result.at[tuple(spot)].set(largest)


def shard_levels(key, dims, shards, low, high):
    level, own = 1.0, jax.random.fold_in(key, 6)
    for dim, blocks in shards:
        heights = jnp.exp(jax.random.uniform(jax.random.fold_in(own, dim), (blocks,), jnp.float32, low / len(shards), high / len(shards)))
        level = level * jnp.repeat(heights, dims[dim] // blocks).reshape([-1 if axis == dim else 1 for axis in range(len(dims))])
    return level


def gaussian(own_key, dims, scale, reach, cuts=(), held_as=jnp.bfloat16):
    entries = scale * jax.random.normal(own_key, dims, jnp.float32)
    if cuts:
        entries = entries * shard_levels(own_key, dims, cuts, -0.22, 0.18)
    return jnp.clip(entries, -reach, reach).astype(held_as)


def setup_inputs(seed: int = 0) -> dict:
    arg_keys = jax.random.split(jax.random.key(seed), 14)
    return {
        "granule_blocks": gaussian(arg_keys[0], (BLOCKS, BANDS, SRC_ROWS, SRC_COLS), 1.0, 6.0, ((0, 128),)),
        "row_weights": gaussian(arg_keys[1], (BLOCKS, WIN_ROWS, SRC_ROWS), SRC_ROWS ** -0.5, 1.5, ((0, 128),)),
        "column_bank": gaussian(arg_keys[2], (BANK, SRC_COLS, TILE_COLS), SRC_COLS ** -0.5, 0.5),
        "destination": draw_destination(jax.random.fold_in(arg_keys[13], 71), 0),
        "window_index": with_ends(jax.random.randint(arg_keys[4], (BLOCKS,), 0, NWIN), jax.random.fold_in(arg_keys[4], 1), 0, NWIN - 1).astype(jnp.int32),
        "bank_index": with_ends(jax.random.randint(arg_keys[5], (BLOCKS,), 0, BANK), jax.random.fold_in(arg_keys[5], 1), 0, BANK - 1).astype(jnp.int32),
        "kernel_one": gaussian(arg_keys[6], (3, 3, BANDS, CH_ONE), (9 * BANDS // 4) ** -0.5, 1.0),
        "reduce_two": gaussian(arg_keys[7], (2, 2, CH_ONE, CH_TWO), (2 * CH_ONE) ** -0.5, 0.5),
        "kernel_two": gaussian(arg_keys[8], (3, 3, CH_TWO, CH_TWO), (9 * CH_TWO // 2) ** -0.5, 0.25),
        "reduce_three": gaussian(arg_keys[9], (2, 2, CH_TWO, CH_THREE), (2 * CH_TWO) ** -0.5, 0.375),
        "kernel_three": gaussian(arg_keys[10], (3, 3, CH_THREE, CH_THREE), (9 * CH_THREE // 2) ** -0.5, 0.1875),
        "reduce_four": gaussian(arg_keys[11], (2, 2, CH_THREE, CH_FOUR), (2 * CH_THREE) ** -0.5, 0.25),
        "kernel_four": gaussian(arg_keys[12], (3, 3, CH_FOUR, CH_FOUR), (9 * CH_FOUR // 2) ** -0.5, 0.125),
    }


def conv_same(field, kernel):
    output = lax.conv_general_dilated(field[None].astype(jnp.float32), kernel.astype(jnp.float32), (1, 1), ((1, 1), (1, 1)), dimension_numbers=("NCHW", "HWIO", "NCHW"), precision=lax.Precision.HIGHEST)[0]
    return jnp.maximum(output, 0.0).astype(jnp.bfloat16)


def reduce_half(field, kernel):
    output = lax.conv_general_dilated(field[None].astype(jnp.float32), kernel.astype(jnp.float32), (2, 2), "VALID", dimension_numbers=("NCHW", "HWIO", "NCHW"), precision=lax.Precision.HIGHEST)[0]
    return jnp.maximum(output, 0.0).astype(jnp.bfloat16)


def reference(granule_blocks, row_weights, column_bank, destination, window_index, bank_index, kernel_one, reduce_two, kernel_two, reduce_three, kernel_three, reduce_four, kernel_four):
    tile_count = N_TX * N_TY
    windows = TILE_ROWS // WIN_ROWS
    segments = tile_count * windows
    raw_parts = granule_blocks.reshape(tile_count, BLK_DEV, BANDS, SRC_ROWS, SRC_COLS)
    weight_parts = row_weights.reshape(tile_count, BLK_DEV, WIN_ROWS, SRC_ROWS)
    dest_parts = destination.reshape(tile_count, BLK_DEV).astype(jnp.int32)
    window_parts = window_index.reshape(tile_count, BLK_DEV).astype(jnp.int32)
    bank_parts = bank_index.reshape(tile_count, BLK_DEV).astype(jnp.int32)

    def step_over(carry, inputs):
        sums, counts = carry
        raw_part, weight_part, dest_part, window_part, bank_part = inputs
        rowed = jnp.einsum("nrk,nbkc->nbrc", weight_part.astype(jnp.float32), raw_part.astype(jnp.float32), precision=lax.Precision.HIGHEST).astype(jnp.bfloat16)
        matrices = column_bank[bank_part].astype(jnp.float32)
        resampled = jnp.einsum("nbrc,nct->nbrt", rowed.astype(jnp.float32), matrices, precision=lax.Precision.HIGHEST).astype(jnp.bfloat16)
        target = (dest_part * windows + window_part).astype(jnp.int32)
        sums = sums + jax.ops.segment_sum(resampled.astype(jnp.float32), target, num_segments=segments)
        counts = counts + jax.ops.segment_sum(jnp.ones((BLK_DEV,), jnp.int32), target, num_segments=segments)
        return (sums, counts), None

    start = (jnp.zeros((segments, BANDS, WIN_ROWS, TILE_COLS), jnp.float32), jnp.zeros((segments,), jnp.int32))
    (sums, counts), unused = lax.scan(step_over, start, (raw_parts, weight_parts, dest_parts, window_parts, bank_parts))
    divisor = jnp.maximum(counts, 1).astype(jnp.float32)
    averaged = sums / divisor[:, None, None, None]
    averaged = averaged.reshape(N_TX, N_TY, windows, BANDS, WIN_ROWS, TILE_COLS)
    gridded = jnp.transpose(averaged, (3, 1, 2, 4, 0, 5)).reshape(BANDS, ROWS, COLS).astype(jnp.bfloat16)
    level_one = conv_same(gridded, kernel_one)
    level_two = conv_same(reduce_half(level_one, reduce_two), kernel_two)
    level_three = conv_same(reduce_half(level_two, reduce_three), kernel_three)
    bottleneck = conv_same(reduce_half(level_three, reduce_four), kernel_four)
    return gridded, bottleneck
```

```python
import functools

import jax
import jax.numpy as jnp
import numpy as np
from jax import lax
from jax.experimental import pallas as pl
from jax.experimental.pallas import tpu as pltpu
from jax.sharding import PartitionSpec as P

MESH = pl.DeviceIdType.MESH
BANDS = 13
CAP = 2
WIN = 8
NWIN = 32
BR = BANDS * WIN
HALO = 16


def resample_kernel(dest, bank_index, raw, weights, bank, out, tiled, res, count, sem):
    step = pl.program_id(0)
    per = raw.shape[0]
    held = res.shape[0]
    lanes = BANDS * 16

    @pl.when(step == 0)
    def _():
        spread = (
            lax.broadcasted_iota(jnp.int32, (16, lanes), 1) % 16
            == lax.broadcasted_iota(jnp.int32, (16, lanes), 0)
        ).astype(jnp.bfloat16)
        tiled[...] = jnp.dot(weights[...], spread, preferred_element_type=jnp.float32)

        @pl.loop(0, count.shape[0])
        def _(t):
            count[t] = 0

    own_band = (
        lax.broadcasted_iota(jnp.int32, (BANDS, WIN, lanes), 2) // 16
        == lax.broadcasted_iota(jnp.int32, (BANDS, WIN, lanes), 0)
    )
    for k in range(per):
        n = step * per + k
        row = tiled[pl.ds(pl.multiple_of(n * WIN, WIN), WIN), :]
        block = jnp.where(own_band, row[None], 0.0).reshape(BR, lanes).astype(jnp.bfloat16)
        rowed = jnp.dot(
            block, raw[k].reshape(lanes, 128), preferred_element_type=jnp.float32
        ).astype(jnp.bfloat16)
        res[n] = jnp.dot(
            rowed, bank[bank_index[n]], preferred_element_type=jnp.float32
        ).astype(jnp.bfloat16)
        tile = dest[n]
        rank = count[tile]
        count[tile] = rank + 1
        pltpu.make_async_copy(res.at[n], out.at[tile * CAP + rank], sem).start()

    @pl.when(step == pl.num_programs(0) - 1)
    def _():
        pltpu.make_async_copy(res, out.at[pl.ds(0, held)], sem).wait()


def resample(raw, weights, bank, dest, bank_index, tiles):
    held = raw.shape[0]
    per = 8
    return pl.pallas_call(
        resample_kernel,
        grid=(held // per,),
        in_specs=[
            pl.BlockSpec(memory_space=pltpu.SMEM),
            pl.BlockSpec(memory_space=pltpu.SMEM),
            pl.BlockSpec((per, BANDS, 16, 128), lambda i: (i, 0, 0, 0)),
            pl.BlockSpec((held * WIN, 16), lambda i: (0, 0)),
            pl.BlockSpec(bank.shape, lambda i: (0, 0, 0)),
        ],
        out_specs=pl.BlockSpec(memory_space=pl.ANY),
        out_shape=jax.ShapeDtypeStruct((tiles * CAP, BR, 128), jnp.bfloat16),
        scratch_shapes=[
            pltpu.VMEM((held * WIN, BANDS * 16), jnp.float32),
            pltpu.VMEM((held, BR, 128), jnp.bfloat16),
            pltpu.SMEM((tiles,), jnp.int32),
            pltpu.SemaphoreType.DMA,
        ],
        compiler_params=pltpu.CompilerParams(vmem_limit_bytes=24 << 20),
        name="resample",
    )(dest, bank_index, raw, weights.reshape(held * WIN, 16), bank)


def gather_kernel(window, got, gridded, turned, acc, count):
    step = pl.program_id(0)
    per = got.shape[0]

    @pl.when(step == 0)
    def _():
        acc[...] = jnp.zeros_like(acc)

        @pl.loop(0, NWIN)
        def _(t):
            count[t] = 0

    @pl.loop(0, per)
    def _(k):
        w = window[step * per + k]

        @pl.when(w >= 0)
        def _():
            acc[w] += got[k].astype(jnp.float32)
            count[w] = count[w] + 1

    @pl.when(step == pl.num_programs(0) - 1)
    def _():
        pad = jnp.zeros((128 - BR, 128), jnp.float32)

        @pl.loop(0, NWIN // 2)
        def _(p):
            pair = []
            for e in range(2):
                w = p * 2 + e
                divisor = jnp.maximum(count[w], 1).astype(jnp.float32)
                mean = acc[w] / jnp.full((BR, 128), divisor, jnp.float32)
                pair.append(mean)
                turned[w] = jnp.concatenate([mean, pad], axis=0).T.astype(jnp.bfloat16)
            for b in range(BANDS):
                rows = slice(b * WIN, (b + 1) * WIN)
                gridded[b, pl.ds(pl.multiple_of(p * 16, 16), 16), :] = jnp.concatenate(
                    [pair[0][rows], pair[1][rows]], axis=0
                ).astype(jnp.bfloat16)


def gather_windows(got, window):
    slots = got.shape[0]
    per = 16
    return pl.pallas_call(
        gather_kernel,
        grid=(slots // per,),
        in_specs=[
            pl.BlockSpec(memory_space=pltpu.SMEM),
            pl.BlockSpec((per, BR, 128), lambda i: (i, 0, 0)),
        ],
        out_specs=[
            pl.BlockSpec((BANDS, NWIN * WIN, 128), lambda i: (0, 0, 0)),
            pl.BlockSpec((NWIN, 128, 128), lambda i: (0, 0, 0)),
        ],
        out_shape=[
            jax.ShapeDtypeStruct((BANDS, NWIN * WIN, 128), jnp.bfloat16),
            jax.ShapeDtypeStruct((NWIN, 128, 128), jnp.bfloat16),
        ],
        scratch_shapes=[
            pltpu.VMEM((NWIN, BR, 128), jnp.float32),
            pltpu.SMEM((NWIN,), jnp.int32),
        ],
        compiler_params=pltpu.CompilerParams(vmem_limit_bytes=24 << 20),
        name="gather_windows",
    )(window, got)


HALO_WIN = HALO // WIN
LAST_WIN = NWIN + HALO_WIN
LAST_COL = 128 + HALO
SIDE = {
    -1: ((0, HALO_WIN), (LAST_WIN, HALO_WIN)),
    0: ((0, NWIN), (HALO_WIN, NWIN)),
    1: ((NWIN - HALO_WIN, HALO_WIN), (0, HALO_WIN)),
}
EDGE = {
    -1: ((0, HALO), (LAST_COL, HALO)),
    0: ((0, 128), (HALO, 128)),
    1: ((128 - HALO, HALO), (0, HALO)),
}
MOVES = [(1, 0), (-1, 0), (0, 1), (0, -1), (1, 1), (1, -1), (-1, 1), (-1, -1)]


def widen_kernel(zeros, tile, wide, own_sem, zero_sem, send_sem, recv_sem):
    tx, ty = lax.axis_index("tx"), lax.axis_index("ty")
    nx, ny = lax.axis_size("tx"), lax.axis_size("ty")

    def inside(dx, dy):
        ok = None
        for d, at, n in ((dx, tx, nx), (dy, ty, ny)):
            if d:
                here = at + d >= 0 if d < 0 else at + d < n
                ok = here if ok is None else jnp.logical_and(ok, here)
        return ok

    def source(dx, dy):
        (w, wn), (c, cn) = SIDE[dy][0], EDGE[dx][0]
        return tile.at[pl.ds(w, wn), pl.ds(c, cn)]

    def target(dx, dy):
        (w, wn), (c, cn) = SIDE[dy][1], EDGE[dx][1]
        return wide.at[pl.ds(w, wn), pl.ds(c, cn)]

    barrier = pltpu.get_barrier_semaphore()
    for dx, dy in MOVES:

        @pl.when(inside(dx, dy))
        def _():
            pl.semaphore_signal(
                barrier, inc=1, device_id=(tx + dx, ty + dy), device_id_type=MESH
            )

    own = pltpu.make_async_copy(tile, target(0, 0), own_sem)
    own.start()
    peers = sum(inside(dx, dy).astype(jnp.int32) for dx, dy in MOVES)
    pl.semaphore_wait(barrier, peers)

    copies = []
    for i, (dx, dy) in enumerate(MOVES):
        send = pltpu.make_async_remote_copy(
            src_ref=source(dx, dy),
            dst_ref=target(dx, dy),
            send_sem=send_sem.at[i],
            recv_sem=recv_sem.at[i],
            device_id=(tx + dx, ty + dy),
            device_id_type=MESH,
        )
        (w, wn), (c, cn) = SIDE[dy][1], EDGE[dx][1]
        blank = pltpu.make_async_copy(
            zeros.at[pl.ds(0, wn), pl.ds(0, cn)], target(dx, dy), zero_sem.at[i]
        )
        copies.append((send, blank, inside(dx, dy), inside(-dx, -dy)))
    for send, blank, goes, comes in copies:

        @pl.when(goes)
        def _():
            send.start()

        @pl.when(jnp.logical_not(comes))
        def _():
            blank.start()

    own.wait()
    for send, blank, goes, comes in copies:

        @pl.when(goes)
        def _():
            send.wait_send()

        @pl.when(comes)
        def _():
            send.wait_recv()

        @pl.when(jnp.logical_not(comes))
        def _():
            blank.wait()


def widen(turned):
    moves = len(MOVES)
    return pl.pallas_call(
        widen_kernel,
        in_specs=[pl.BlockSpec(memory_space=pltpu.VMEM), pl.BlockSpec(memory_space=pl.ANY)],
        out_specs=pl.BlockSpec(memory_space=pl.ANY),
        out_shape=jax.ShapeDtypeStruct(
            (NWIN + 2 * HALO_WIN, 128 + 2 * HALO, 128), jnp.bfloat16
        ),
        scratch_shapes=[
            pltpu.SemaphoreType.DMA,
            pltpu.SemaphoreType.DMA((moves,)),
            pltpu.SemaphoreType.DMA((moves,)),
            pltpu.SemaphoreType.DMA((moves,)),
        ],
        compiler_params=pltpu.CompilerParams(
            collective_id=0, has_side_effects=True, vmem_limit_bytes=16 << 20
        ),
        name="widen",
    )(jnp.zeros((NWIN, 128, 128), jnp.bfloat16), turned)


HALVES = 8
PIX = 80


def level_one_kernel(limits, wide, weight_one, weight_two, out, slab, patch):
    step = pl.program_id(0)
    last = wide.shape[0] - 1
    cols = wide.shape[1]
    low = lax.broadcasted_iota(jnp.int32, (cols, 128), 1) % 8 < 4
    for k in range(HALVES):
        w = step * (HALVES // 2) + k // 2
        here = wide[jnp.minimum(w, last)].astype(jnp.float32)
        if k % 2:
            after = wide[jnp.minimum(w + 1, last)].astype(jnp.float32)
            here = jnp.where(low, pltpu.roll(here, 124, 1), pltpu.roll(after, 4, 1))
        slab[k, pl.ds(0, cols), :] = here
        for q in range(4):
            patch[k, :, q * 128 : (q + 1) * 128] = slab[
                k, pl.ds(1 + q, PIX, stride=2), :
            ].astype(jnp.bfloat16)
    hidden = jnp.dot(
        patch[...].reshape(HALVES * PIX, 512), weight_one[...], preferred_element_type=jnp.float32
    )
    hidden = jnp.maximum(hidden, 0.0).astype(jnp.bfloat16)
    col = lax.broadcasted_iota(jnp.int32, (PIX, 128), 0) - 7
    col_ok = jnp.logical_and(col >= limits[2], col < limits[3])
    for e in range(2):
        down = jnp.dot(
            hidden[:, e * 256 : (e + 1) * 256],
            weight_two[...],
            preferred_element_type=jnp.float32,
        )
        down = jnp.maximum(down, 0.0).reshape(HALVES, PIX, 128)
        for k in range(HALVES):
            row = (step * HALVES + k) * 2 + e - 7
            row_ok = jnp.logical_and(row >= limits[0], row < limits[1])
            keep = jnp.logical_and(col_ok, row_ok)
            out[k * 2 + e] = jnp.where(keep, down[k], 0.0).astype(jnp.bfloat16)


def level_one(wide, weight_one, weight_two, limits):
    steps = 9
    return pl.pallas_call(
        level_one_kernel,
        grid=(steps,),
        in_specs=[
            pl.BlockSpec(memory_space=pltpu.SMEM),
            pl.BlockSpec(wide.shape, lambda i: (0, 0, 0)),
            pl.BlockSpec(weight_one.shape, lambda i: (0, 0)),
            pl.BlockSpec(weight_two.shape, lambda i: (0, 0)),
        ],
        out_specs=pl.BlockSpec((2 * HALVES, PIX, 128), lambda i: (i, 0, 0)),
        out_shape=jax.ShapeDtypeStruct((steps * 2 * HALVES, PIX, 128), jnp.bfloat16),
        scratch_shapes=[
            pltpu.VMEM((HALVES, 168, 128), jnp.float32),
            pltpu.VMEM((HALVES, PIX, 512), jnp.bfloat16),
        ],
        compiler_params=pltpu.CompilerParams(vmem_limit_bytes=32 << 20),
        name="level_one",
    )(limits, wide, weight_one, weight_two)


def patch_weights(kernel):
    rows = np.zeros((8, 4, 3), np.float32)
    for r in range(8):
        for y in range(4):
            u = r - (2 + y) + 1
            if 0 <= u < 3:
                rows[r, y, u] = 1
    cols = np.zeros((4, 2, 3), np.float32)
    for q in range(4):
        for g in range(2):
            v = q - g
            if 0 <= v < 3:
                cols[q, g, v] = 1
    spread = jnp.einsum("ryu,uvbo->rybvo", jnp.asarray(rows, jnp.bfloat16), kernel)
    spread = jnp.einsum("qgv,rybvo->qbrygo", jnp.asarray(cols, jnp.bfloat16), spread)
    spread = spread.reshape(4, BR, 512).astype(jnp.bfloat16)
    return jnp.pad(spread, ((0, 0), (0, 128 - BR), (0, 0))).reshape(512, 512)


def conv(field, kernel, stride):
    out = lax.conv_general_dilated(
        field[None],
        kernel,
        (stride, stride),
        "VALID",
        dimension_numbers=("NHWC", "HWIO", "NHWC"),
        preferred_element_type=jnp.float32,
    )[0]
    return jnp.maximum(out, 0.0)


def on_map(field, halo, tx, ty, nx, ny):
    rows = jnp.arange(field.shape[0]) - halo
    cols = jnp.arange(field.shape[1]) - halo
    r = (rows + ty * (field.shape[0] - 2 * halo) >= 0) & (
        rows + ty * (field.shape[0] - 2 * halo) < ny * (field.shape[0] - 2 * halo)
    )
    c = (cols + tx * (field.shape[1] - 2 * halo) >= 0) & (
        cols + tx * (field.shape[1] - 2 * halo) < nx * (field.shape[1] - 2 * halo)
    )
    return jnp.where((r[:, None] & c[None, :])[:, :, None], field, 0.0)


def body(
    granule_blocks,
    row_weights,
    column_bank,
    destination,
    window_index,
    bank_index,
    kernel_one,
    reduce_two,
    kernel_two,
    reduce_three,
    kernel_three,
    reduce_four,
    kernel_four,
):
    nx, ny = lax.axis_size("tx"), lax.axis_size("ty")
    tx, ty = lax.axis_index("tx"), lax.axis_index("ty")
    tiles = nx * ny
    held = destination.shape[0]
    tags = lax.all_gather(destination * NWIN + window_index, ("tx", "ty"), tiled=False)
    sent = resample(granule_blocks, row_weights, column_bank, destination, bank_index, tiles)
    got = lax.all_to_all(
        sent.reshape(tiles, CAP * BR, 128), ("tx", "ty"), split_axis=0, concat_axis=0, tiled=True
    ).reshape(tiles * CAP, BR, 128)
    tags = tags.reshape(tiles, held)
    mine = tags // NWIN == tx * ny + ty
    code = jnp.arange(held, dtype=jnp.int32)[None, :] * NWIN + tags % NWIN
    hits = jnp.sum(mine.astype(jnp.int32), axis=1)
    first = jnp.min(jnp.where(mine, code, held * NWIN), axis=1)
    second = jnp.max(jnp.where(mine, code, -1), axis=1)
    window = jnp.stack(
        [
            jnp.where(hits >= 1, first % NWIN, -1),
            jnp.where(hits >= 2, second % NWIN, -1),
        ],
        axis=1,
    ).reshape(tiles * CAP)
    gridded, turned = gather_windows(got, window)
    wide = widen(turned)
    far = 1 << 20
    limits = jnp.stack(
        [
            jnp.where(ty == 0, 0, -far),
            jnp.where(ty == ny - 1, 128, far),
            jnp.where(tx == 0, 0, -far),
            jnp.where(tx == nx - 1, 64, far),
        ]
    ).astype(jnp.int32)
    down_two = level_one(wide, patch_weights(kernel_one), reduce_two.reshape(256, 128), limits)
    level_two = conv(down_two[:142, :78], kernel_two, 1).astype(jnp.bfloat16)
    down_three = on_map(conv(level_two, reduce_three, 2), 3, tx, ty, nx, ny).astype(jnp.bfloat16)
    level_three = conv(down_three, kernel_three, 1).astype(jnp.bfloat16)
    down_four = on_map(conv(level_three, reduce_four, 2), 1, tx, ty, nx, ny).astype(jnp.bfloat16)
    bottleneck = conv(down_four, kernel_four, 1).astype(jnp.bfloat16)
    return (gridded, jnp.transpose(bottleneck, (2, 0, 1)))


def solution(mesh):
    in_specs = (
        P(("tx", "ty"), None, None, None),
        P(("tx", "ty"), None, None),
        P(),
        P(("tx", "ty")),
        P(("tx", "ty")),
        P(("tx", "ty")),
        P(),
        P(),
        P(),
        P(),
        P(),
        P(),
        P(),
    )
    out_specs = (P(None, "ty", "tx"), P(None, "ty", "tx"))
    return jax.shard_map(body, mesh=mesh, in_specs=in_specs, out_specs=out_specs, check_vma=False)
```

```python
import functools

import jax
import jax.numpy as jnp
import numpy as np
from jax import lax
from jax.experimental import pallas as pl
from jax.experimental.pallas import tpu as pltpu
from jax.sharding import PartitionSpec as P

MESH = pl.DeviceIdType.MESH
BANDS = 13
CAP = 2
WIN = 8
NWIN = 32
BR = BANDS * WIN
HALO = 16
BIG_VMEM = 56 << 20


def resample_kernel(dest, bank_index, raw, weights, bank, out, tiled, res, count, sem):
    step = pl.program_id(0)
    per = raw.shape[0]
    held = res.shape[0]
    lanes = BANDS * 16

    @pl.when(step == 0)
    def _():
        spread = (
            lax.broadcasted_iota(jnp.int32, (16, lanes), 1) % 16
            == lax.broadcasted_iota(jnp.int32, (16, lanes), 0)
        ).astype(jnp.bfloat16)
        tiled[...] = jnp.dot(weights[...], spread, preferred_element_type=jnp.float32)

        @pl.loop(0, count.shape[0])
        def _(t):
            count[t] = 0

    own_band = (
        lax.broadcasted_iota(jnp.int32, (BANDS, WIN, lanes), 2) // 16
        == lax.broadcasted_iota(jnp.int32, (BANDS, WIN, lanes), 0)
    )
    rowed = []
    for k in range(per):
        n = step * per + k
        row = tiled[pl.ds(pl.multiple_of(n * WIN, WIN), WIN), :]
        block = jnp.where(own_band, row[None], 0.0).reshape(BR, lanes).astype(jnp.bfloat16)
        rowed.append(
            jnp.dot(
                block, raw[k].reshape(lanes, 128), preferred_element_type=jnp.float32
            ).astype(jnp.bfloat16)
        )
    for k in range(per):
        n = step * per + k
        res[n] = jnp.dot(
            rowed[k], bank[bank_index[n]], preferred_element_type=jnp.float32
        ).astype(jnp.bfloat16)
    for k in range(per):
        n = step * per + k
        tile = dest[n]
        rank = count[tile]
        count[tile] = rank + 1
        pltpu.make_async_copy(res.at[n], out.at[tile * CAP + rank], sem).start()

    @pl.when(step == pl.num_programs(0) - 1)
    def _():
        pltpu.make_async_copy(res, out.at[pl.ds(0, held)], sem).wait()


def resample(raw, weights, bank, dest, bank_index, tiles):
    held = raw.shape[0]
    per = 16
    return pl.pallas_call(
        resample_kernel,
        grid=(held // per,),
        in_specs=[
            pl.BlockSpec(memory_space=pltpu.SMEM),
            pl.BlockSpec(memory_space=pltpu.SMEM),
            pl.BlockSpec((per, BANDS, 16, 128), lambda i: (i, 0, 0, 0)),
            pl.BlockSpec((held * WIN, 16), lambda i: (0, 0)),
            pl.BlockSpec(bank.shape, lambda i: (0, 0, 0)),
        ],
        out_specs=pl.BlockSpec(memory_space=pltpu.HBM),
        out_shape=jax.ShapeDtypeStruct((tiles * CAP, BR, 128), jnp.bfloat16),
        scratch_shapes=[
            pltpu.VMEM((held * WIN, BANDS * 16), jnp.float32),
            pltpu.VMEM((held, BR, 128), jnp.bfloat16),
            pltpu.SMEM((tiles,), jnp.int32),
            pltpu.SemaphoreType.DMA,
        ],
        compiler_params=pltpu.CompilerParams(vmem_limit_bytes=BIG_VMEM),
        name="resample",
    )(dest, bank_index, raw, weights.reshape(held * WIN, 16), bank)


def gather_kernel(window, inverse, got, gridded, turned, even, odd):
    step = pl.program_id(0)
    per = got.shape[0]

    @pl.when(step == 0)
    def _():
        even[...] = jnp.zeros_like(even)
        odd[...] = jnp.zeros_like(odd)

    @pl.loop(0, per // 8)
    def _(group):
        for u in range(8):
            k = group * 8 + u
            total = odd if u % 2 else even
            total[window[step * per + k]] += got[k].astype(jnp.float32)

    @pl.when(step == pl.num_programs(0) - 1)
    def _():
        pad = jnp.zeros((128 - BR, 128), jnp.float32)
        for p in range(NWIN // 2):
            pair = []
            for w in (2 * p, 2 * p + 1):
                mean = (even[w] + odd[w]) * inverse[w : w + 1, :]
                pair.append(mean)
                turned[w] = jnp.concatenate([mean, pad], axis=0).astype(jnp.bfloat16).T
            for b in range(BANDS):
                rows = slice(b * WIN, (b + 1) * WIN)
                gridded[b, p * 16 : (p + 1) * 16, :] = jnp.concatenate(
                    [pair[0][rows], pair[1][rows]], axis=0
                ).astype(jnp.bfloat16)


def gather_windows(got, window, inverse):
    slots = got.shape[0]
    per = 64
    return pl.pallas_call(
        gather_kernel,
        grid=(slots // per,),
        in_specs=[
            pl.BlockSpec(memory_space=pltpu.SMEM),
            pl.BlockSpec((NWIN, 128), lambda i: (0, 0)),
            pl.BlockSpec((per, BR, 128), lambda i: (i, 0, 0)),
        ],
        out_specs=[
            pl.BlockSpec((BANDS, NWIN * WIN, 128), lambda i: (0, 0, 0)),
            pl.BlockSpec((NWIN, 128, 128), lambda i: (0, 0, 0)),
        ],
        out_shape=[
            jax.ShapeDtypeStruct((BANDS, NWIN * WIN, 128), jnp.bfloat16),
            jax.ShapeDtypeStruct((NWIN, 128, 128), jnp.bfloat16),
        ],
        scratch_shapes=[pltpu.VMEM((NWIN + 1, BR, 128), jnp.float32)] * 2,
        compiler_params=pltpu.CompilerParams(vmem_limit_bytes=32 << 20),
        name="gather_windows",
    )(window, inverse, got)


HALO_WIN = HALO // WIN
LAST_WIN = NWIN + HALO_WIN
LAST_COL = 128 + HALO
SIDE = {
    -1: ((0, HALO_WIN), (LAST_WIN, HALO_WIN)),
    0: ((0, NWIN), (HALO_WIN, NWIN)),
    1: ((NWIN - HALO_WIN, HALO_WIN), (0, HALO_WIN)),
}
EDGE = {
    -1: ((0, HALO), (LAST_COL, HALO)),
    0: ((0, 128), (HALO, 128)),
    1: ((128 - HALO, HALO), (0, HALO)),
}
MOVES = [(1, 0), (-1, 0), (0, 1), (0, -1), (1, 1), (1, -1), (-1, 1), (-1, -1)]


def widen_kernel(zeros, tile, wide, own_sem, zero_sem, send_sem, recv_sem):
    tx, ty = lax.axis_index("tx"), lax.axis_index("ty")
    nx, ny = lax.axis_size("tx"), lax.axis_size("ty")

    def inside(dx, dy):
        ok = None
        for d, at, n in ((dx, tx, nx), (dy, ty, ny)):
            if d:
                here = at + d >= 0 if d < 0 else at + d < n
                ok = here if ok is None else jnp.logical_and(ok, here)
        return ok

    def source(dx, dy):
        (w, wn), (c, cn) = SIDE[dy][0], EDGE[dx][0]
        return tile.at[pl.ds(w, wn), pl.ds(c, cn)]

    def target(dx, dy):
        (w, wn), (c, cn) = SIDE[dy][1], EDGE[dx][1]
        return wide.at[pl.ds(w, wn), pl.ds(c, cn)]

    barrier = pltpu.get_barrier_semaphore()
    for dx, dy in MOVES:

        @pl.when(inside(dx, dy))
        def _():
            pl.semaphore_signal(
                barrier, inc=1, device_id=(tx + dx, ty + dy), device_id_type=MESH
            )

    own = pltpu.make_async_copy(tile, target(0, 0), own_sem)
    own.start()
    peers = sum(inside(dx, dy).astype(jnp.int32) for dx, dy in MOVES)
    pl.semaphore_wait(barrier, peers)

    copies = []
    for i, (dx, dy) in enumerate(MOVES):
        send = pltpu.make_async_remote_copy(
            src_ref=source(dx, dy),
            dst_ref=target(dx, dy),
            send_sem=send_sem.at[i],
            recv_sem=recv_sem.at[i],
            device_id=(tx + dx, ty + dy),
            device_id_type=MESH,
        )
        (w, wn), (c, cn) = SIDE[dy][1], EDGE[dx][1]
        blank = pltpu.make_async_copy(
            zeros.at[pl.ds(0, wn), pl.ds(0, cn)], target(dx, dy), zero_sem.at[i]
        )
        copies.append((send, blank, inside(dx, dy), inside(-dx, -dy)))
    for send, blank, goes, comes in copies:

        @pl.when(goes)
        def _():
            send.start()

        @pl.when(jnp.logical_not(comes))
        def _():
            blank.start()

    own.wait()
    for send, blank, goes, comes in copies:

        @pl.when(goes)
        def _():
            send.wait_send()

        @pl.when(comes)
        def _():
            send.wait_recv()

        @pl.when(jnp.logical_not(comes))
        def _():
            blank.wait()


def widen(turned):
    moves = len(MOVES)
    return pl.pallas_call(
        widen_kernel,
        in_specs=[pl.BlockSpec(memory_space=pltpu.VMEM), pl.BlockSpec(memory_space=pl.ANY)],
        out_specs=pl.BlockSpec(memory_space=pl.ANY),
        out_shape=jax.ShapeDtypeStruct(
            (NWIN + 2 * HALO_WIN, 128 + 2 * HALO, 128), jnp.bfloat16
        ),
        scratch_shapes=[
            pltpu.SemaphoreType.DMA,
            pltpu.SemaphoreType.DMA((moves,)),
            pltpu.SemaphoreType.DMA((moves,)),
            pltpu.SemaphoreType.DMA((moves,)),
        ],
        compiler_params=pltpu.CompilerParams(
            collective_id=0, has_side_effects=True, vmem_limit_bytes=16 << 20
        ),
        name="widen",
    )(jnp.zeros((NWIN, 128, 128), jnp.bfloat16), turned)


HALVES = 8
PIX = 80


def level_one_kernel(limits, wide, weight_one, weight_two, out, slab, patch):
    step = pl.program_id(0)
    last = wide.shape[0] - 1
    cols = wide.shape[1]
    low = lax.broadcasted_iota(jnp.int32, (cols, 128), 1) % 8 < 4
    for k in range(HALVES):
        w = step * (HALVES // 2) + k // 2
        here = wide[jnp.minimum(w, last)].astype(jnp.float32)
        if k % 2:
            after = wide[jnp.minimum(w + 1, last)].astype(jnp.float32)
            here = jnp.where(low, pltpu.roll(here, 124, 1), pltpu.roll(after, 4, 1))
        slab[k, pl.ds(0, cols), :] = here
        for q in range(4):
            patch[k, :, q * 128 : (q + 1) * 128] = slab[
                k, pl.ds(1 + q, PIX, stride=2), :
            ].astype(jnp.bfloat16)
    hidden = jnp.dot(
        patch[...].reshape(HALVES * PIX, 512), weight_one[...], preferred_element_type=jnp.float32
    )
    hidden = jnp.maximum(hidden, 0.0).astype(jnp.bfloat16)
    col = lax.broadcasted_iota(jnp.int32, (PIX, 128), 0) - 7
    col_ok = jnp.logical_and(col >= limits[2], col < limits[3])
    for e in range(2):
        down = jnp.dot(
            hidden[:, e * 256 : (e + 1) * 256],
            weight_two[...],
            preferred_element_type=jnp.float32,
        )
        down = jnp.maximum(down, 0.0).reshape(HALVES, PIX, 128)
        for k in range(HALVES):
            row = (step * HALVES + k) * 2 + e - 7
            row_ok = jnp.logical_and(row >= limits[0], row < limits[1])
            keep = jnp.logical_and(col_ok, row_ok)
            out[k * 2 + e] = jnp.where(keep, down[k], 0.0).astype(jnp.bfloat16)


def level_one(wide, weight_one, weight_two, limits):
    steps = 9
    return pl.pallas_call(
        level_one_kernel,
        grid=(steps,),
        in_specs=[
            pl.BlockSpec(memory_space=pltpu.SMEM),
            pl.BlockSpec(wide.shape, lambda i: (0, 0, 0)),
            pl.BlockSpec(weight_one.shape, lambda i: (0, 0)),
            pl.BlockSpec(weight_two.shape, lambda i: (0, 0)),
        ],
        out_specs=pl.BlockSpec((2 * HALVES, PIX, 128), lambda i: (i, 0, 0)),
        out_shape=jax.ShapeDtypeStruct((steps * 2 * HALVES, PIX, 128), jnp.bfloat16),
        scratch_shapes=[
            pltpu.VMEM((HALVES, 168, 128), jnp.float32),
            pltpu.VMEM((HALVES, PIX, 512), jnp.bfloat16),
        ],
        compiler_params=pltpu.CompilerParams(vmem_limit_bytes=32 << 20),
        name="level_one",
    )(limits, wide, weight_one, weight_two)


def patch_weights(kernel):
    rows = np.zeros((8, 4, 3), np.float32)
    for r in range(8):
        for y in range(4):
            u = r - (2 + y) + 1
            if 0 <= u < 3:
                rows[r, y, u] = 1
    cols = np.zeros((4, 2, 3), np.float32)
    for q in range(4):
        for g in range(2):
            v = q - g
            if 0 <= v < 3:
                cols[q, g, v] = 1
    spread = jnp.einsum("ryu,uvbo->rybvo", jnp.asarray(rows, jnp.bfloat16), kernel)
    spread = jnp.einsum("qgv,rybvo->qbrygo", jnp.asarray(cols, jnp.bfloat16), spread)
    spread = spread.reshape(4, BR, 512).astype(jnp.bfloat16)
    return jnp.pad(spread, ((0, 0), (0, 128 - BR), (0, 0))).reshape(512, 512)


def conv(field, kernel, stride):
    out = lax.conv_general_dilated(
        field[None],
        kernel,
        (stride, stride),
        "VALID",
        dimension_numbers=("NHWC", "HWIO", "NHWC"),
        preferred_element_type=jnp.float32,
    )[0]
    return jnp.maximum(out, 0.0)


def on_map(field, halo, tx, ty, nx, ny):
    rows = jnp.arange(field.shape[0]) - halo
    cols = jnp.arange(field.shape[1]) - halo
    r = (rows + ty * (field.shape[0] - 2 * halo) >= 0) & (
        rows + ty * (field.shape[0] - 2 * halo) < ny * (field.shape[0] - 2 * halo)
    )
    c = (cols + tx * (field.shape[1] - 2 * halo) >= 0) & (
        cols + tx * (field.shape[1] - 2 * halo) < nx * (field.shape[1] - 2 * halo)
    )
    return jnp.where((r[:, None] & c[None, :])[:, :, None], field, 0.0)


def body(
    granule_blocks,
    row_weights,
    column_bank,
    destination,
    window_index,
    bank_index,
    kernel_one,
    reduce_two,
    kernel_two,
    reduce_three,
    kernel_three,
    reduce_four,
    kernel_four,
):
    nx, ny = lax.axis_size("tx"), lax.axis_size("ty")
    tx, ty = lax.axis_index("tx"), lax.axis_index("ty")
    tiles = nx * ny
    held = destination.shape[0]
    tags = jnp.pad((destination * NWIN + window_index)[None, :], ((0, 15), (0, 128 - held)))
    tags = lax.all_gather(tags, ("tx", "ty"), tiled=True)
    sent = resample(granule_blocks, row_weights, column_bank, destination, bank_index, tiles)
    got = lax.all_to_all(
        sent.reshape(tiles, CAP * BR, 128), ("tx", "ty"), split_axis=0, concat_axis=0, tiled=True
    ).reshape(tiles * CAP, BR, 128)
    tags = tags.reshape(tiles, 16, 128)[:, 0, :held]
    mine = tags // NWIN == tx * ny + ty
    code = jnp.arange(held, dtype=jnp.int32)[None, :] * NWIN + tags % NWIN
    hits = jnp.sum(mine.astype(jnp.int32), axis=1)
    first = jnp.min(jnp.where(mine, code, held * NWIN), axis=1)
    second = jnp.max(jnp.where(mine, code, -1), axis=1)
    window = jnp.stack(
        [
            jnp.where(hits >= 1, first % NWIN, NWIN),
            jnp.where(hits >= 2, second % NWIN, NWIN),
        ],
        axis=1,
    ).reshape(tiles * CAP)
    counts = jnp.sum(
        (window[None, :] == jnp.arange(NWIN, dtype=jnp.int32)[:, None]).astype(jnp.int32), axis=1
    )
    inverse = jnp.broadcast_to(
        (1.0 / jnp.maximum(counts, 1).astype(jnp.float32))[:, None], (NWIN, 128)
    )
    gridded, turned = gather_windows(got, window, inverse)
    wide = widen(turned)
    far = 1 << 20
    limits = jnp.stack(
        [
            jnp.where(ty == 0, 0, -far),
            jnp.where(ty == ny - 1, 128, far),
            jnp.where(tx == 0, 0, -far),
            jnp.where(tx == nx - 1, 64, far),
        ]
    ).astype(jnp.int32)
    down_two = level_one(wide, patch_weights(kernel_one), reduce_two.reshape(256, 128), limits)
    level_two = conv(down_two[:142, :78], kernel_two, 1).astype(jnp.bfloat16)
    down_three = on_map(conv(level_two, reduce_three, 2), 3, tx, ty, nx, ny).astype(jnp.bfloat16)
    level_three = conv(down_three, kernel_three, 1).astype(jnp.bfloat16)
    down_four = on_map(conv(level_three, reduce_four, 2), 1, tx, ty, nx, ny).astype(jnp.bfloat16)
    bottleneck = conv(down_four, kernel_four, 1).astype(jnp.bfloat16)
    return (gridded, jnp.transpose(bottleneck, (2, 0, 1)))


def solution(mesh):
    in_specs = (
        P(("tx", "ty"), None, None, None),
        P(("tx", "ty"), None, None),
        P(),
        P(("tx", "ty")),
        P(("tx", "ty")),
        P(("tx", "ty")),
        P(),
        P(),
        P(),
        P(),
        P(),
        P(),
        P(),
    )
    out_specs = (P(None, "ty", "tx"), P(None, "ty", "tx"))
    return jax.shard_map(body, mesh=mesh, in_specs=in_specs, out_specs=out_specs, check_vma=False)
```

```python
import functools

import jax
import jax.numpy as jnp
import numpy as np
from jax import lax
from jax.experimental import pallas as pl
from jax.experimental.pallas import tpu as pltpu
from jax.sharding import PartitionSpec as P

MESH = pl.DeviceIdType.MESH
BANDS = 13
CAP = 2
WIN = 8
NWIN = 32
BR = BANDS * WIN
HALO = 16
BIG_VMEM = 56 << 20


def resample_kernel(
    dest, window, bank_index, raw, weights, bank, out, tiled, res, tags, tags_out, count, sem, tag_sem
):
    step = pl.program_id(0)
    per = raw.shape[0]
    held = res.shape[0]
    tiles = out.shape[0]
    lanes = BANDS * 16

    @pl.when(step == 0)
    def _():
        spread = (
            lax.broadcasted_iota(jnp.int32, (16, lanes), 1) % 16
            == lax.broadcasted_iota(jnp.int32, (16, lanes), 0)
        ).astype(jnp.bfloat16)
        tiled[...] = jnp.dot(weights[...], spread, preferred_element_type=jnp.float32)
        tags[...] = jnp.full_like(tags, float(NWIN))

        @pl.loop(0, tiles)
        def _(t):
            count[t] = 0

        @pl.loop(0, held)
        def _(n):
            tile = dest[n]
            tags[tile, pl.ds(count[tile], 1), :] = jnp.full((1, 128), window[n], jnp.int32).astype(
                jnp.float32
            )
            count[tile] = count[tile] + 1

        tags_out[...] = tags[...].astype(jnp.bfloat16)
        pltpu.make_async_copy(tags_out, out.at[:, pl.ds(CAP * BR, 8)], tag_sem).start()

        @pl.loop(0, tiles)
        def _(t):
            count[t] = 0

    own_band = (
        lax.broadcasted_iota(jnp.int32, (BANDS, WIN, lanes), 2) // 16
        == lax.broadcasted_iota(jnp.int32, (BANDS, WIN, lanes), 0)
    )
    rowed = []
    for k in range(per):
        n = step * per + k
        row = tiled[pl.ds(pl.multiple_of(n * WIN, WIN), WIN), :]
        block = jnp.where(own_band, row[None], 0.0).reshape(BR, lanes).astype(jnp.bfloat16)
        rowed.append(
            jnp.dot(
                block, raw[k].reshape(lanes, 128), preferred_element_type=jnp.float32
            ).astype(jnp.bfloat16)
        )
    for k in range(per):
        n = step * per + k
        res[n] = jnp.dot(
            rowed[k], bank[bank_index[n]], preferred_element_type=jnp.float32
        ).astype(jnp.bfloat16)
    for k in range(per):
        n = step * per + k
        tile = dest[n]
        rank = count[tile]
        count[tile] = rank + 1
        pltpu.make_async_copy(
            res.at[n], out.at[tile, pl.ds(pl.multiple_of(rank * BR, 8), BR)], sem
        ).start()

    @pl.when(step == pl.num_programs(0) - 1)
    def _():
        pltpu.make_async_copy(res, res, sem).wait()
        pltpu.make_async_copy(tags_out, out.at[:, pl.ds(CAP * BR, 8)], tag_sem).wait()


def resample(raw, weights, bank, dest, window, bank_index, tiles):
    held = raw.shape[0]
    per = 16
    return pl.pallas_call(
        resample_kernel,
        grid=(held // per,),
        in_specs=[
            pl.BlockSpec(memory_space=pltpu.SMEM),
            pl.BlockSpec(memory_space=pltpu.SMEM),
            pl.BlockSpec(memory_space=pltpu.SMEM),
            pl.BlockSpec((per, BANDS, 16, 128), lambda i: (i, 0, 0, 0)),
            pl.BlockSpec((held * WIN, 16), lambda i: (0, 0)),
            pl.BlockSpec(bank.shape, lambda i: (0, 0, 0)),
        ],
        out_specs=pl.BlockSpec(memory_space=pltpu.HBM),
        out_shape=jax.ShapeDtypeStruct((tiles, CAP * BR + 8, 128), jnp.bfloat16),
        scratch_shapes=[
            pltpu.VMEM((held * WIN, BANDS * 16), jnp.float32),
            pltpu.VMEM((held, BR, 128), jnp.bfloat16),
            pltpu.VMEM((tiles, 8, 128), jnp.float32),
            pltpu.VMEM((tiles, 8, 128), jnp.bfloat16),
            pltpu.SMEM((tiles,), jnp.int32),
            pltpu.SemaphoreType.DMA,
            pltpu.SemaphoreType.DMA,
        ],
        compiler_params=pltpu.CompilerParams(vmem_limit_bytes=BIG_VMEM),
        name="resample",
    )(dest, window, bank_index, raw, weights.reshape(held * WIN, 16), bank)


def gather_kernel(
    got, all_got, gridded, turned, even, odd, tags, dense, window, inverse, sem, tag_sem
):
    step = pl.program_id(0)
    per = got.shape[0]
    tiles = all_got.shape[0]

    @pl.when(step == 0)
    def _():
        fetch = pltpu.make_async_copy(all_got.at[:, pl.ds(CAP * BR, 8)], tags, tag_sem)
        fetch.start()
        even[...] = jnp.zeros_like(even)
        odd[...] = jnp.zeros_like(odd)
        fetch.wait()
        lane = lax.broadcasted_iota(jnp.int32, (8, 128), 1)
        total = jnp.zeros((8, 128), jnp.float32)
        for t in range(tiles):
            total = total + jnp.where(lane == t, tags[t].astype(jnp.float32), 0.0)
        dense[...] = total.astype(jnp.int32)
        scalars = pltpu.make_async_copy(dense, window, sem)
        scalars.start()
        which = lax.broadcasted_iota(jnp.int32, (NWIN, 128), 0).astype(jnp.float32)
        hits = jnp.zeros((NWIN, 128), jnp.float32)
        for k in range(CAP):
            hits = hits + jnp.where(which == total[k : k + 1, :], 1.0, 0.0)
        counts = jnp.sum(hits, axis=1, keepdims=True)
        inverse[...] = jnp.broadcast_to(1.0 / jnp.maximum(counts, 1.0), (NWIN, 128))
        scalars.wait()

    @pl.loop(0, per // 4)
    def _(group):
        for u in range(4):
            t = group * 4 + u
            for k, total in ((0, even), (1, odd)):
                total[window[k, step * per + t]] += got[t, k * BR : (k + 1) * BR, :].astype(
                    jnp.float32
                )

    @pl.when(step == pl.num_programs(0) - 1)
    def _():
        pad = jnp.zeros((128 - BR, 128), jnp.float32)
        for p in range(NWIN // 2):
            pair = []
            for w in (2 * p, 2 * p + 1):
                mean = (even[w] + odd[w]) * inverse[w : w + 1, :]
                pair.append(mean)
                turned[w] = jnp.concatenate([mean, pad], axis=0).astype(jnp.bfloat16).T
            for b in range(BANDS):
                rows = slice(b * WIN, (b + 1) * WIN)
                gridded[b, p * 16 : (p + 1) * 16, :] = jnp.concatenate(
                    [pair[0][rows], pair[1][rows]], axis=0
                ).astype(jnp.bfloat16)


def gather_windows(got):
    tiles, rows, _ = got.shape
    per = 32
    return pl.pallas_call(
        gather_kernel,
        grid=(tiles // per,),
        in_specs=[
            pl.BlockSpec((per, rows, 128), lambda i: (i, 0, 0)),
            pl.BlockSpec(memory_space=pl.ANY),
        ],
        out_specs=[
            pl.BlockSpec((BANDS, NWIN * WIN, 128), lambda i: (0, 0, 0)),
            pl.BlockSpec((NWIN, 128, 128), lambda i: (0, 0, 0)),
        ],
        out_shape=[
            jax.ShapeDtypeStruct((BANDS, NWIN * WIN, 128), jnp.bfloat16),
            jax.ShapeDtypeStruct((NWIN, 128, 128), jnp.bfloat16),
        ],
        scratch_shapes=[
            pltpu.VMEM((NWIN + 1, BR, 128), jnp.float32),
            pltpu.VMEM((NWIN + 1, BR, 128), jnp.float32),
            pltpu.VMEM((tiles, 8, 128), jnp.bfloat16),
            pltpu.VMEM((8, 128), jnp.int32),
            pltpu.SMEM((8, 128), jnp.int32),
            pltpu.VMEM((NWIN, 128), jnp.float32),
            pltpu.SemaphoreType.DMA,
            pltpu.SemaphoreType.DMA,
        ],
        compiler_params=pltpu.CompilerParams(vmem_limit_bytes=32 << 20),
        name="gather_windows",
    )(got, got)


HALO_WIN = HALO // WIN
LAST_WIN = NWIN + HALO_WIN
LAST_COL = 128 + HALO
SIDE = {
    -1: ((0, HALO_WIN), (LAST_WIN, HALO_WIN)),
    0: ((0, NWIN), (HALO_WIN, NWIN)),
    1: ((NWIN - HALO_WIN, HALO_WIN), (0, HALO_WIN)),
}
EDGE = {
    -1: ((0, HALO), (LAST_COL, HALO)),
    0: ((0, 128), (HALO, 128)),
    1: ((128 - HALO, HALO), (0, HALO)),
}
MOVES = [(1, 0), (-1, 0), (0, 1), (0, -1), (1, 1), (1, -1), (-1, 1), (-1, -1)]


def widen_kernel(zeros, tile, wide, own_sem, zero_sem, send_sem, recv_sem):
    tx, ty = lax.axis_index("tx"), lax.axis_index("ty")
    nx, ny = lax.axis_size("tx"), lax.axis_size("ty")

    def inside(dx, dy):
        ok = None
        for d, at, n in ((dx, tx, nx), (dy, ty, ny)):
            if d:
                here = at + d >= 0 if d < 0 else at + d < n
                ok = here if ok is None else jnp.logical_and(ok, here)
        return ok

    def source(dx, dy):
        (w, wn), (c, cn) = SIDE[dy][0], EDGE[dx][0]
        return tile.at[pl.ds(w, wn), pl.ds(c, cn)]

    def target(dx, dy):
        (w, wn), (c, cn) = SIDE[dy][1], EDGE[dx][1]
        return wide.at[pl.ds(w, wn), pl.ds(c, cn)]

    barrier = pltpu.get_barrier_semaphore()
    for dx, dy in MOVES:

        @pl.when(inside(dx, dy))
        def _():
            pl.semaphore_signal(
                barrier, inc=1, device_id=(tx + dx, ty + dy), device_id_type=MESH
            )

    own = pltpu.make_async_copy(tile, target(0, 0), own_sem)
    own.start()
    peers = sum(inside(dx, dy).astype(jnp.int32) for dx, dy in MOVES)
    pl.semaphore_wait(barrier, peers)

    copies = []
    for i, (dx, dy) in enumerate(MOVES):
        send = pltpu.make_async_remote_copy(
            src_ref=source(dx, dy),
            dst_ref=target(dx, dy),
            send_sem=send_sem.at[i],
            recv_sem=recv_sem.at[i],
            device_id=(tx + dx, ty + dy),
            device_id_type=MESH,
        )
        (w, wn), (c, cn) = SIDE[dy][1], EDGE[dx][1]
        blank = pltpu.make_async_copy(
            zeros.at[pl.ds(0, wn), pl.ds(0, cn)], target(dx, dy), zero_sem.at[i]
        )
        copies.append((send, blank, inside(dx, dy), inside(-dx, -dy)))
    for send, blank, goes, comes in copies:

        @pl.when(goes)
        def _():
            send.start()

        @pl.when(jnp.logical_not(comes))
        def _():
            blank.start()

    own.wait()
    for send, blank, goes, comes in copies:

        @pl.when(goes)
        def _():
            send.wait_send()

        @pl.when(comes)
        def _():
            send.wait_recv()

        @pl.when(jnp.logical_not(comes))
        def _():
            blank.wait()


def widen(turned):
    moves = len(MOVES)
    return pl.pallas_call(
        widen_kernel,
        in_specs=[pl.BlockSpec(memory_space=pltpu.VMEM), pl.BlockSpec(memory_space=pl.ANY)],
        out_specs=pl.BlockSpec(memory_space=pl.ANY),
        out_shape=jax.ShapeDtypeStruct(
            (NWIN + 2 * HALO_WIN, 128 + 2 * HALO, 128), jnp.bfloat16
        ),
        scratch_shapes=[
            pltpu.SemaphoreType.DMA,
            pltpu.SemaphoreType.DMA((moves,)),
            pltpu.SemaphoreType.DMA((moves,)),
            pltpu.SemaphoreType.DMA((moves,)),
        ],
        compiler_params=pltpu.CompilerParams(
            collective_id=0, has_side_effects=True, vmem_limit_bytes=16 << 20
        ),
        name="widen",
    )(jnp.zeros((NWIN, 128, 128), jnp.bfloat16), turned)


HALVES = 8
PIX = 80


def level_one_kernel(limits, wide, weight_one, weight_two, out, slab, patch):
    step = pl.program_id(0)
    last = wide.shape[0] - 1
    cols = wide.shape[1]
    low = lax.broadcasted_iota(jnp.int32, (cols, 128), 1) % 8 < 4
    for k in range(HALVES):
        w = step * (HALVES // 2) + k // 2
        here = wide[jnp.minimum(w, last)].astype(jnp.float32)
        if k % 2:
            after = wide[jnp.minimum(w + 1, last)].astype(jnp.float32)
            here = jnp.where(low, pltpu.roll(here, 124, 1), pltpu.roll(after, 4, 1))
        slab[k, pl.ds(0, cols), :] = here
        for q in range(4):
            patch[k, :, q * 128 : (q + 1) * 128] = slab[
                k, pl.ds(1 + q, PIX, stride=2), :
            ].astype(jnp.bfloat16)
    hidden = jnp.dot(
        patch[...].reshape(HALVES * PIX, 512), weight_one[...], preferred_element_type=jnp.float32
    )
    hidden = jnp.maximum(hidden, 0.0).astype(jnp.bfloat16)
    col = lax.broadcasted_iota(jnp.int32, (PIX, 128), 0) - 7
    col_ok = jnp.logical_and(col >= limits[2], col < limits[3])
    for e in range(2):
        down = jnp.dot(
            hidden[:, e * 256 : (e + 1) * 256],
            weight_two[...],
            preferred_element_type=jnp.float32,
        )
        down = jnp.maximum(down, 0.0).reshape(HALVES, PIX, 128)
        for k in range(HALVES):
            row = (step * HALVES + k) * 2 + e - 7
            row_ok = jnp.logical_and(row >= limits[0], row < limits[1])
            keep = jnp.logical_and(col_ok, row_ok)
            out[k * 2 + e] = jnp.where(keep, down[k], 0.0).astype(jnp.bfloat16)


def level_one(wide, weight_one, weight_two, limits):
    steps = 9
    return pl.pallas_call(
        level_one_kernel,
        grid=(steps,),
        in_specs=[
            pl.BlockSpec(memory_space=pltpu.SMEM),
            pl.BlockSpec(wide.shape, lambda i: (0, 0, 0)),
            pl.BlockSpec(weight_one.shape, lambda i: (0, 0)),
            pl.BlockSpec(weight_two.shape, lambda i: (0, 0)),
        ],
        out_specs=pl.BlockSpec((2 * HALVES, PIX, 128), lambda i: (i, 0, 0)),
        out_shape=jax.ShapeDtypeStruct((steps * 2 * HALVES, PIX, 128), jnp.bfloat16),
        scratch_shapes=[
            pltpu.VMEM((HALVES, 168, 128), jnp.float32),
            pltpu.VMEM((HALVES, PIX, 512), jnp.bfloat16),
        ],
        compiler_params=pltpu.CompilerParams(vmem_limit_bytes=32 << 20),
        name="level_one",
    )(limits, wide, weight_one, weight_two)


def patch_weights(kernel):
    rows = np.zeros((8, 4, 3), np.float32)
    for r in range(8):
        for y in range(4):
            u = r - (2 + y) + 1
            if 0 <= u < 3:
                rows[r, y, u] = 1
    cols = np.zeros((4, 2, 3), np.float32)
    for q in range(4):
        for g in range(2):
            v = q - g
            if 0 <= v < 3:
                cols[q, g, v] = 1
    spread = jnp.einsum("ryu,uvbo->rybvo", jnp.asarray(rows, jnp.bfloat16), kernel)
    spread = jnp.einsum("qgv,rybvo->qbrygo", jnp.asarray(cols, jnp.bfloat16), spread)
    spread = spread.reshape(4, BR, 512).astype(jnp.bfloat16)
    return jnp.pad(spread, ((0, 0), (0, 128 - BR), (0, 0))).reshape(512, 512)


def conv(field, kernel, stride):
    out = lax.conv_general_dilated(
        field[None],
        kernel,
        (stride, stride),
        "VALID",
        dimension_numbers=("NHWC", "HWIO", "NHWC"),
        preferred_element_type=jnp.float32,
    )[0]
    return jnp.maximum(out, 0.0)


def on_map(field, halo, tx, ty, nx, ny):
    rows = jnp.arange(field.shape[0]) - halo
    cols = jnp.arange(field.shape[1]) - halo
    r = (rows + ty * (field.shape[0] - 2 * halo) >= 0) & (
        rows + ty * (field.shape[0] - 2 * halo) < ny * (field.shape[0] - 2 * halo)
    )
    c = (cols + tx * (field.shape[1] - 2 * halo) >= 0) & (
        cols + tx * (field.shape[1] - 2 * halo) < nx * (field.shape[1] - 2 * halo)
    )
    return jnp.where((r[:, None] & c[None, :])[:, :, None], field, 0.0)


def body(
    granule_blocks,
    row_weights,
    column_bank,
    destination,
    window_index,
    bank_index,
    kernel_one,
    reduce_two,
    kernel_two,
    reduce_three,
    kernel_three,
    reduce_four,
    kernel_four,
):
    nx, ny = lax.axis_size("tx"), lax.axis_size("ty")
    tx, ty = lax.axis_index("tx"), lax.axis_index("ty")
    tiles = nx * ny
    sent = resample(
        granule_blocks, row_weights, column_bank, destination, window_index, bank_index, tiles
    )
    got = lax.all_to_all(sent, ("tx", "ty"), split_axis=0, concat_axis=0, tiled=True)
    gridded, turned = gather_windows(got)
    wide = widen(turned)
    far = 1 << 20
    limits = jnp.stack(
        [
            jnp.where(ty == 0, 0, -far),
            jnp.where(ty == ny - 1, 128, far),
            jnp.where(tx == 0, 0, -far),
            jnp.where(tx == nx - 1, 64, far),
        ]
    ).astype(jnp.int32)
    down_two = level_one(wide, patch_weights(kernel_one), reduce_two.reshape(256, 128), limits)
    level_two = conv(down_two[:142, :78], kernel_two, 1).astype(jnp.bfloat16)
    down_three = on_map(conv(level_two, reduce_three, 2), 3, tx, ty, nx, ny).astype(jnp.bfloat16)
    level_three = conv(down_three, kernel_three, 1).astype(jnp.bfloat16)
    down_four = on_map(conv(level_three, reduce_four, 2), 1, tx, ty, nx, ny).astype(jnp.bfloat16)
    bottleneck = conv(down_four, kernel_four, 1).astype(jnp.bfloat16)
    return (gridded, jnp.transpose(bottleneck, (2, 0, 1)))


def solution(mesh):
    in_specs = (
        P(("tx", "ty"), None, None, None),
        P(("tx", "ty"), None, None),
        P(),
        P(("tx", "ty")),
        P(("tx", "ty")),
        P(("tx", "ty")),
        P(),
        P(),
        P(),
        P(),
        P(),
        P(),
        P(),
    )
    out_specs = (P(None, "ty", "tx"), P(None, "ty", "tx"))
    return jax.shard_map(body, mesh=mesh, in_specs=in_specs, out_specs=out_specs, check_vma=False)
```

```python
import functools

import jax
import jax.numpy as jnp
import numpy as np
from jax import lax
from jax.experimental import pallas as pl
from jax.experimental.pallas import tpu as pltpu
from jax.sharding import PartitionSpec as P

MESH = pl.DeviceIdType.MESH
BANDS = 13
CAP = 2
WIN = 8
NWIN = 32
BR = BANDS * WIN
HALO = 16
BIG_VMEM = 56 << 20


def resample_kernel(
    dest, window, bank_index, raw, weights, bank, out, tiled, res, tags, tags_out, count, sem, tag_sem
):
    step = pl.program_id(0)
    per = raw.shape[0]
    held = res.shape[0]
    tiles = out.shape[0]
    lanes = BANDS * 16

    @pl.when(step == 0)
    def _():
        spread = (
            lax.broadcasted_iota(jnp.int32, (16, lanes), 1) % 16
            == lax.broadcasted_iota(jnp.int32, (16, lanes), 0)
        ).astype(jnp.bfloat16)
        tiled[...] = jnp.dot(weights[...], spread, preferred_element_type=jnp.float32)
        tags[...] = jnp.full_like(tags, float(NWIN))

        @pl.loop(0, tiles)
        def _(t):
            count[t] = 0

        @pl.loop(0, held)
        def _(n):
            tile = dest[n]
            tags[tile, pl.ds(count[tile], 1), :] = jnp.full((1, 128), window[n], jnp.int32).astype(
                jnp.float32
            )
            count[tile] = count[tile] + 1

        tags_out[...] = tags[...].astype(jnp.bfloat16)
        pltpu.make_async_copy(tags_out, out.at[:, pl.ds(CAP * BR, 8)], tag_sem).start()

        @pl.loop(0, tiles)
        def _(t):
            count[t] = 0

    own_band = (
        lax.broadcasted_iota(jnp.int32, (BANDS, WIN, lanes), 2) // 16
        == lax.broadcasted_iota(jnp.int32, (BANDS, WIN, lanes), 0)
    )
    rowed = []
    for k in range(per):
        n = step * per + k
        row = tiled[pl.ds(pl.multiple_of(n * WIN, WIN), WIN), :]
        block = jnp.where(own_band, row[None], 0.0).reshape(BR, lanes).astype(jnp.bfloat16)
        rowed.append(
            jnp.dot(
                block, raw[k].reshape(lanes, 128), preferred_element_type=jnp.float32
            ).astype(jnp.bfloat16)
        )
    for k in range(per):
        n = step * per + k
        res[n] = jnp.dot(
            rowed[k], bank[bank_index[n]], preferred_element_type=jnp.float32
        ).astype(jnp.bfloat16)
    for k in range(per):
        n = step * per + k
        tile = dest[n]
        rank = count[tile]
        count[tile] = rank + 1
        pltpu.make_async_copy(
            res.at[n], out.at[tile, pl.ds(pl.multiple_of(rank * BR, 8), BR)], sem
        ).start()

    @pl.when(step == pl.num_programs(0) - 1)
    def _():
        pltpu.make_async_copy(res, res, sem).wait()
        pltpu.make_async_copy(tags_out, out.at[:, pl.ds(CAP * BR, 8)], tag_sem).wait()


def resample(raw, weights, bank, dest, window, bank_index, tiles):
    held = raw.shape[0]
    per = 16
    return pl.pallas_call(
        resample_kernel,
        grid=(held // per,),
        in_specs=[
            pl.BlockSpec(memory_space=pltpu.SMEM),
            pl.BlockSpec(memory_space=pltpu.SMEM),
            pl.BlockSpec(memory_space=pltpu.SMEM),
            pl.BlockSpec((per, BANDS, 16, 128), lambda i: (i, 0, 0, 0)),
            pl.BlockSpec((held * WIN, 16), lambda i: (0, 0)),
            pl.BlockSpec(bank.shape, lambda i: (0, 0, 0)),
        ],
        out_specs=pl.BlockSpec(memory_space=pltpu.HBM),
        out_shape=jax.ShapeDtypeStruct((tiles, CAP * BR + 8, 128), jnp.bfloat16),
        scratch_shapes=[
            pltpu.VMEM((held * WIN, BANDS * 16), jnp.float32),
            pltpu.VMEM((held, BR, 128), jnp.bfloat16),
            pltpu.VMEM((tiles, 8, 128), jnp.float32),
            pltpu.VMEM((tiles, 8, 128), jnp.bfloat16),
            pltpu.SMEM((tiles,), jnp.int32),
            pltpu.SemaphoreType.DMA,
            pltpu.SemaphoreType.DMA,
        ],
        compiler_params=pltpu.CompilerParams(vmem_limit_bytes=BIG_VMEM),
        name="resample",
    )(dest, window, bank_index, raw, weights.reshape(held * WIN, 16), bank)


def gather_kernel(
    got, all_got, gridded, turned, even, odd, tags, dense, window, inverse, sem, tag_sem
):
    step = pl.program_id(0)
    per = got.shape[0]
    tiles = all_got.shape[0]

    @pl.when(step == 0)
    def _():
        fetch = pltpu.make_async_copy(all_got.at[:, pl.ds(CAP * BR, 8)], tags, tag_sem)
        fetch.start()
        even[...] = jnp.zeros_like(even)
        odd[...] = jnp.zeros_like(odd)
        fetch.wait()
        lane = lax.broadcasted_iota(jnp.int32, (8, 128), 1)
        total = jnp.zeros((8, 128), jnp.float32)
        for t in range(tiles):
            total = total + jnp.where(lane == t, tags[t].astype(jnp.float32), 0.0)
        dense[...] = total.astype(jnp.int32)
        scalars = pltpu.make_async_copy(dense, window, sem)
        scalars.start()
        which = lax.broadcasted_iota(jnp.int32, (NWIN, 128), 0).astype(jnp.float32)
        hits = jnp.zeros((NWIN, 128), jnp.float32)
        for k in range(CAP):
            hits = hits + jnp.where(which == total[k : k + 1, :], 1.0, 0.0)
        counts = jnp.sum(hits, axis=1, keepdims=True)
        inverse[...] = jnp.broadcast_to(1.0 / jnp.maximum(counts, 1.0), (NWIN, 128))
        scalars.wait()

    @pl.loop(0, per // 4)
    def _(group):
        for u in range(4):
            t = group * 4 + u
            for k, total in ((0, even), (1, odd)):
                total[window[k, step * per + t]] += got[t, k * BR : (k + 1) * BR, :].astype(
                    jnp.float32
                )

    @pl.when(step == pl.num_programs(0) - 1)
    def _():
        pad = jnp.zeros((128 - BR, 128), jnp.float32)
        for p in range(NWIN // 2):
            pair = []
            for w in (2 * p, 2 * p + 1):
                mean = (even[w] + odd[w]) * inverse[w : w + 1, :]
                pair.append(mean)
                turned[w] = jnp.concatenate([mean, pad], axis=0).astype(jnp.bfloat16).T
            for b in range(BANDS):
                rows = slice(b * WIN, (b + 1) * WIN)
                gridded[b, p * 16 : (p + 1) * 16, :] = jnp.concatenate(
                    [pair[0][rows], pair[1][rows]], axis=0
                ).astype(jnp.bfloat16)


def gather_windows(got):
    tiles, rows, _ = got.shape
    per = 32
    return pl.pallas_call(
        gather_kernel,
        grid=(tiles // per,),
        in_specs=[
            pl.BlockSpec((per, rows, 128), lambda i: (i, 0, 0)),
            pl.BlockSpec(memory_space=pl.ANY),
        ],
        out_specs=[
            pl.BlockSpec((BANDS, NWIN * WIN, 128), lambda i: (0, 0, 0)),
            pl.BlockSpec((NWIN, 128, 128), lambda i: (0, 0, 0)),
        ],
        out_shape=[
            jax.ShapeDtypeStruct((BANDS, NWIN * WIN, 128), jnp.bfloat16),
            jax.ShapeDtypeStruct((NWIN, 128, 128), jnp.bfloat16),
        ],
        scratch_shapes=[
            pltpu.VMEM((NWIN + 1, BR, 128), jnp.float32),
            pltpu.VMEM((NWIN + 1, BR, 128), jnp.float32),
            pltpu.VMEM((tiles, 8, 128), jnp.bfloat16),
            pltpu.VMEM((8, 128), jnp.int32),
            pltpu.SMEM((8, 128), jnp.int32),
            pltpu.VMEM((NWIN, 128), jnp.float32),
            pltpu.SemaphoreType.DMA,
            pltpu.SemaphoreType.DMA,
        ],
        compiler_params=pltpu.CompilerParams(vmem_limit_bytes=32 << 20),
        name="gather_windows",
    )(got, got)


HALO_WIN = HALO // WIN
LAST_WIN = NWIN + HALO_WIN
LAST_COL = 128 + HALO
SIDE = {
    -1: ((0, HALO_WIN), (LAST_WIN, HALO_WIN)),
    0: ((0, NWIN), (HALO_WIN, NWIN)),
    1: ((NWIN - HALO_WIN, HALO_WIN), (0, HALO_WIN)),
}
EDGE = {
    -1: ((0, HALO), (LAST_COL, HALO)),
    0: ((0, 128), (HALO, 128)),
    1: ((128 - HALO, HALO), (0, HALO)),
}
MOVES = [(1, 0), (-1, 0), (0, 1), (0, -1), (1, 1), (1, -1), (-1, 1), (-1, -1)]


def widen_kernel(zeros, tile, wide, own_sem, zero_sem, send_sem, recv_sem):
    tx, ty = lax.axis_index("tx"), lax.axis_index("ty")
    nx, ny = lax.axis_size("tx"), lax.axis_size("ty")

    def inside(dx, dy):
        ok = None
        for d, at, n in ((dx, tx, nx), (dy, ty, ny)):
            if d:
                here = at + d >= 0 if d < 0 else at + d < n
                ok = here if ok is None else jnp.logical_and(ok, here)
        return ok

    def source(dx, dy):
        (w, wn), (c, cn) = SIDE[dy][0], EDGE[dx][0]
        return tile.at[pl.ds(w, wn), pl.ds(c, cn)]

    def target(dx, dy):
        (w, wn), (c, cn) = SIDE[dy][1], EDGE[dx][1]
        return wide.at[pl.ds(w, wn), pl.ds(c, cn)]

    barrier = pltpu.get_barrier_semaphore()
    for dx, dy in MOVES:

        @pl.when(inside(dx, dy))
        def _():
            pl.semaphore_signal(
                barrier, inc=1, device_id=(tx + dx, ty + dy), device_id_type=MESH
            )

    own = pltpu.make_async_copy(tile, target(0, 0), own_sem)
    own.start()
    peers = sum(inside(dx, dy).astype(jnp.int32) for dx, dy in MOVES)
    pl.semaphore_wait(barrier, peers)

    copies = []
    for i, (dx, dy) in enumerate(MOVES):
        send = pltpu.make_async_remote_copy(
            src_ref=source(dx, dy),
            dst_ref=target(dx, dy),
            send_sem=send_sem.at[i],
            recv_sem=recv_sem.at[i],
            device_id=(tx + dx, ty + dy),
            device_id_type=MESH,
        )
        (w, wn), (c, cn) = SIDE[dy][1], EDGE[dx][1]
        blank = pltpu.make_async_copy(
            zeros.at[pl.ds(0, wn), pl.ds(0, cn)], target(dx, dy), zero_sem.at[i]
        )
        copies.append((send, blank, inside(dx, dy), inside(-dx, -dy)))
    for send, blank, goes, comes in copies:

        @pl.when(goes)
        def _():
            send.start()

        @pl.when(jnp.logical_not(comes))
        def _():
            blank.start()

    own.wait()
    for send, blank, goes, comes in copies:

        @pl.when(goes)
        def _():
            send.wait_send()

        @pl.when(comes)
        def _():
            send.wait_recv()

        @pl.when(jnp.logical_not(comes))
        def _():
            blank.wait()


def widen(turned):
    moves = len(MOVES)
    return pl.pallas_call(
        widen_kernel,
        in_specs=[pl.BlockSpec(memory_space=pltpu.VMEM), pl.BlockSpec(memory_space=pl.ANY)],
        out_specs=pl.BlockSpec(memory_space=pl.ANY),
        out_shape=jax.ShapeDtypeStruct(
            (NWIN + 2 * HALO_WIN, 128 + 2 * HALO, 128), jnp.bfloat16
        ),
        scratch_shapes=[
            pltpu.SemaphoreType.DMA,
            pltpu.SemaphoreType.DMA((moves,)),
            pltpu.SemaphoreType.DMA((moves,)),
            pltpu.SemaphoreType.DMA((moves,)),
        ],
        compiler_params=pltpu.CompilerParams(
            collective_id=0, has_side_effects=True, vmem_limit_bytes=16 << 20
        ),
        name="widen",
    )(jnp.zeros((NWIN, 128, 128), jnp.bfloat16), turned)


FAR = 1 << 20
HALVES = 8
STEPS_ONE = 9
PAIRS = 40
PIX = 2 * PAIRS
ROWS_TWO = STEPS_ONE * HALVES
ROWS_THREE = 10
STEPS_THREE = 7
ROWS_FOUR = 6
STEPS_FOUR = 6
WIDE_FOUR = 24


def encoder_kernel(
    edges,
    wide,
    weight_one,
    reduce_two,
    hbm_two,
    hbm_reduce_three,
    hbm_three,
    hbm_reduce_four,
    hbm_four,
    out,
    slab,
    patch,
    even_two,
    odd_two,
    carry_two,
    even_three,
    odd_three,
    carry_three,
    spread_three,
    taps_four,
    weight_two,
    reduce_three,
    weight_three,
    reduce_four,
    weight_four,
    sems,
):
    fetches = [
        pltpu.make_async_copy(source, target, sems.at[i])
        for i, (source, target) in enumerate(
            (
                (hbm_two, weight_two),
                (hbm_reduce_three, reduce_three),
                (hbm_three, weight_three),
                (hbm_reduce_four, reduce_four),
                (hbm_four, weight_four),
            )
        )
    ]
    for fetch in fetches:
        fetch.start()

    def dot(a, b):
        return jnp.dot(a, b, preferred_element_type=jnp.float32)

    def bounds(tile_rows, tile_cols):
        return (
            jnp.where(edges[0] == 1, 0, -FAR),
            jnp.where(edges[1] == 1, tile_rows, FAR),
            jnp.where(edges[2] == 1, 0, -FAR),
            jnp.where(edges[3] == 1, tile_cols, FAR),
        )

    def on_map(value, row, col, limits):
        top, bottom, left, right = limits
        right = jnp.where(jnp.logical_and(row >= top, row < bottom), right, -FAR)
        return jnp.where(jnp.logical_and(col >= left, col < right), value, 0.0)

    def following(value, by):
        return pltpu.roll(value, value.shape[0] - by, 0)

    last = wide.shape[0] - 1
    cols = wide.shape[1]
    low = lax.broadcasted_iota(jnp.int32, (cols, 128), 1) % 8 < 4
    at = lax.broadcasted_iota(jnp.int32, (PIX, 128), 0)
    col_two = jnp.where(at < PAIRS, 2 * at, 2 * (at - PAIRS) + 1) - 7
    limits_two = bounds(128, 64)
    carry_two[...] = jnp.zeros_like(carry_two)

    @pl.loop(0, STEPS_ONE)
    def _(step):
        for k in range(HALVES):
            w = step * (HALVES // 2) + k // 2
            here = wide[jnp.minimum(w, last)].astype(jnp.float32)
            if k % 2:
                after = wide[jnp.minimum(w + 1, last)].astype(jnp.float32)
                here = jnp.where(low, pltpu.roll(here, 124, 1), pltpu.roll(after, 4, 1))
            slab[k, pl.ds(0, cols), :] = here
            for q in range(4):
                both = [slab[k, pl.ds(first + q, PAIRS, stride=4), :] for first in (1, 3)]
                patch[k, :, q * 128 : (q + 1) * 128] = jnp.concatenate(both, axis=0).astype(
                    jnp.bfloat16
                )
        hidden = dot(patch[...].reshape(HALVES * PIX, 512), weight_one[...])
        hidden = jnp.maximum(hidden, 0.0).astype(jnp.bfloat16)
        down = [
            jnp.maximum(dot(hidden[:, e * 256 : (e + 1) * 256], reduce_two[...]), 0.0).reshape(
                HALVES, PIX, 128
            )
            for e in range(2)
        ]
        before = carry_two[...]
        for k in range(HALVES):
            h = step * HALVES + k
            lines = []
            for e in range(2):
                value = on_map(down[e][k], 2 * h + e - 7, col_two, limits_two)
                first, second = value[:PAIRS], value[PAIRS:]
                lines.append(
                    jnp.concatenate(
                        [first, second, following(first, 1), following(second, 1)], axis=1
                    )
                )
            even_two[h] = jnp.concatenate(lines, axis=0).astype(jnp.bfloat16)
            odd_two[h] = jnp.concatenate([before, lines[0]], axis=0).astype(jnp.bfloat16)
            before = lines[1]
        carry_two[...] = before

    fetches[0].wait()
    fetches[1].wait()
    col_three = lax.broadcasted_iota(jnp.int32, (PAIRS, 256), 0) - 3
    limits_three = bounds(64, 32)
    carry_three[...] = jnp.zeros_like(carry_three)
    size = ROWS_THREE * PIX

    @pl.loop(0, STEPS_THREE)
    def _(step):
        first = step * ROWS_THREE
        hidden = (
            dot(even_two[pl.ds(first, ROWS_THREE)].reshape(size, 512), weight_two[0])
            + dot(odd_two[pl.ds(first + 1, ROWS_THREE)].reshape(size, 512), weight_two[1])
            + dot(even_two[pl.ds(first + 1, ROWS_THREE)].reshape(size, 512), weight_two[2])
        )
        hidden = jnp.maximum(hidden, 0.0).reshape(ROWS_THREE, 2, PAIRS, 256)
        hidden = jnp.concatenate([hidden[:, 0], hidden[:, 1]], axis=-1)
        hidden = hidden.reshape(ROWS_THREE * PAIRS, 512).astype(jnp.bfloat16)
        down = jnp.maximum(dot(hidden, reduce_three[...]), 0.0).reshape(ROWS_THREE, PAIRS, 256)
        before = carry_three[...]
        for k in range(0, ROWS_THREE, 2):
            lines = []
            for e in range(2):
                value = on_map(down[k + e], first + k + e - 3, col_three, limits_three)
                lines.append(
                    jnp.concatenate([value, following(value, 1), following(value, 2)], axis=1)
                )
            i = step * (ROWS_THREE // 2) + k // 2
            even_three[i] = jnp.concatenate(lines, axis=0).astype(jnp.bfloat16)
            odd_three[i] = jnp.concatenate([before, lines[0]], axis=0).astype(jnp.bfloat16)
            before = lines[1]
        carry_three[...] = before

    fetches[2].wait()
    fetches[3].wait()
    col_four = lax.broadcasted_iota(jnp.int32, (WIDE_FOUR, 512), 0) - 1
    limits_four = bounds(32, 16)
    size_four = ROWS_FOUR * PIX

    @pl.loop(0, STEPS_FOUR)
    def _(step):
        first = step * ROWS_FOUR
        hidden = (
            dot(even_three[pl.ds(first, ROWS_FOUR)].reshape(size_four, 768), weight_three[0])
            + dot(odd_three[pl.ds(first + 1, ROWS_FOUR)].reshape(size_four, 768), weight_three[1])
            + dot(even_three[pl.ds(first + 1, ROWS_FOUR)].reshape(size_four, 768), weight_three[2])
        )
        hidden = jnp.maximum(hidden, 0.0)
        for half in range(2):
            spread_three[half, pl.ds(0, size_four), :] = hidden[:, half * 128 : (half + 1) * 128]
        rows = []
        for k in range(ROWS_FOUR):
            rows.append(
                jnp.concatenate(
                    [
                        spread_three[
                            half,
                            pl.ds(k * PIX + e * PAIRS + g, WIDE_FOUR, stride=2),
                            :,
                        ]
                        for e in range(2)
                        for g in range(2)
                        for half in range(2)
                    ],
                    axis=1,
                )
            )
        hidden = jnp.concatenate(rows, axis=0).astype(jnp.bfloat16)
        down = jnp.maximum(dot(hidden, reduce_four[...]), 0.0)
        for k in range(ROWS_FOUR):
            value = down[k * WIDE_FOUR : (k + 1) * WIDE_FOUR]
            value = on_map(value, first + k - 1, col_four, limits_four)
            taps_four[first + k] = jnp.concatenate(
                [value[:16], following(value, 1)[:16], following(value, 2)[:16]], axis=1
            ).astype(jnp.bfloat16)

    fetches[4].wait()
    for half in range(2):
        lanes = slice(half * 256, (half + 1) * 256)
        hidden = sum(
            dot(taps_four[u : u + 32].reshape(512, 1536), weight_four[u, :, lanes])
            for u in range(3)
        )
        out[:, lanes] = jnp.maximum(hidden, 0.0).astype(jnp.bfloat16)


def encode(wide, edges, one, two, reduce_three, three, reduce_four, four, reduce_two):
    hbm = pl.BlockSpec(memory_space=pltpu.HBM)
    vmem = pl.BlockSpec(memory_space=pltpu.VMEM)
    big = (two, reduce_three, three, reduce_four, four)
    return pl.pallas_call(
        encoder_kernel,
        in_specs=[pl.BlockSpec(memory_space=pltpu.SMEM), vmem, vmem, vmem] + [hbm] * len(big),
        out_specs=vmem,
        out_shape=jax.ShapeDtypeStruct((512, 512), jnp.bfloat16),
        scratch_shapes=[
            pltpu.VMEM((HALVES, 168, 128), jnp.float32),
            pltpu.VMEM((HALVES, PIX, 512), jnp.bfloat16),
            pltpu.VMEM((ROWS_TWO, PIX, 512), jnp.bfloat16),
            pltpu.VMEM((ROWS_TWO, PIX, 512), jnp.bfloat16),
            pltpu.VMEM((PAIRS, 512), jnp.float32),
            pltpu.VMEM((STEPS_FOUR * ROWS_FOUR + 1, PIX, 768), jnp.bfloat16),
            pltpu.VMEM((STEPS_FOUR * ROWS_FOUR + 1, PIX, 768), jnp.bfloat16),
            pltpu.VMEM((PAIRS, 768), jnp.float32),
            pltpu.VMEM((2, ROWS_FOUR * PIX + 16, 128), jnp.float32),
            pltpu.VMEM((STEPS_FOUR * ROWS_FOUR, 16, 1536), jnp.bfloat16),
        ]
        + [pltpu.VMEM(w.shape, jnp.bfloat16) for w in big]
        + [pltpu.SemaphoreType.DMA((len(big),))],
        compiler_params=pltpu.CompilerParams(vmem_limit_bytes=BIG_VMEM),
        name="encoder",
    )(edges, wide, one, reduce_two, *big)


def patch_weights(kernel):
    rows = np.zeros((8, 4, 3), np.float32)
    for r in range(8):
        for y in range(4):
            u = r - (2 + y) + 1
            if 0 <= u < 3:
                rows[r, y, u] = 1
    cols = np.zeros((4, 2, 3), np.float32)
    for q in range(4):
        for g in range(2):
            v = q - g
            if 0 <= v < 3:
                cols[q, g, v] = 1
    spread = jnp.einsum("ryu,uvbo->rybvo", jnp.asarray(rows, jnp.bfloat16), kernel)
    spread = jnp.einsum("qgv,rybvo->qbrygo", jnp.asarray(cols, jnp.bfloat16), spread)
    spread = spread.reshape(4, BR, 512).astype(jnp.bfloat16)
    return jnp.pad(spread, ((0, 0), (0, 128 - BR), (0, 0))).reshape(512, 512)


def pair_weights(kernel):
    taps = jnp.stack(
        [jnp.pad(kernel, ((0, 0), (g, 1 - g), (0, 0), (0, 0))) for g in range(2)], axis=3
    )
    return taps.reshape(3, 512, 256)


def body(
    granule_blocks,
    row_weights,
    column_bank,
    destination,
    window_index,
    bank_index,
    kernel_one,
    reduce_two,
    kernel_two,
    reduce_three,
    kernel_three,
    reduce_four,
    kernel_four,
):
    nx, ny = lax.axis_size("tx"), lax.axis_size("ty")
    tx, ty = lax.axis_index("tx"), lax.axis_index("ty")
    tiles = nx * ny
    sent = resample(
        granule_blocks, row_weights, column_bank, destination, window_index, bank_index, tiles
    )
    got = lax.all_to_all(sent, ("tx", "ty"), split_axis=0, concat_axis=0, tiled=True)
    gridded, turned = gather_windows(got)
    wide = widen(turned)
    edges = jnp.stack([ty == 0, ty == ny - 1, tx == 0, tx == nx - 1]).astype(jnp.int32)
    bottleneck = encode(
        wide,
        edges,
        patch_weights(kernel_one),
        pair_weights(kernel_two),
        reduce_three.reshape(512, 256),
        kernel_three.reshape(3, 768, 256),
        reduce_four.reshape(1024, 512),
        kernel_four.reshape(3, 1536, 512),
        reduce_two.reshape(256, 128),
    )
    return (gridded, jnp.transpose(bottleneck.reshape(32, 16, 512), (2, 0, 1)))


def solution(mesh):
    in_specs = (
        P(("tx", "ty"), None, None, None),
        P(("tx", "ty"), None, None),
        P(),
        P(("tx", "ty")),
        P(("tx", "ty")),
        P(("tx", "ty")),
        P(),
        P(),
        P(),
        P(),
        P(),
        P(),
        P(),
    )
    out_specs = (P(None, "ty", "tx"), P(None, "ty", "tx"))
    return jax.shard_map(body, mesh=mesh, in_specs=in_specs, out_specs=out_specs, check_vma=False)
```

```python
import functools

import jax
import jax.numpy as jnp
import numpy as np
from jax import lax
from jax.experimental import pallas as pl
from jax.experimental.pallas import tpu as pltpu
from jax.sharding import PartitionSpec as P

MESH = pl.DeviceIdType.MESH
BANDS = 13
CAP = 2
WIN = 8
NWIN = 32
BR = BANDS * WIN
HALO = 16
BIG_VMEM = 58 << 20


def resample_kernel(
    dest,
    window,
    bank_index,
    raw,
    weights,
    bank,
    out,
    tiled_low,
    tiled_high,
    res,
    tags,
    tags_out,
    count,
    rank,
    sem,
    tag_sem,
):
    step = pl.program_id(0)
    per = raw.shape[0]
    held = res.shape[0]
    tiles = out.shape[0]
    lanes = BANDS * 16

    @pl.when(step == 0)
    def _():
        spread = (
            lax.broadcasted_iota(jnp.int32, (16, 256), 1) % 16
            == lax.broadcasted_iota(jnp.int32, (16, 256), 0)
        ).astype(jnp.bfloat16)
        for r in range(WIN):
            both = lax.dot_general(
                weights[r],
                spread,
                (((0,), (0,)), ((), ())),
                preferred_element_type=jnp.float32,
            )
            tiled_low[pl.ds(r, held, stride=WIN), :] = both[:, :128]
            tiled_high[pl.ds(r, held, stride=WIN), :] = both[:, 128:]
        tags[...] = jnp.full_like(tags, float(NWIN))

        @pl.loop(0, tiles // 8)
        def _(t):
            for u in range(8):
                count[t * 8 + u] = 0

        @pl.loop(0, held // 4)
        def _(group):
            for u in range(4):
                n = group * 4 + u
                tile = dest[n]
                place = count[tile]
                rank[n] = place
                count[tile] = place + 1
                tags[tile, pl.ds(place, 1), :] = jnp.full((1, 128), window[n], jnp.int32).astype(
                    jnp.float32
                )

        tags_out[...] = tags[...].astype(jnp.bfloat16)
        pltpu.make_async_copy(tags_out, out.at[:, pl.ds(CAP * BR, 8)], tag_sem).start()

    own_band = (
        lax.broadcasted_iota(jnp.int32, (BANDS, WIN, lanes), 2) // 16
        == lax.broadcasted_iota(jnp.int32, (BANDS, WIN, lanes), 0)
    )
    rowed = []
    for k in range(per):
        n = step * per + k
        rows = pl.ds(pl.multiple_of(n * WIN, WIN), WIN)
        row = jnp.concatenate([tiled_low[rows, :], tiled_high[rows, : lanes - 128]], axis=1)
        block = jnp.where(own_band, row[None], 0.0).reshape(BR, lanes).astype(jnp.bfloat16)
        rowed.append(
            jnp.dot(
                block, raw[k].reshape(lanes, 128), preferred_element_type=jnp.float32
            ).astype(jnp.bfloat16)
        )
    for k in range(per):
        n = step * per + k
        res[n] = jnp.dot(
            rowed[k], bank[bank_index[n]], preferred_element_type=jnp.float32
        ).astype(jnp.bfloat16)
    for k in range(per):
        n = step * per + k
        pltpu.make_async_copy(
            res.at[n], out.at[dest[n], pl.ds(pl.multiple_of(rank[n] * BR, 8), BR)], sem
        ).start()

    @pl.when(step == pl.num_programs(0) - 1)
    def _():
        pltpu.make_async_copy(res, res, sem).wait()
        pltpu.make_async_copy(tags_out, out.at[:, pl.ds(CAP * BR, 8)], tag_sem).wait()


def resample(raw, weights, bank, dest, window, bank_index, tiles):
    held = raw.shape[0]
    per = 16
    return pl.pallas_call(
        resample_kernel,
        grid=(held // per,),
        in_specs=[
            pl.BlockSpec(memory_space=pltpu.SMEM),
            pl.BlockSpec(memory_space=pltpu.SMEM),
            pl.BlockSpec(memory_space=pltpu.SMEM),
            pl.BlockSpec((per, BANDS, 16, 128), lambda i: (i, 0, 0, 0)),
            pl.BlockSpec((WIN, 16, held), lambda i: (0, 0, 0)),
            pl.BlockSpec(bank.shape, lambda i: (0, 0, 0)),
        ],
        out_specs=pl.BlockSpec(memory_space=pltpu.HBM),
        out_shape=jax.ShapeDtypeStruct((tiles, CAP * BR + 8, 128), jnp.bfloat16),
        scratch_shapes=[
            pltpu.VMEM((held * WIN, 128), jnp.float32),
            pltpu.VMEM((held * WIN, 128), jnp.float32),
            pltpu.VMEM((held, BR, 128), jnp.bfloat16),
            pltpu.VMEM((tiles, 8, 128), jnp.float32),
            pltpu.VMEM((tiles, 8, 128), jnp.bfloat16),
            pltpu.SMEM((tiles,), jnp.int32),
            pltpu.SMEM((held,), jnp.int32),
            pltpu.SemaphoreType.DMA,
            pltpu.SemaphoreType.DMA,
        ],
        compiler_params=pltpu.CompilerParams(vmem_limit_bytes=BIG_VMEM),
        name="resample",
    )(dest, window, bank_index, raw, jnp.transpose(weights, (1, 2, 0)), bank)


def gather_kernel(
    got, all_got, gridded, turned, even, odd, tags, dense, window, inverse, sem, tag_sem
):
    step = pl.program_id(0)
    per = got.shape[0]
    tiles = all_got.shape[0]

    @pl.when(step == 0)
    def _():
        fetch = pltpu.make_async_copy(all_got.at[:, pl.ds(CAP * BR, 8)], tags, tag_sem)
        fetch.start()
        even[...] = jnp.zeros_like(even)
        odd[...] = jnp.zeros_like(odd)
        fetch.wait()
        lane = lax.broadcasted_iota(jnp.int32, (8, 128), 1)
        total = jnp.zeros((8, 128), jnp.float32)
        for t in range(tiles):
            total = total + jnp.where(lane == t, tags[t].astype(jnp.float32), 0.0)
        dense[...] = total.astype(jnp.int32)
        scalars = pltpu.make_async_copy(dense, window, sem)
        scalars.start()
        which = lax.broadcasted_iota(jnp.int32, (NWIN, 128), 0).astype(jnp.float32)
        hits = jnp.zeros((NWIN, 128), jnp.float32)
        for k in range(CAP):
            hits = hits + jnp.where(which == total[k : k + 1, :], 1.0, 0.0)
        counts = jnp.sum(hits, axis=1, keepdims=True)
        inverse[...] = jnp.broadcast_to(1.0 / jnp.maximum(counts, 1.0), (NWIN, 128))
        scalars.wait()

    @pl.loop(0, per // 4)
    def _(group):
        for u in range(4):
            t = group * 4 + u
            for k, total in ((0, even), (1, odd)):
                total[window[k, step * per + t]] += got[t, k * BR : (k + 1) * BR, :].astype(
                    jnp.float32
                )

    @pl.when(step == pl.num_programs(0) - 1)
    def _():
        pad = jnp.zeros((128 - BR, 128), jnp.float32)
        for p in range(NWIN // 2):
            pair = []
            for w in (2 * p, 2 * p + 1):
                mean = (even[w] + odd[w]) * inverse[w : w + 1, :]
                pair.append(mean)
                turned[w] = jnp.concatenate([mean, pad], axis=0).astype(jnp.bfloat16).T
            for b in range(BANDS):
                rows = slice(b * WIN, (b + 1) * WIN)
                gridded[b, p * 16 : (p + 1) * 16, :] = jnp.concatenate(
                    [pair[0][rows], pair[1][rows]], axis=0
                ).astype(jnp.bfloat16)


def gather_windows(got):
    tiles, rows, _ = got.shape
    per = 32
    return pl.pallas_call(
        gather_kernel,
        grid=(tiles // per,),
        in_specs=[
            pl.BlockSpec((per, rows, 128), lambda i: (i, 0, 0)),
            pl.BlockSpec(memory_space=pl.ANY),
        ],
        out_specs=[
            pl.BlockSpec((BANDS, NWIN * WIN, 128), lambda i: (0, 0, 0)),
            pl.BlockSpec((NWIN, 128, 128), lambda i: (0, 0, 0)),
        ],
        out_shape=[
            jax.ShapeDtypeStruct((BANDS, NWIN * WIN, 128), jnp.bfloat16),
            jax.ShapeDtypeStruct((NWIN, 128, 128), jnp.bfloat16),
        ],
        scratch_shapes=[
            pltpu.VMEM((NWIN + 1, BR, 128), jnp.float32),
            pltpu.VMEM((NWIN + 1, BR, 128), jnp.float32),
            pltpu.VMEM((tiles, 8, 128), jnp.bfloat16),
            pltpu.VMEM((8, 128), jnp.int32),
            pltpu.SMEM((8, 128), jnp.int32),
            pltpu.VMEM((NWIN, 128), jnp.float32),
            pltpu.SemaphoreType.DMA,
            pltpu.SemaphoreType.DMA,
        ],
        compiler_params=pltpu.CompilerParams(vmem_limit_bytes=BIG_VMEM),
        name="gather_windows",
    )(got, got)


HALO_WIN = HALO // WIN
LAST_WIN = NWIN + HALO_WIN
LAST_COL = 128 + HALO
SIDE = {
    -1: ((0, HALO_WIN), (LAST_WIN, HALO_WIN)),
    0: ((0, NWIN), (HALO_WIN, NWIN)),
    1: ((NWIN - HALO_WIN, HALO_WIN), (0, HALO_WIN)),
}
EDGE = {
    -1: ((0, HALO), (LAST_COL, HALO)),
    0: ((0, 128), (HALO, 128)),
    1: ((128 - HALO, HALO), (0, HALO)),
}
MOVES = [(1, 0), (-1, 0), (0, 1), (0, -1), (1, 1), (1, -1), (-1, 1), (-1, -1)]


def widen_kernel(tile, wide, zero_rows, zero_cols, own_sem, zero_sem, send_sem, recv_sem):
    tx, ty = lax.axis_index("tx"), lax.axis_index("ty")
    nx, ny = lax.axis_size("tx"), lax.axis_size("ty")

    def inside(dx, dy):
        ok = None
        for d, at, n in ((dx, tx, nx), (dy, ty, ny)):
            if d:
                here = at + d >= 0 if d < 0 else at + d < n
                ok = here if ok is None else jnp.logical_and(ok, here)
        return ok

    def source(dx, dy):
        (w, wn), (c, cn) = SIDE[dy][0], EDGE[dx][0]
        return tile.at[pl.ds(w, wn), pl.ds(c, cn)]

    def target(dx, dy):
        (w, wn), (c, cn) = SIDE[dy][1], EDGE[dx][1]
        return wide.at[pl.ds(w, wn), pl.ds(c, cn)]

    barrier = pltpu.get_barrier_semaphore()
    for dx, dy in MOVES:

        @pl.when(inside(dx, dy))
        def _():
            pl.semaphore_signal(
                barrier, inc=1, device_id=(tx + dx, ty + dy), device_id_type=MESH
            )

    own = pltpu.make_async_copy(tile, target(0, 0), own_sem)
    own.start()
    zero_rows[...] = jnp.zeros_like(zero_rows)
    zero_cols[...] = jnp.zeros_like(zero_cols)
    peers = sum(inside(dx, dy).astype(jnp.int32) for dx, dy in MOVES)
    pl.semaphore_wait(barrier, peers)

    copies = []
    for i, (dx, dy) in enumerate(MOVES):
        send = pltpu.make_async_remote_copy(
            src_ref=source(dx, dy),
            dst_ref=target(dx, dy),
            send_sem=send_sem.at[i],
            recv_sem=recv_sem.at[i],
            device_id=(tx + dx, ty + dy),
            device_id_type=MESH,
        )
        (w, wn), (c, cn) = SIDE[dy][1], EDGE[dx][1]
        zeros = zero_rows if dy else zero_cols
        blank = pltpu.make_async_copy(
            zeros.at[pl.ds(0, wn), pl.ds(0, cn)], target(dx, dy), zero_sem.at[i]
        )
        copies.append((send, blank, inside(dx, dy), inside(-dx, -dy)))
    for send, blank, goes, comes in copies:

        @pl.when(goes)
        def _():
            send.start()

        @pl.when(jnp.logical_not(comes))
        def _():
            blank.start()

    own.wait()
    for send, blank, goes, comes in copies:

        @pl.when(goes)
        def _():
            send.wait_send()

        @pl.when(comes)
        def _():
            send.wait_recv()

        @pl.when(jnp.logical_not(comes))
        def _():
            blank.wait()


def widen(turned):
    moves = len(MOVES)
    return pl.pallas_call(
        widen_kernel,
        in_specs=[pl.BlockSpec(memory_space=pl.ANY)],
        out_specs=pl.BlockSpec(memory_space=pl.ANY),
        out_shape=jax.ShapeDtypeStruct(
            (NWIN + 2 * HALO_WIN, 128 + 2 * HALO, 128), jnp.bfloat16
        ),
        scratch_shapes=[
            pltpu.VMEM((HALO_WIN, 128, 128), jnp.bfloat16),
            pltpu.VMEM((NWIN, HALO, 128), jnp.bfloat16),
            pltpu.SemaphoreType.DMA,
            pltpu.SemaphoreType.DMA((moves,)),
            pltpu.SemaphoreType.DMA((moves,)),
            pltpu.SemaphoreType.DMA((moves,)),
        ],
        compiler_params=pltpu.CompilerParams(
            collective_id=0, has_side_effects=True, vmem_limit_bytes=BIG_VMEM
        ),
        name="widen",
    )(turned)


FAR = 1 << 20
HALVES = 18
STEPS_ONE = 4
PAIRS = 40
PIX = 2 * PAIRS
ROWS_TWO = STEPS_ONE * HALVES
ROWS_THREE = 14
STEPS_THREE = 5
ROWS_FOUR = 17
STEPS_FOUR = 2
WIDE_FOUR = 24


def encoder_kernel(
    edges,
    hbm_wide,
    weight_one,
    reduce_two,
    hbm_two,
    hbm_reduce_three,
    hbm_three,
    hbm_reduce_four,
    hbm_four,
    out,
    wide,
    slab,
    patch,
    even_two,
    odd_two,
    carry_two,
    even_three,
    odd_three,
    carry_three,
    spread_three,
    taps_four,
    weight_two,
    reduce_three,
    weight_three,
    reduce_four,
    weight_four,
    sems,
    wide_sems,
):
    def part(i):
        here = pl.ds(i * (HALVES // 2), HALVES // 2)
        return pltpu.make_async_copy(hbm_wide.at[here], wide.at[here], wide_sems.at[i])

    for i in range(STEPS_ONE):
        part(i).start()
    fetches = [
        pltpu.make_async_copy(source, target, sems.at[i])
        for i, (source, target) in enumerate(
            (
                (hbm_two, weight_two),
                (hbm_reduce_three, reduce_three),
                (hbm_three, weight_three),
                (hbm_reduce_four, reduce_four),
                (hbm_four, weight_four),
            )
        )
    ]
    for fetch in fetches:
        fetch.start()

    def dot(a, b):
        return jnp.dot(a, b, preferred_element_type=jnp.float32)

    def bounds(tile_rows, tile_cols):
        return (
            jnp.where(edges[0] == 1, 0, -FAR),
            jnp.where(edges[1] == 1, tile_rows, FAR),
            jnp.where(edges[2] == 1, 0, -FAR),
            jnp.where(edges[3] == 1, tile_cols, FAR),
        )

    def on_map(value, row, col, limits):
        top, bottom, left, right = limits
        right = jnp.where(jnp.logical_and(row >= top, row < bottom), right, -FAR)
        return jnp.where(jnp.logical_and(col >= left, col < right), value, 0.0)

    def following(value, by):
        return pltpu.roll(value, value.shape[0] - by, 0)

    last = wide.shape[0] - 1
    cols = wide.shape[1]
    low = lax.broadcasted_iota(jnp.int32, (cols, 128), 1) % 8 < 4
    at = lax.broadcasted_iota(jnp.int32, (PIX, 128), 0)
    col_two = jnp.where(at < PAIRS, 2 * at, 2 * (at - PAIRS) + 1) - 7
    limits_two = bounds(128, 64)
    carry_two[...] = jnp.zeros_like(carry_two)
    part(0).wait()

    @pl.loop(0, STEPS_ONE)
    def _(step):
        @pl.when(step < STEPS_ONE - 1)
        def _():
            part(step + 1).wait()

        for k in range(HALVES):
            w = step * (HALVES // 2) + k // 2
            here = wide[jnp.minimum(w, last)].astype(jnp.float32)
            if k % 2:
                after = wide[jnp.minimum(w + 1, last)].astype(jnp.float32)
                here = jnp.where(low, pltpu.roll(here, 124, 1), pltpu.roll(after, 4, 1))
            slab[k, pl.ds(0, cols), :] = here
            for q in range(4):
                both = [slab[k, pl.ds(first + q, PAIRS, stride=4), :] for first in (1, 3)]
                patch[k, :, q * 128 : (q + 1) * 128] = jnp.concatenate(both, axis=0).astype(
                    jnp.bfloat16
                )
        hidden = dot(patch[...].reshape(HALVES * PIX, 512), weight_one[...])
        hidden = jnp.maximum(hidden, 0.0).astype(jnp.bfloat16)
        down = [
            jnp.maximum(dot(hidden[:, e * 256 : (e + 1) * 256], reduce_two[...]), 0.0).reshape(
                HALVES, PIX, 128
            )
            for e in range(2)
        ]
        before = carry_two[...]
        for k in range(HALVES):
            h = step * HALVES + k
            lines = []
            for e in range(2):
                value = on_map(down[e][k], 2 * h + e - 7, col_two, limits_two)
                first, second = value[:PAIRS], value[PAIRS:]
                lines.append(
                    jnp.concatenate(
                        [first, second, following(first, 1), following(second, 1)], axis=1
                    )
                )
            even_two[h] = jnp.concatenate(lines, axis=0).astype(jnp.bfloat16)
            odd_two[h] = jnp.concatenate([before, lines[0]], axis=0).astype(jnp.bfloat16)
            before = lines[1]
        carry_two[...] = before

    fetches[0].wait()
    fetches[1].wait()
    col_three = lax.broadcasted_iota(jnp.int32, (PAIRS, 256), 0) - 3
    limits_three = bounds(64, 32)
    carry_three[...] = jnp.zeros_like(carry_three)
    size = ROWS_THREE * PIX

    @pl.loop(0, STEPS_THREE)
    def _(step):
        first = step * ROWS_THREE
        hidden = (
            dot(even_two[pl.ds(first, ROWS_THREE)].reshape(size, 512), weight_two[0])
            + dot(odd_two[pl.ds(first + 1, ROWS_THREE)].reshape(size, 512), weight_two[1])
            + dot(even_two[pl.ds(first + 1, ROWS_THREE)].reshape(size, 512), weight_two[2])
        )
        hidden = jnp.maximum(hidden, 0.0).reshape(ROWS_THREE, 2, PAIRS, 256)
        hidden = jnp.concatenate([hidden[:, 0], hidden[:, 1]], axis=-1)
        hidden = hidden.reshape(ROWS_THREE * PAIRS, 512).astype(jnp.bfloat16)
        down = jnp.maximum(dot(hidden, reduce_three[...]), 0.0).reshape(ROWS_THREE, PAIRS, 256)
        before = carry_three[...]
        for k in range(0, ROWS_THREE, 2):
            lines = []
            for e in range(2):
                value = on_map(down[k + e], first + k + e - 3, col_three, limits_three)
                lines.append(
                    jnp.concatenate([value, following(value, 1), following(value, 2)], axis=1)
                )
            i = step * (ROWS_THREE // 2) + k // 2
            even_three[i] = jnp.concatenate(lines, axis=0).astype(jnp.bfloat16)
            odd_three[i] = jnp.concatenate([before, lines[0]], axis=0).astype(jnp.bfloat16)
            before = lines[1]
        carry_three[...] = before

    fetches[2].wait()
    fetches[3].wait()
    col_four = lax.broadcasted_iota(jnp.int32, (WIDE_FOUR, 512), 0) - 1
    limits_four = bounds(32, 16)
    size_four = ROWS_FOUR * PIX

    @pl.loop(0, STEPS_FOUR)
    def _(step):
        first = step * ROWS_FOUR
        hidden = (
            dot(even_three[pl.ds(first, ROWS_FOUR)].reshape(size_four, 768), weight_three[0])
            + dot(odd_three[pl.ds(first + 1, ROWS_FOUR)].reshape(size_four, 768), weight_three[1])
            + dot(even_three[pl.ds(first + 1, ROWS_FOUR)].reshape(size_four, 768), weight_three[2])
        )
        hidden = jnp.maximum(hidden, 0.0)
        for half in range(2):
            spread_three[half, pl.ds(0, size_four), :] = hidden[:, half * 128 : (half + 1) * 128]
        rows = []
        for k in range(ROWS_FOUR):
            rows.append(
                jnp.concatenate(
                    [
                        spread_three[
                            half,
                            pl.ds(k * PIX + e * PAIRS + g, WIDE_FOUR, stride=2),
                            :,
                        ]
                        for e in range(2)
                        for g in range(2)
                        for half in range(2)
                    ],
                    axis=1,
                )
            )
        hidden = jnp.concatenate(rows, axis=0).astype(jnp.bfloat16)
        down = jnp.maximum(dot(hidden, reduce_four[...]), 0.0)
        for k in range(ROWS_FOUR):
            value = down[k * WIDE_FOUR : (k + 1) * WIDE_FOUR]
            value = on_map(value, first + k - 1, col_four, limits_four)
            taps_four[first + k] = jnp.concatenate(
                [value[:16], following(value, 1)[:16], following(value, 2)[:16]], axis=1
            ).astype(jnp.bfloat16)

    fetches[4].wait()
    for half in range(2):
        lanes = slice(half * 256, (half + 1) * 256)
        hidden = sum(
            dot(taps_four[u : u + 32].reshape(512, 1536), weight_four[u, :, lanes])
            for u in range(3)
        )
        out[:, lanes] = jnp.maximum(hidden, 0.0).astype(jnp.bfloat16)


def encode(wide, edges, one, two, reduce_three, three, reduce_four, four, reduce_two):
    hbm = pl.BlockSpec(memory_space=pltpu.HBM)
    vmem = pl.BlockSpec(memory_space=pltpu.VMEM)
    big = (two, reduce_three, three, reduce_four, four)
    return pl.pallas_call(
        encoder_kernel,
        in_specs=[pl.BlockSpec(memory_space=pltpu.SMEM), hbm, vmem, vmem] + [hbm] * len(big),
        out_specs=vmem,
        out_shape=jax.ShapeDtypeStruct((512, 512), jnp.bfloat16),
        scratch_shapes=[
            pltpu.VMEM(wide.shape, jnp.bfloat16),
            pltpu.VMEM((HALVES, 168, 128), jnp.float32),
            pltpu.VMEM((HALVES, PIX, 512), jnp.bfloat16),
            pltpu.VMEM((ROWS_TWO, PIX, 512), jnp.bfloat16),
            pltpu.VMEM((ROWS_TWO, PIX, 512), jnp.bfloat16),
            pltpu.VMEM((PAIRS, 512), jnp.float32),
            pltpu.VMEM((STEPS_FOUR * ROWS_FOUR + 1, PIX, 768), jnp.bfloat16),
            pltpu.VMEM((STEPS_FOUR * ROWS_FOUR + 1, PIX, 768), jnp.bfloat16),
            pltpu.VMEM((PAIRS, 768), jnp.float32),
            pltpu.VMEM((2, ROWS_FOUR * PIX + 16, 128), jnp.float32),
            pltpu.VMEM((STEPS_FOUR * ROWS_FOUR, 16, 1536), jnp.bfloat16),
        ]
        + [pltpu.VMEM(w.shape, jnp.bfloat16) for w in big]
        + [pltpu.SemaphoreType.DMA((len(big),)), pltpu.SemaphoreType.DMA((STEPS_ONE,))],
        compiler_params=pltpu.CompilerParams(vmem_limit_bytes=BIG_VMEM),
        name="encoder",
    )(edges, wide, one, reduce_two, *big)


def patch_weights(kernel):
    rows = np.zeros((8, 4, 3), np.float32)
    for r in range(8):
        for y in range(4):
            u = r - (2 + y) + 1
            if 0 <= u < 3:
                rows[r, y, u] = 1
    cols = np.zeros((4, 2, 3), np.float32)
    for q in range(4):
        for g in range(2):
            v = q - g
            if 0 <= v < 3:
                cols[q, g, v] = 1
    spread = jnp.einsum("ryu,uvbo->rybvo", jnp.asarray(rows, jnp.bfloat16), kernel)
    spread = jnp.einsum("qgv,rybvo->qbrygo", jnp.asarray(cols, jnp.bfloat16), spread)
    spread = spread.reshape(4, BR, 512).astype(jnp.bfloat16)
    return jnp.pad(spread, ((0, 0), (0, 128 - BR), (0, 0))).reshape(512, 512)


def pair_weights(kernel):
    taps = jnp.stack(
        [jnp.pad(kernel, ((0, 0), (g, 1 - g), (0, 0), (0, 0))) for g in range(2)], axis=3
    )
    return taps.reshape(3, 512, 256)


def body(
    granule_blocks,
    row_weights,
    column_bank,
    destination,
    window_index,
    bank_index,
    kernel_one,
    reduce_two,
    kernel_two,
    reduce_three,
    kernel_three,
    reduce_four,
    kernel_four,
):
    nx, ny = lax.axis_size("tx"), lax.axis_size("ty")
    tx, ty = lax.axis_index("tx"), lax.axis_index("ty")
    tiles = nx * ny
    sent = resample(
        granule_blocks, row_weights, column_bank, destination, window_index, bank_index, tiles
    )
    got = lax.all_to_all(sent, ("tx", "ty"), split_axis=0, concat_axis=0, tiled=True)
    gridded, turned = gather_windows(got)
    wide = widen(turned)
    edges = jnp.stack([ty == 0, ty == ny - 1, tx == 0, tx == nx - 1]).astype(jnp.int32)
    bottleneck = encode(
        wide,
        edges,
        patch_weights(kernel_one),
        pair_weights(kernel_two),
        reduce_three.reshape(512, 256),
        kernel_three.reshape(3, 768, 256),
        reduce_four.reshape(1024, 512),
        kernel_four.reshape(3, 1536, 512),
        reduce_two.reshape(256, 128),
    )
    return (gridded, jnp.transpose(bottleneck.reshape(32, 16, 512), (2, 0, 1)))


def solution(mesh):
    in_specs = (
        P(("tx", "ty"), None, None, None),
        P(("tx", "ty"), None, None),
        P(),
        P(("tx", "ty")),
        P(("tx", "ty")),
        P(("tx", "ty")),
        P(),
        P(),
        P(),
        P(),
        P(),
        P(),
        P(),
    )
    out_specs = (P(None, "ty", "tx"), P(None, "ty", "tx"))
    return jax.shard_map(body, mesh=mesh, in_specs=in_specs, out_specs=out_specs, check_vma=False)
```

```python
import functools

import jax
import jax.numpy as jnp
import numpy as np
from jax import lax
from jax.experimental import pallas as pl
from jax.experimental.pallas import tpu as pltpu
from jax.sharding import PartitionSpec as P

MESH = pl.DeviceIdType.MESH
BANDS = 13
CAP = 2
WIN = 8
NWIN = 32
BR = BANDS * WIN
HALO = 16
BIG_VMEM = 58 << 20


def resample_kernel(
    dest,
    window,
    bank_index,
    raw,
    weights,
    bank,
    out,
    tiled_low,
    tiled_high,
    res,
    tags,
    tags_out,
    count,
    rank,
    sem,
    tag_sem,
):
    step = pl.program_id(0)
    per = raw.shape[0]
    held = res.shape[0]
    tiles = out.shape[0]
    lanes = BANDS * 16

    @pl.when(step == 0)
    def _():
        spread = (
            lax.broadcasted_iota(jnp.int32, (16, 256), 1) % 16
            == lax.broadcasted_iota(jnp.int32, (16, 256), 0)
        ).astype(jnp.bfloat16)
        for r in range(WIN):
            both = lax.dot_general(
                weights[r],
                spread,
                (((0,), (0,)), ((), ())),
                preferred_element_type=jnp.float32,
            )
            tiled_low[pl.ds(r, held, stride=WIN), :] = both[:, :128]
            tiled_high[pl.ds(r, held, stride=WIN), :] = both[:, 128:]
        tags[...] = jnp.full_like(tags, float(NWIN))

        @pl.loop(0, tiles // 8)
        def _(t):
            for u in range(8):
                count[t * 8 + u] = 0

        @pl.loop(0, held // 4)
        def _(group):
            for u in range(4):
                n = group * 4 + u
                tile = dest[n]
                place = count[tile]
                rank[n] = place
                count[tile] = place + 1
                tags[tile, pl.ds(place, 1), :] = jnp.full((1, 128), window[n], jnp.int32).astype(
                    jnp.float32
                )

        tags_out[...] = tags[...].astype(jnp.bfloat16)
        pltpu.make_async_copy(tags_out, out.at[:, pl.ds(CAP * BR, 8)], tag_sem).start()

    own_band = (
        lax.broadcasted_iota(jnp.int32, (BANDS, WIN, lanes), 2) // 16
        == lax.broadcasted_iota(jnp.int32, (BANDS, WIN, lanes), 0)
    )
    rowed = []
    for k in range(per):
        n = step * per + k
        rows = pl.ds(pl.multiple_of(n * WIN, WIN), WIN)
        row = jnp.concatenate([tiled_low[rows, :], tiled_high[rows, : lanes - 128]], axis=1)
        block = jnp.where(own_band, row[None], 0.0).reshape(BR, lanes).astype(jnp.bfloat16)
        rowed.append(
            jnp.dot(
                block, raw[k].reshape(lanes, 128), preferred_element_type=jnp.float32
            ).astype(jnp.bfloat16)
        )
    for k in range(per):
        n = step * per + k
        res[n] = jnp.dot(
            rowed[k], bank[bank_index[n]], preferred_element_type=jnp.float32
        ).astype(jnp.bfloat16)
    for k in range(per):
        n = step * per + k
        pltpu.make_async_copy(
            res.at[n], out.at[dest[n], pl.ds(pl.multiple_of(rank[n] * BR, 8), BR)], sem
        ).start()

    @pl.when(step == pl.num_programs(0) - 1)
    def _():
        pltpu.make_async_copy(res, res, sem).wait()
        pltpu.make_async_copy(tags_out, out.at[:, pl.ds(CAP * BR, 8)], tag_sem).wait()


def resample(raw, weights, bank, dest, window, bank_index, tiles):
    held = raw.shape[0]
    per = 16
    return pl.pallas_call(
        resample_kernel,
        grid=(held // per,),
        in_specs=[
            pl.BlockSpec(memory_space=pltpu.SMEM),
            pl.BlockSpec(memory_space=pltpu.SMEM),
            pl.BlockSpec(memory_space=pltpu.SMEM),
            pl.BlockSpec((per, BANDS, 16, 128), lambda i: (i, 0, 0, 0)),
            pl.BlockSpec((WIN, 16, held), lambda i: (0, 0, 0)),
            pl.BlockSpec(bank.shape, lambda i: (0, 0, 0)),
        ],
        out_specs=pl.BlockSpec(memory_space=pltpu.HBM),
        out_shape=jax.ShapeDtypeStruct((tiles, CAP * BR + 8, 128), jnp.bfloat16),
        scratch_shapes=[
            pltpu.VMEM((held * WIN, 128), jnp.float32),
            pltpu.VMEM((held * WIN, 128), jnp.float32),
            pltpu.VMEM((held, BR, 128), jnp.bfloat16),
            pltpu.VMEM((tiles, 8, 128), jnp.float32),
            pltpu.VMEM((tiles, 8, 128), jnp.bfloat16),
            pltpu.SMEM((tiles,), jnp.int32),
            pltpu.SMEM((held,), jnp.int32),
            pltpu.SemaphoreType.DMA,
            pltpu.SemaphoreType.DMA,
        ],
        compiler_params=pltpu.CompilerParams(vmem_limit_bytes=BIG_VMEM),
        name="resample",
    )(dest, window, bank_index, raw, jnp.transpose(weights, (1, 2, 0)), bank)


def gather_kernel(
    got, all_got, gridded, turned, even, odd, tags, dense, window, inverse, sem, tag_sem
):
    step = pl.program_id(0)
    per = got.shape[0]
    tiles = all_got.shape[0]

    @pl.when(step == 0)
    def _():
        fetch = pltpu.make_async_copy(all_got.at[:, pl.ds(CAP * BR, 8)], tags, tag_sem)
        fetch.start()
        even[...] = jnp.zeros_like(even)
        odd[...] = jnp.zeros_like(odd)
        fetch.wait()
        lane = lax.broadcasted_iota(jnp.int32, (8, 128), 1)
        total = jnp.zeros((8, 128), jnp.float32)
        for t in range(tiles):
            total = total + jnp.where(lane == t, tags[t].astype(jnp.float32), 0.0)
        dense[...] = total.astype(jnp.int32)
        scalars = pltpu.make_async_copy(dense, window, sem)
        scalars.start()
        which = lax.broadcasted_iota(jnp.int32, (NWIN, 128), 0).astype(jnp.float32)
        hits = jnp.zeros((NWIN, 128), jnp.float32)
        for k in range(CAP):
            hits = hits + jnp.where(which == total[k : k + 1, :], 1.0, 0.0)
        counts = jnp.sum(hits, axis=1, keepdims=True)
        inverse[...] = jnp.broadcast_to(1.0 / jnp.maximum(counts, 1.0), (NWIN, 128))
        scalars.wait()

    @pl.loop(0, per // 4)
    def _(group):
        for u in range(4):
            t = group * 4 + u
            for k, total in ((0, even), (1, odd)):
                total[window[k, step * per + t]] += got[t, k * BR : (k + 1) * BR, :].astype(
                    jnp.float32
                )

    @pl.when(step == pl.num_programs(0) - 1)
    def _():
        pad = jnp.zeros((128 - BR, 128), jnp.float32)
        for p in range(NWIN // 2):
            pair = []
            for w in (2 * p, 2 * p + 1):
                mean = (even[w] + odd[w]) * inverse[w : w + 1, :]
                pair.append(mean)
                turned[w] = jnp.concatenate([mean, pad], axis=0).astype(jnp.bfloat16).T
            for b in range(BANDS):
                rows = slice(b * WIN, (b + 1) * WIN)
                gridded[b, p * 16 : (p + 1) * 16, :] = jnp.concatenate(
                    [pair[0][rows], pair[1][rows]], axis=0
                ).astype(jnp.bfloat16)


def gather_windows(got):
    tiles, rows, _ = got.shape
    per = 32
    return pl.pallas_call(
        gather_kernel,
        grid=(tiles // per,),
        in_specs=[
            pl.BlockSpec((per, rows, 128), lambda i: (i, 0, 0)),
            pl.BlockSpec(memory_space=pl.ANY),
        ],
        out_specs=[
            pl.BlockSpec((BANDS, NWIN * WIN, 128), lambda i: (0, 0, 0)),
            pl.BlockSpec((NWIN, 128, 128), lambda i: (0, 0, 0)),
        ],
        out_shape=[
            jax.ShapeDtypeStruct((BANDS, NWIN * WIN, 128), jnp.bfloat16),
            jax.ShapeDtypeStruct((NWIN, 128, 128), jnp.bfloat16),
        ],
        scratch_shapes=[
            pltpu.VMEM((NWIN + 1, BR, 128), jnp.float32),
            pltpu.VMEM((NWIN + 1, BR, 128), jnp.float32),
            pltpu.VMEM((tiles, 8, 128), jnp.bfloat16),
            pltpu.VMEM((8, 128), jnp.int32),
            pltpu.SMEM((8, 128), jnp.int32),
            pltpu.VMEM((NWIN, 128), jnp.float32),
            pltpu.SemaphoreType.DMA,
            pltpu.SemaphoreType.DMA,
        ],
        compiler_params=pltpu.CompilerParams(vmem_limit_bytes=BIG_VMEM),
        name="gather_windows",
    )(got, got)


HALO_WIN = HALO // WIN
WIDE_WIN = NWIN + 2 * HALO_WIN
WIDE_COL = 128 + 2 * HALO
MOVES = [(1, 0), (-1, 0), (0, 1), (0, -1), (1, 1), (1, -1), (-1, 1), (-1, -1)]


def rim_kernel(
    tile,
    rim_rows,
    rim_cols,
    edge_rows,
    edge_cols,
    zero_rows,
    zero_cols,
    edge_sem,
    zero_sem,
    send_sem,
    recv_sem,
):
    tx, ty = lax.axis_index("tx"), lax.axis_index("ty")
    nx, ny = lax.axis_size("tx"), lax.axis_size("ty")

    def inside(dx, dy):
        ok = None
        for d, at, n in ((dx, tx, nx), (dy, ty, ny)):
            if d:
                here = at + d >= 0 if d < 0 else at + d < n
                ok = here if ok is None else jnp.logical_and(ok, here)
        return ok

    def source(dx, dy):
        if dy == 0:
            return edge_cols.at[:, pl.ds(HALO if dx > 0 else 0, HALO)]
        c, cn = {-1: (0, HALO), 0: (0, 128), 1: (128 - HALO, HALO)}[dx]
        return edge_rows.at[pl.ds(HALO_WIN if dy > 0 else 0, HALO_WIN), pl.ds(c, cn)]

    def target(dx, dy):
        if dy == 0:
            return rim_cols.at[:, pl.ds(0 if dx > 0 else HALO, HALO)]
        c, cn = {-1: (HALO + 128, HALO), 0: (HALO, 128), 1: (0, HALO)}[dx]
        return rim_rows.at[pl.ds(0 if dy > 0 else HALO_WIN, HALO_WIN), pl.ds(c, cn)]

    barrier = pltpu.get_barrier_semaphore()
    for dx, dy in MOVES:

        @pl.when(inside(dx, dy))
        def _():
            pl.semaphore_signal(
                barrier, inc=1, device_id=(tx + dx, ty + dy), device_id_type=MESH
            )

    edges = [
        pltpu.make_async_copy(src, dst, edge_sem.at[i])
        for i, (src, dst) in enumerate(
            (
                (tile.at[pl.ds(0, HALO_WIN)], edge_rows.at[pl.ds(0, HALO_WIN)]),
                (
                    tile.at[pl.ds(NWIN - HALO_WIN, HALO_WIN)],
                    edge_rows.at[pl.ds(HALO_WIN, HALO_WIN)],
                ),
                (tile.at[:, pl.ds(0, HALO)], edge_cols.at[:, pl.ds(0, HALO)]),
                (tile.at[:, pl.ds(128 - HALO, HALO)], edge_cols.at[:, pl.ds(HALO, HALO)]),
            )
        )
    ]
    for edge in edges:
        edge.start()
    zero_rows[...] = jnp.zeros_like(zero_rows)
    zero_cols[...] = jnp.zeros_like(zero_cols)
    for edge in edges:
        edge.wait()
    peers = sum(inside(dx, dy).astype(jnp.int32) for dx, dy in MOVES)
    pl.semaphore_wait(barrier, peers)

    copies = []
    for i, (dx, dy) in enumerate(MOVES):
        send = pltpu.make_async_remote_copy(
            src_ref=source(dx, dy),
            dst_ref=target(dx, dy),
            send_sem=send_sem.at[i],
            recv_sem=recv_sem.at[i],
            device_id=(tx + dx, ty + dy),
            device_id_type=MESH,
        )
        zeros = zero_rows.at[:, pl.ds(0, HALO if dx else 128)] if dy else zero_cols
        blank = pltpu.make_async_copy(zeros, target(dx, dy), zero_sem.at[i])
        copies.append((send, blank, inside(dx, dy), inside(-dx, -dy)))
    for send, blank, goes, comes in copies:

        @pl.when(goes)
        def _():
            send.start()

        @pl.when(jnp.logical_not(comes))
        def _():
            blank.start()

    for send, blank, goes, comes in copies:

        @pl.when(goes)
        def _():
            send.wait_send()

        @pl.when(comes)
        def _():
            send.wait_recv()

        @pl.when(jnp.logical_not(comes))
        def _():
            blank.wait()


def rim(turned):
    moves = len(MOVES)
    vmem = pl.BlockSpec(memory_space=pltpu.VMEM)
    return pl.pallas_call(
        rim_kernel,
        in_specs=[pl.BlockSpec(memory_space=pl.ANY)],
        out_specs=[vmem, vmem],
        out_shape=[
            jax.ShapeDtypeStruct((2 * HALO_WIN, WIDE_COL, 128), jnp.bfloat16),
            jax.ShapeDtypeStruct((NWIN, 2 * HALO, 128), jnp.bfloat16),
        ],
        scratch_shapes=[
            pltpu.VMEM((2 * HALO_WIN, 128, 128), jnp.bfloat16),
            pltpu.VMEM((NWIN, 2 * HALO, 128), jnp.bfloat16),
            pltpu.VMEM((HALO_WIN, 128, 128), jnp.bfloat16),
            pltpu.VMEM((NWIN, HALO, 128), jnp.bfloat16),
            pltpu.SemaphoreType.DMA((4,)),
            pltpu.SemaphoreType.DMA((moves,)),
            pltpu.SemaphoreType.DMA((moves,)),
            pltpu.SemaphoreType.DMA((moves,)),
        ],
        compiler_params=pltpu.CompilerParams(
            collective_id=0, has_side_effects=True, vmem_limit_bytes=BIG_VMEM
        ),
        name="rim",
    )(turned)


FAR = 1 << 20
HALVES = 18
STEPS_ONE = 4
PAIRS = 40
PIX = 2 * PAIRS
ROWS_TWO = STEPS_ONE * HALVES
ROWS_THREE = 14
STEPS_THREE = 5
ROWS_FOUR = 17
STEPS_FOUR = 2
WIDE_FOUR = 24


def encoder_kernel(
    edges,
    tile,
    rim_rows,
    rim_cols,
    weight_one,
    reduce_two,
    hbm_two,
    hbm_reduce_three,
    hbm_three,
    hbm_reduce_four,
    hbm_four,
    out,
    wide,
    slab,
    patch,
    even_two,
    odd_two,
    carry_two,
    even_three,
    odd_three,
    carry_three,
    spread_three,
    taps_four,
    weight_two,
    reduce_three,
    weight_three,
    reduce_four,
    weight_four,
    sems,
    wide_sems,
):
    per = HALVES // 2
    parts = []
    for i in range(STEPS_ONE):
        low_win, high_win = max(i * per, HALO_WIN), min((i + 1) * per, HALO_WIN + NWIN)
        inner = pl.ds(low_win - HALO_WIN, high_win - low_win)
        outer = pl.ds(low_win, high_win - low_win)
        moves = [
            (tile.at[inner], wide.at[outer, pl.ds(HALO, 128)]),
            (rim_cols.at[inner, pl.ds(0, HALO)], wide.at[outer, pl.ds(0, HALO)]),
            (rim_cols.at[inner, pl.ds(HALO, HALO)], wide.at[outer, pl.ds(HALO + 128, HALO)]),
        ]
        if i == 0:
            moves.append((rim_rows.at[pl.ds(0, HALO_WIN)], wide.at[pl.ds(0, HALO_WIN)]))
        if i == STEPS_ONE - 1:
            moves.append(
                (rim_rows.at[pl.ds(HALO_WIN, HALO_WIN)], wide.at[pl.ds(WIDE_WIN - HALO_WIN, HALO_WIN)])
            )
        parts.append(
            [
                pltpu.make_async_copy(src, dst, wide_sems.at[i, j])
                for j, (src, dst) in enumerate(moves)
            ]
        )
    for copies in parts:
        for copy in copies:
            copy.start()
    fetches = [
        pltpu.make_async_copy(source, target, sems.at[i])
        for i, (source, target) in enumerate(
            (
                (hbm_two, weight_two),
                (hbm_reduce_three, reduce_three),
                (hbm_three, weight_three),
                (hbm_reduce_four, reduce_four),
                (hbm_four, weight_four),
            )
        )
    ]
    for fetch in fetches:
        fetch.start()

    def dot(a, b):
        return jnp.dot(a, b, preferred_element_type=jnp.float32)

    def bounds(tile_rows, tile_cols):
        return (
            jnp.where(edges[0] == 1, 0, -FAR),
            jnp.where(edges[1] == 1, tile_rows, FAR),
            jnp.where(edges[2] == 1, 0, -FAR),
            jnp.where(edges[3] == 1, tile_cols, FAR),
        )

    def on_map(value, row, col, limits):
        top, bottom, left, right = limits
        right = jnp.where(jnp.logical_and(row >= top, row < bottom), right, -FAR)
        return jnp.where(jnp.logical_and(col >= left, col < right), value, 0.0)

    def following(value, by):
        return pltpu.roll(value, value.shape[0] - by, 0)

    last = wide.shape[0] - 1
    cols = wide.shape[1]
    low = lax.broadcasted_iota(jnp.int32, (cols, 128), 1) % 8 < 4
    at = lax.broadcasted_iota(jnp.int32, (PIX, 128), 0)
    col_two = jnp.where(at < PAIRS, 2 * at, 2 * (at - PAIRS) + 1) - 7
    limits_two = bounds(128, 64)
    carry_two[...] = jnp.zeros_like(carry_two)
    for copy in parts[0]:
        copy.wait()

    @pl.loop(0, STEPS_ONE)
    def _(step):
        for i in range(1, STEPS_ONE):

            @pl.when(step == i - 1)
            def _():
                for copy in parts[i]:
                    copy.wait()

        for k in range(HALVES):
            w = step * (HALVES // 2) + k // 2
            here = wide[jnp.minimum(w, last)].astype(jnp.float32)
            if k % 2:
                after = wide[jnp.minimum(w + 1, last)].astype(jnp.float32)
                here = jnp.where(low, pltpu.roll(here, 124, 1), pltpu.roll(after, 4, 1))
            slab[k, pl.ds(0, cols), :] = here
            for q in range(4):
                both = [slab[k, pl.ds(first + q, PAIRS, stride=4), :] for first in (1, 3)]
                patch[k, :, q * 128 : (q + 1) * 128] = jnp.concatenate(both, axis=0).astype(
                    jnp.bfloat16
                )
        hidden = dot(patch[...].reshape(HALVES * PIX, 512), weight_one[...])
        hidden = jnp.maximum(hidden, 0.0).astype(jnp.bfloat16)
        down = [
            jnp.maximum(dot(hidden[:, e * 256 : (e + 1) * 256], reduce_two[...]), 0.0).reshape(
                HALVES, PIX, 128
            )
            for e in range(2)
        ]
        before = carry_two[...]
        for k in range(HALVES):
            h = step * HALVES + k
            lines = []
            for e in range(2):
                value = on_map(down[e][k], 2 * h + e - 7, col_two, limits_two)
                first, second = value[:PAIRS], value[PAIRS:]
                lines.append(
                    jnp.concatenate(
                        [first, second, following(first, 1), following(second, 1)], axis=1
                    )
                )
            even_two[h] = jnp.concatenate(lines, axis=0).astype(jnp.bfloat16)
            odd_two[h] = jnp.concatenate([before, lines[0]], axis=0).astype(jnp.bfloat16)
            before = lines[1]
        carry_two[...] = before

    fetches[0].wait()
    fetches[1].wait()
    col_three = lax.broadcasted_iota(jnp.int32, (PAIRS, 256), 0) - 3
    limits_three = bounds(64, 32)
    carry_three[...] = jnp.zeros_like(carry_three)
    size = ROWS_THREE * PIX

    @pl.loop(0, STEPS_THREE)
    def _(step):
        first = step * ROWS_THREE
        hidden = (
            dot(even_two[pl.ds(first, ROWS_THREE)].reshape(size, 512), weight_two[0])
            + dot(odd_two[pl.ds(first + 1, ROWS_THREE)].reshape(size, 512), weight_two[1])
            + dot(even_two[pl.ds(first + 1, ROWS_THREE)].reshape(size, 512), weight_two[2])
        )
        hidden = jnp.maximum(hidden, 0.0).reshape(ROWS_THREE, 2, PAIRS, 256)
        hidden = jnp.concatenate([hidden[:, 0], hidden[:, 1]], axis=-1)
        hidden = hidden.reshape(ROWS_THREE * PAIRS, 512).astype(jnp.bfloat16)
        down = jnp.maximum(dot(hidden, reduce_three[...]), 0.0).reshape(ROWS_THREE, PAIRS, 256)
        before = carry_three[...]
        for k in range(0, ROWS_THREE, 2):
            lines = []
            for e in range(2):
                value = on_map(down[k + e], first + k + e - 3, col_three, limits_three)
                lines.append(
                    jnp.concatenate([value, following(value, 1), following(value, 2)], axis=1)
                )
            i = step * (ROWS_THREE // 2) + k // 2
            even_three[i] = jnp.concatenate(lines, axis=0).astype(jnp.bfloat16)
            odd_three[i] = jnp.concatenate([before, lines[0]], axis=0).astype(jnp.bfloat16)
            before = lines[1]
        carry_three[...] = before

    fetches[2].wait()
    fetches[3].wait()
    col_four = lax.broadcasted_iota(jnp.int32, (WIDE_FOUR, 512), 0) - 1
    limits_four = bounds(32, 16)
    size_four = ROWS_FOUR * PIX

    @pl.loop(0, STEPS_FOUR)
    def _(step):
        first = step * ROWS_FOUR
        hidden = (
            dot(even_three[pl.ds(first, ROWS_FOUR)].reshape(size_four, 768), weight_three[0])
            + dot(odd_three[pl.ds(first + 1, ROWS_FOUR)].reshape(size_four, 768), weight_three[1])
            + dot(even_three[pl.ds(first + 1, ROWS_FOUR)].reshape(size_four, 768), weight_three[2])
        )
        hidden = jnp.maximum(hidden, 0.0)
        for half in range(2):
            spread_three[half, pl.ds(0, size_four), :] = hidden[:, half * 128 : (half + 1) * 128]
        rows = []
        for k in range(ROWS_FOUR):
            rows.append(
                jnp.concatenate(
                    [
                        spread_three[
                            half,
                            pl.ds(k * PIX + e * PAIRS + g, WIDE_FOUR, stride=2),
                            :,
                        ]
                        for e in range(2)
                        for g in range(2)
                        for half in range(2)
                    ],
                    axis=1,
                )
            )
        hidden = jnp.concatenate(rows, axis=0).astype(jnp.bfloat16)
        down = jnp.maximum(dot(hidden, reduce_four[...]), 0.0)
        for k in range(ROWS_FOUR):
            value = down[k * WIDE_FOUR : (k + 1) * WIDE_FOUR]
            value = on_map(value, first + k - 1, col_four, limits_four)
            taps_four[first + k] = jnp.concatenate(
                [value[:16], following(value, 1)[:16], following(value, 2)[:16]], axis=1
            ).astype(jnp.bfloat16)

    fetches[4].wait()
    for half in range(2):
        lanes = slice(half * 256, (half + 1) * 256)
        hidden = sum(
            dot(taps_four[u : u + 32].reshape(512, 1536), weight_four[u, :, lanes])
            for u in range(3)
        )
        out[:, lanes] = jnp.maximum(hidden, 0.0).astype(jnp.bfloat16)


def encode(tile, rims, edges, one, two, reduce_three, three, reduce_four, four, reduce_two):
    hbm = pl.BlockSpec(memory_space=pltpu.HBM)
    vmem = pl.BlockSpec(memory_space=pltpu.VMEM)
    big = (two, reduce_three, three, reduce_four, four)
    return pl.pallas_call(
        encoder_kernel,
        in_specs=[pl.BlockSpec(memory_space=pltpu.SMEM)]
        + [hbm] * 3
        + [vmem] * 2
        + [hbm] * len(big),
        out_specs=vmem,
        out_shape=jax.ShapeDtypeStruct((512, 512), jnp.bfloat16),
        scratch_shapes=[
            pltpu.VMEM((WIDE_WIN, WIDE_COL, 128), jnp.bfloat16),
            pltpu.VMEM((HALVES, 168, 128), jnp.float32),
            pltpu.VMEM((HALVES, PIX, 512), jnp.bfloat16),
            pltpu.VMEM((ROWS_TWO, PIX, 512), jnp.bfloat16),
            pltpu.VMEM((ROWS_TWO, PIX, 512), jnp.bfloat16),
            pltpu.VMEM((PAIRS, 512), jnp.float32),
            pltpu.VMEM((STEPS_FOUR * ROWS_FOUR + 1, PIX, 768), jnp.bfloat16),
            pltpu.VMEM((STEPS_FOUR * ROWS_FOUR + 1, PIX, 768), jnp.bfloat16),
            pltpu.VMEM((PAIRS, 768), jnp.float32),
            pltpu.VMEM((2, ROWS_FOUR * PIX + 16, 128), jnp.float32),
            pltpu.VMEM((STEPS_FOUR * ROWS_FOUR, 16, 1536), jnp.bfloat16),
        ]
        + [pltpu.VMEM(w.shape, jnp.bfloat16) for w in big]
        + [pltpu.SemaphoreType.DMA((len(big),)), pltpu.SemaphoreType.DMA((STEPS_ONE, 4))],
        compiler_params=pltpu.CompilerParams(vmem_limit_bytes=BIG_VMEM),
        name="encoder",
    )(edges, tile, *rims, one, reduce_two, *big)


def patch_weights(kernel):
    rows = np.zeros((8, 4, 3), np.float32)
    for r in range(8):
        for y in range(4):
            u = r - (2 + y) + 1
            if 0 <= u < 3:
                rows[r, y, u] = 1
    cols = np.zeros((4, 2, 3), np.float32)
    for q in range(4):
        for g in range(2):
            v = q - g
            if 0 <= v < 3:
                cols[q, g, v] = 1
    spread = jnp.einsum("ryu,uvbo->rybvo", jnp.asarray(rows, jnp.bfloat16), kernel)
    spread = jnp.einsum("qgv,rybvo->qbrygo", jnp.asarray(cols, jnp.bfloat16), spread)
    spread = spread.reshape(4, BR, 512).astype(jnp.bfloat16)
    return jnp.pad(spread, ((0, 0), (0, 128 - BR), (0, 0))).reshape(512, 512)


def pair_weights(kernel):
    taps = jnp.stack(
        [jnp.pad(kernel, ((0, 0), (g, 1 - g), (0, 0), (0, 0))) for g in range(2)], axis=3
    )
    return taps.reshape(3, 512, 256)


def body(
    granule_blocks,
    row_weights,
    column_bank,
    destination,
    window_index,
    bank_index,
    kernel_one,
    reduce_two,
    kernel_two,
    reduce_three,
    kernel_three,
    reduce_four,
    kernel_four,
):
    nx, ny = lax.axis_size("tx"), lax.axis_size("ty")
    tx, ty = lax.axis_index("tx"), lax.axis_index("ty")
    tiles = nx * ny
    sent = resample(
        granule_blocks, row_weights, column_bank, destination, window_index, bank_index, tiles
    )
    got = lax.all_to_all(sent, ("tx", "ty"), split_axis=0, concat_axis=0, tiled=True)
    gridded, turned = gather_windows(got)
    edges = jnp.stack([ty == 0, ty == ny - 1, tx == 0, tx == nx - 1]).astype(jnp.int32)
    bottleneck = encode(
        turned,
        rim(turned),
        edges,
        patch_weights(kernel_one),
        pair_weights(kernel_two),
        reduce_three.reshape(512, 256),
        kernel_three.reshape(3, 768, 256),
        reduce_four.reshape(1024, 512),
        kernel_four.reshape(3, 1536, 512),
        reduce_two.reshape(256, 128),
    )
    return (gridded, jnp.transpose(bottleneck.reshape(32, 16, 512), (2, 0, 1)))


def solution(mesh):
    in_specs = (
        P(("tx", "ty"), None, None, None),
        P(("tx", "ty"), None, None),
        P(),
        P(("tx", "ty")),
        P(("tx", "ty")),
        P(("tx", "ty")),
        P(),
        P(),
        P(),
        P(),
        P(),
        P(),
        P(),
    )
    out_specs = (P(None, "ty", "tx"), P(None, "ty", "tx"))
    return jax.shard_map(body, mesh=mesh, in_specs=in_specs, out_specs=out_specs, check_vma=False)
```

```python
import functools

import jax
import jax.numpy as jnp
import numpy as np
from jax import lax
from jax.experimental import pallas as pl
from jax.experimental.pallas import tpu as pltpu
from jax.sharding import PartitionSpec as P

MESH = pl.DeviceIdType.MESH
BANDS = 13
CAP = 2
WIN = 8
NWIN = 32
BR = BANDS * WIN
HALO = 16
BIG_VMEM = 58 << 20


def resample_kernel(
    dest,
    window,
    bank_index,
    raw,
    weights,
    bank,
    out,
    tiled_low,
    tiled_high,
    res,
    tags,
    tags_out,
    count,
    rank,
    sem,
    tag_sem,
):
    step = pl.program_id(0)
    per = raw.shape[0]
    held = res.shape[0]
    tiles = out.shape[0]
    lanes = BANDS * 16

    @pl.when(step == 0)
    def _():
        spread = (
            lax.broadcasted_iota(jnp.int32, (16, 256), 1) % 16
            == lax.broadcasted_iota(jnp.int32, (16, 256), 0)
        ).astype(jnp.bfloat16)
        for r in range(WIN):
            both = lax.dot_general(
                weights[r],
                spread,
                (((0,), (0,)), ((), ())),
                preferred_element_type=jnp.float32,
            )
            tiled_low[pl.ds(r, held, stride=WIN), :] = both[:, :128]
            tiled_high[pl.ds(r, held, stride=WIN), :] = both[:, 128:]
        tags[...] = jnp.full_like(tags, float(NWIN))

        @pl.loop(0, tiles // 8)
        def _(t):
            for u in range(8):
                count[t * 8 + u] = 0

        @pl.loop(0, held // 4)
        def _(group):
            for u in range(4):
                n = group * 4 + u
                tile = dest[n]
                place = count[tile]
                rank[n] = place
                count[tile] = place + 1
                tags[tile, pl.ds(place, 1), :] = jnp.full((1, 128), window[n], jnp.int32).astype(
                    jnp.float32
                )

        tags_out[...] = tags[...].astype(jnp.bfloat16)
        pltpu.make_async_copy(tags_out, out.at[:, pl.ds(CAP * BR, 8)], tag_sem).start()

    own_band = (
        lax.broadcasted_iota(jnp.int32, (BANDS, WIN, lanes), 2) // 16
        == lax.broadcasted_iota(jnp.int32, (BANDS, WIN, lanes), 0)
    )
    rowed = []
    for k in range(per):
        n = step * per + k
        rows = pl.ds(pl.multiple_of(n * WIN, WIN), WIN)
        row = jnp.concatenate([tiled_low[rows, :], tiled_high[rows, : lanes - 128]], axis=1)
        block = jnp.where(own_band, row[None], 0.0).reshape(BR, lanes).astype(jnp.bfloat16)
        rowed.append(
            jnp.dot(
                block, raw[k].reshape(lanes, 128), preferred_element_type=jnp.float32
            ).astype(jnp.bfloat16)
        )
    for k in range(per):
        n = step * per + k
        res[n] = jnp.dot(
            rowed[k], bank[bank_index[n]], preferred_element_type=jnp.float32
        ).astype(jnp.bfloat16)
    for k in range(per):
        n = step * per + k
        pltpu.make_async_copy(
            res.at[n], out.at[dest[n], pl.ds(pl.multiple_of(rank[n] * BR, 8), BR)], sem
        ).start()

    @pl.when(step == pl.num_programs(0) - 1)
    def _():
        pltpu.make_async_copy(res, res, sem).wait()
        pltpu.make_async_copy(tags_out, out.at[:, pl.ds(CAP * BR, 8)], tag_sem).wait()


def resample(raw, weights, bank, dest, window, bank_index, tiles):
    held = raw.shape[0]
    per = 32
    return pl.pallas_call(
        resample_kernel,
        grid=(held // per,),
        in_specs=[
            pl.BlockSpec(memory_space=pltpu.SMEM),
            pl.BlockSpec(memory_space=pltpu.SMEM),
            pl.BlockSpec(memory_space=pltpu.SMEM),
            pl.BlockSpec((per, BANDS, 16, 128), lambda i: (i, 0, 0, 0)),
            pl.BlockSpec((WIN, 16, held), lambda i: (0, 0, 0)),
            pl.BlockSpec(bank.shape, lambda i: (0, 0, 0)),
        ],
        out_specs=pl.BlockSpec(memory_space=pltpu.HBM),
        out_shape=jax.ShapeDtypeStruct((tiles, CAP * BR + 8, 128), jnp.bfloat16),
        scratch_shapes=[
            pltpu.VMEM((held * WIN, 128), jnp.float32),
            pltpu.VMEM((held * WIN, 128), jnp.float32),
            pltpu.VMEM((held, BR, 128), jnp.bfloat16),
            pltpu.VMEM((tiles, 8, 128), jnp.float32),
            pltpu.VMEM((tiles, 8, 128), jnp.bfloat16),
            pltpu.SMEM((tiles,), jnp.int32),
            pltpu.SMEM((held,), jnp.int32),
            pltpu.SemaphoreType.DMA,
            pltpu.SemaphoreType.DMA,
        ],
        compiler_params=pltpu.CompilerParams(vmem_limit_bytes=BIG_VMEM),
        name="resample",
    )(dest, window, bank_index, raw, jnp.transpose(weights, (1, 2, 0)), bank)


CHUNKS = 4
QUARTERS = 4


def gather_kernel(
    got,
    gridded_out,
    turned_out,
    held,
    gridded,
    turned,
    even,
    odd,
    tags,
    dense,
    window,
    inverse,
    tag_sem,
    dense_sem,
    chunk_sem,
    out_sem,
):
    tiles = got.shape[0]
    per = tiles // CHUNKS
    fetch = pltpu.make_async_copy(got.at[:, pl.ds(CAP * BR, 8)], tags, tag_sem)
    fetch.start()
    chunks = [
        pltpu.make_async_copy(
            got.at[pl.ds(i * per, per), pl.ds(0, CAP * BR)],
            held.at[pl.ds(i * per, per)],
            chunk_sem.at[i],
        )
        for i in range(CHUNKS)
    ]
    for chunk in chunks:
        chunk.start()
    even[...] = jnp.zeros_like(even)
    odd[...] = jnp.zeros_like(odd)
    fetch.wait()
    lane = lax.broadcasted_iota(jnp.int32, (8, 128), 1)
    total = jnp.zeros((8, 128), jnp.float32)
    for t in range(tiles):
        total = total + jnp.where(lane == t, tags[t].astype(jnp.float32), 0.0)
    dense[...] = total.astype(jnp.int32)
    scalars = pltpu.make_async_copy(dense, window, dense_sem)
    scalars.start()
    which = lax.broadcasted_iota(jnp.int32, (NWIN, 128), 0).astype(jnp.float32)
    hits = jnp.zeros((NWIN, 128), jnp.float32)
    for k in range(CAP):
        hits = hits + jnp.where(which == total[k : k + 1, :], 1.0, 0.0)
    counts = jnp.sum(hits, axis=1, keepdims=True)
    inverse[...] = jnp.broadcast_to(1.0 / jnp.maximum(counts, 1.0), (NWIN, 128))
    scalars.wait()

    for i in range(CHUNKS):
        chunks[i].wait()

        @pl.loop(0, per // 4)
        def _(group):
            for u in range(4):
                t = i * per + group * 4 + u
                for k, sums in ((0, even), (1, odd)):
                    sums[window[k, t]] += held[t, k * BR : (k + 1) * BR, :].astype(jnp.float32)

    pad = jnp.zeros((128 - BR, 128), jnp.float32)
    outs = []
    pairs = NWIN // 2 // QUARTERS
    for q in range(QUARTERS):
        for p in range(q * pairs, (q + 1) * pairs):
            pair = []
            for w in (2 * p, 2 * p + 1):
                mean = (even[w] + odd[w]) * inverse[w : w + 1, :]
                pair.append(mean)
                turned[w] = jnp.concatenate([mean, pad], axis=0).astype(jnp.bfloat16).T
            for b in range(BANDS):
                rows = slice(b * WIN, (b + 1) * WIN)
                gridded[b, p * 16 : (p + 1) * 16, :] = jnp.concatenate(
                    [pair[0][rows], pair[1][rows]], axis=0
                ).astype(jnp.bfloat16)
        wins = pl.ds(q * 2 * pairs, 2 * pairs)
        rows = pl.ds(q * 16 * pairs, 16 * pairs)
        outs.append(pltpu.make_async_copy(turned.at[wins], turned_out.at[wins], out_sem.at[q, 0]))
        outs.append(
            pltpu.make_async_copy(gridded.at[:, rows], gridded_out.at[:, rows], out_sem.at[q, 1])
        )
        outs[-2].start()
        outs[-1].start()
    for copy in outs:
        copy.wait()


def gather_windows(got):
    tiles = got.shape[0]
    hbm = pl.BlockSpec(memory_space=pltpu.HBM)
    grid_shape = (BANDS, NWIN * WIN, 128)
    turned_shape = (NWIN, 128, 128)
    return pl.pallas_call(
        gather_kernel,
        in_specs=[hbm],
        out_specs=[hbm, hbm],
        out_shape=[
            jax.ShapeDtypeStruct(grid_shape, jnp.bfloat16),
            jax.ShapeDtypeStruct(turned_shape, jnp.bfloat16),
        ],
        scratch_shapes=[
            pltpu.VMEM((tiles, CAP * BR, 128), jnp.bfloat16),
            pltpu.VMEM(grid_shape, jnp.bfloat16),
            pltpu.VMEM(turned_shape, jnp.bfloat16),
            pltpu.VMEM((NWIN + 1, BR, 128), jnp.float32),
            pltpu.VMEM((NWIN + 1, BR, 128), jnp.float32),
            pltpu.VMEM((tiles, 8, 128), jnp.bfloat16),
            pltpu.VMEM((8, 128), jnp.int32),
            pltpu.SMEM((8, 128), jnp.int32),
            pltpu.VMEM((NWIN, 128), jnp.float32),
            pltpu.SemaphoreType.DMA,
            pltpu.SemaphoreType.DMA,
            pltpu.SemaphoreType.DMA((CHUNKS,)),
            pltpu.SemaphoreType.DMA((QUARTERS, 2)),
        ],
        compiler_params=pltpu.CompilerParams(vmem_limit_bytes=BIG_VMEM),
        name="gather_windows",
    )(got)


HALO_WIN = HALO // WIN
WIDE_WIN = NWIN + 2 * HALO_WIN
WIDE_COL = 128 + 2 * HALO
MOVES = [(1, 0), (-1, 0), (0, 1), (0, -1), (1, 1), (1, -1), (-1, 1), (-1, -1)]


def rim_kernel(
    tile,
    rim_rows,
    rim_cols,
    edge_rows,
    edge_cols,
    zero_rows,
    zero_cols,
    edge_sem,
    zero_sem,
    send_sem,
    recv_sem,
):
    tx, ty = lax.axis_index("tx"), lax.axis_index("ty")
    nx, ny = lax.axis_size("tx"), lax.axis_size("ty")

    def inside(dx, dy):
        ok = None
        for d, at, n in ((dx, tx, nx), (dy, ty, ny)):
            if d:
                here = at + d >= 0 if d < 0 else at + d < n
                ok = here if ok is None else jnp.logical_and(ok, here)
        return ok

    def source(dx, dy):
        if dy == 0:
            return edge_cols.at[:, pl.ds(HALO if dx > 0 else 0, HALO)]
        c, cn = {-1: (0, HALO), 0: (0, 128), 1: (128 - HALO, HALO)}[dx]
        return edge_rows.at[pl.ds(HALO_WIN if dy > 0 else 0, HALO_WIN), pl.ds(c, cn)]

    def target(dx, dy):
        if dy == 0:
            return rim_cols.at[:, pl.ds(0 if dx > 0 else HALO, HALO)]
        c, cn = {-1: (HALO + 128, HALO), 0: (HALO, 128), 1: (0, HALO)}[dx]
        return rim_rows.at[pl.ds(0 if dy > 0 else HALO_WIN, HALO_WIN), pl.ds(c, cn)]

    barrier = pltpu.get_barrier_semaphore()
    for dx, dy in MOVES:

        @pl.when(inside(dx, dy))
        def _():
            pl.semaphore_signal(
                barrier, inc=1, device_id=(tx + dx, ty + dy), device_id_type=MESH
            )

    edges = [
        pltpu.make_async_copy(src, dst, edge_sem.at[i])
        for i, (src, dst) in enumerate(
            (
                (tile.at[pl.ds(0, HALO_WIN)], edge_rows.at[pl.ds(0, HALO_WIN)]),
                (
                    tile.at[pl.ds(NWIN - HALO_WIN, HALO_WIN)],
                    edge_rows.at[pl.ds(HALO_WIN, HALO_WIN)],
                ),
                (tile.at[:, pl.ds(0, HALO)], edge_cols.at[:, pl.ds(0, HALO)]),
                (tile.at[:, pl.ds(128 - HALO, HALO)], edge_cols.at[:, pl.ds(HALO, HALO)]),
            )
        )
    ]
    for edge in edges:
        edge.start()
    zero_rows[...] = jnp.zeros_like(zero_rows)
    zero_cols[...] = jnp.zeros_like(zero_cols)
    for edge in edges:
        edge.wait()
    peers = sum(inside(dx, dy).astype(jnp.int32) for dx, dy in MOVES)
    pl.semaphore_wait(barrier, peers)

    copies = []
    for i, (dx, dy) in enumerate(MOVES):
        send = pltpu.make_async_remote_copy(
            src_ref=source(dx, dy),
            dst_ref=target(dx, dy),
            send_sem=send_sem.at[i],
            recv_sem=recv_sem.at[i],
            device_id=(tx + dx, ty + dy),
            device_id_type=MESH,
        )
        zeros = zero_rows.at[:, pl.ds(0, HALO if dx else 128)] if dy else zero_cols
        blank = pltpu.make_async_copy(zeros, target(dx, dy), zero_sem.at[i])
        copies.append((send, blank, inside(dx, dy), inside(-dx, -dy)))
    for send, blank, goes, comes in copies:

        @pl.when(goes)
        def _():
            send.start()

        @pl.when(jnp.logical_not(comes))
        def _():
            blank.start()

    for send, blank, goes, comes in copies:

        @pl.when(goes)
        def _():
            send.wait_send()

        @pl.when(comes)
        def _():
            send.wait_recv()

        @pl.when(jnp.logical_not(comes))
        def _():
            blank.wait()


def rim(turned):
    moves = len(MOVES)
    vmem = pl.BlockSpec(memory_space=pltpu.VMEM)
    return pl.pallas_call(
        rim_kernel,
        in_specs=[pl.BlockSpec(memory_space=pl.ANY)],
        out_specs=[vmem, vmem],
        out_shape=[
            jax.ShapeDtypeStruct((2 * HALO_WIN, WIDE_COL, 128), jnp.bfloat16),
            jax.ShapeDtypeStruct((NWIN, 2 * HALO, 128), jnp.bfloat16),
        ],
        scratch_shapes=[
            pltpu.VMEM((2 * HALO_WIN, 128, 128), jnp.bfloat16),
            pltpu.VMEM((NWIN, 2 * HALO, 128), jnp.bfloat16),
            pltpu.VMEM((HALO_WIN, 128, 128), jnp.bfloat16),
            pltpu.VMEM((NWIN, HALO, 128), jnp.bfloat16),
            pltpu.SemaphoreType.DMA((4,)),
            pltpu.SemaphoreType.DMA((moves,)),
            pltpu.SemaphoreType.DMA((moves,)),
            pltpu.SemaphoreType.DMA((moves,)),
        ],
        compiler_params=pltpu.CompilerParams(
            collective_id=0, has_side_effects=True, vmem_limit_bytes=BIG_VMEM
        ),
        name="rim",
    )(turned)


FAR = 1 << 20
HALVES = 18
STEPS_ONE = 4
PAIRS = 40
PIX = 2 * PAIRS
ROWS_TWO = STEPS_ONE * HALVES
ROWS_THREE = 14
STEPS_THREE = 5
ROWS_FOUR = 17
STEPS_FOUR = 2
WIDE_FOUR = 24


def encoder_kernel(
    edges,
    tile,
    rim_rows,
    rim_cols,
    weight_one,
    reduce_two,
    hbm_two,
    hbm_reduce_three,
    hbm_three,
    hbm_reduce_four,
    hbm_four,
    out,
    wide,
    slab,
    patch,
    even_two,
    odd_two,
    carry_two,
    even_three,
    odd_three,
    carry_three,
    spread_three,
    taps_four,
    weight_two,
    reduce_three,
    weight_three,
    reduce_four,
    weight_four,
    sems,
    wide_sems,
):
    per = HALVES // 2
    parts = []
    for i in range(STEPS_ONE):
        low_win, high_win = max(i * per, HALO_WIN), min((i + 1) * per, HALO_WIN + NWIN)
        inner = pl.ds(low_win - HALO_WIN, high_win - low_win)
        outer = pl.ds(low_win, high_win - low_win)
        moves = [
            (tile.at[inner], wide.at[outer, pl.ds(HALO, 128)]),
            (rim_cols.at[inner, pl.ds(0, HALO)], wide.at[outer, pl.ds(0, HALO)]),
            (rim_cols.at[inner, pl.ds(HALO, HALO)], wide.at[outer, pl.ds(HALO + 128, HALO)]),
        ]
        if i == 0:
            moves.append((rim_rows.at[pl.ds(0, HALO_WIN)], wide.at[pl.ds(0, HALO_WIN)]))
        if i == STEPS_ONE - 1:
            moves.append(
                (rim_rows.at[pl.ds(HALO_WIN, HALO_WIN)], wide.at[pl.ds(WIDE_WIN - HALO_WIN, HALO_WIN)])
            )
        parts.append(
            [
                pltpu.make_async_copy(src, dst, wide_sems.at[i, j])
                for j, (src, dst) in enumerate(moves)
            ]
        )
    for copies in parts:
        for copy in copies:
            copy.start()
    fetches = [
        pltpu.make_async_copy(source, target, sems.at[i])
        for i, (source, target) in enumerate(
            (
                (hbm_two, weight_two),
                (hbm_reduce_three, reduce_three),
                (hbm_three, weight_three),
                (hbm_reduce_four, reduce_four),
                (hbm_four, weight_four),
            )
        )
    ]
    for fetch in fetches:
        fetch.start()

    def dot(a, b):
        return jnp.dot(a, b, preferred_element_type=jnp.float32)

    def bounds(tile_rows, tile_cols):
        return (
            jnp.where(edges[0] == 1, 0, -FAR),
            jnp.where(edges[1] == 1, tile_rows, FAR),
            jnp.where(edges[2] == 1, 0, -FAR),
            jnp.where(edges[3] == 1, tile_cols, FAR),
        )

    def on_map(value, row, col, limits):
        top, bottom, left, right = limits
        right = jnp.where(jnp.logical_and(row >= top, row < bottom), right, -FAR)
        return jnp.where(jnp.logical_and(col >= left, col < right), value, 0.0)

    def following(value, by):
        return pltpu.roll(value, value.shape[0] - by, 0)

    last = wide.shape[0] - 1
    cols = wide.shape[1]
    low = lax.broadcasted_iota(jnp.int32, (cols, 128), 1) % 8 < 4
    at = lax.broadcasted_iota(jnp.int32, (PIX, 128), 0)
    col_two = jnp.where(at < PAIRS, 2 * at, 2 * (at - PAIRS) + 1) - 7
    limits_two = bounds(128, 64)
    carry_two[...] = jnp.zeros_like(carry_two)
    for copy in parts[0]:
        copy.wait()

    @pl.loop(0, STEPS_ONE)
    def _(step):
        for i in range(1, STEPS_ONE):

            @pl.when(step == i - 1)
            def _():
                for copy in parts[i]:
                    copy.wait()

        for k in range(HALVES):
            w = step * (HALVES // 2) + k // 2
            here = wide[jnp.minimum(w, last)].astype(jnp.float32)
            if k % 2:
                after = wide[jnp.minimum(w + 1, last)].astype(jnp.float32)
                here = jnp.where(low, pltpu.roll(here, 124, 1), pltpu.roll(after, 4, 1))
            slab[k, pl.ds(0, cols), :] = here
            for q in range(4):
                both = [slab[k, pl.ds(first + q, PAIRS, stride=4), :] for first in (1, 3)]
                patch[k, :, q * 128 : (q + 1) * 128] = jnp.concatenate(both, axis=0).astype(
                    jnp.bfloat16
                )
        hidden = dot(patch[...].reshape(HALVES * PIX, 512), weight_one[...])
        hidden = jnp.maximum(hidden, 0.0).astype(jnp.bfloat16)
        down = [
            jnp.maximum(dot(hidden[:, e * 256 : (e + 1) * 256], reduce_two[...]), 0.0).reshape(
                HALVES, PIX, 128
            )
            for e in range(2)
        ]
        before = carry_two[...]
        for k in range(HALVES):
            h = step * HALVES + k
            lines = []
            for e in range(2):
                value = on_map(down[e][k], 2 * h + e - 7, col_two, limits_two)
                first, second = value[:PAIRS], value[PAIRS:]
                lines.append(
                    jnp.concatenate(
                        [first, second, following(first, 1), following(second, 1)], axis=1
                    )
                )
            even_two[h] = jnp.concatenate(lines, axis=0).astype(jnp.bfloat16)
            odd_two[h] = jnp.concatenate([before, lines[0]], axis=0).astype(jnp.bfloat16)
            before = lines[1]
        carry_two[...] = before

    fetches[0].wait()
    fetches[1].wait()
    col_three = lax.broadcasted_iota(jnp.int32, (PAIRS, 256), 0) - 3
    limits_three = bounds(64, 32)
    carry_three[...] = jnp.zeros_like(carry_three)
    size = ROWS_THREE * PIX

    @pl.loop(0, STEPS_THREE)
    def _(step):
        first = step * ROWS_THREE
        hidden = (
            dot(even_two[pl.ds(first, ROWS_THREE)].reshape(size, 512), weight_two[0])
            + dot(odd_two[pl.ds(first + 1, ROWS_THREE)].reshape(size, 512), weight_two[1])
            + dot(even_two[pl.ds(first + 1, ROWS_THREE)].reshape(size, 512), weight_two[2])
        )
        hidden = jnp.maximum(hidden, 0.0).reshape(ROWS_THREE, 2, PAIRS, 256)
        hidden = jnp.concatenate([hidden[:, 0], hidden[:, 1]], axis=-1)
        hidden = hidden.reshape(ROWS_THREE * PAIRS, 512).astype(jnp.bfloat16)
        down = jnp.maximum(dot(hidden, reduce_three[...]), 0.0).reshape(ROWS_THREE, PAIRS, 256)
        before = carry_three[...]
        for k in range(0, ROWS_THREE, 2):
            lines = []
            for e in range(2):
                value = on_map(down[k + e], first + k + e - 3, col_three, limits_three)
                lines.append(
                    jnp.concatenate([value, following(value, 1), following(value, 2)], axis=1)
                )
            i = step * (ROWS_THREE // 2) + k // 2
            even_three[i] = jnp.concatenate(lines, axis=0).astype(jnp.bfloat16)
            odd_three[i] = jnp.concatenate([before, lines[0]], axis=0).astype(jnp.bfloat16)
            before = lines[1]
        carry_three[...] = before

    fetches[2].wait()
    fetches[3].wait()
    col_four = lax.broadcasted_iota(jnp.int32, (WIDE_FOUR, 512), 0) - 1
    limits_four = bounds(32, 16)
    size_four = ROWS_FOUR * PIX

    @pl.loop(0, STEPS_FOUR)
    def _(step):
        first = step * ROWS_FOUR
        hidden = (
            dot(even_three[pl.ds(first, ROWS_FOUR)].reshape(size_four, 768), weight_three[0])
            + dot(odd_three[pl.ds(first + 1, ROWS_FOUR)].reshape(size_four, 768), weight_three[1])
            + dot(even_three[pl.ds(first + 1, ROWS_FOUR)].reshape(size_four, 768), weight_three[2])
        )
        hidden = jnp.maximum(hidden, 0.0)
        for half in range(2):
            spread_three[half, pl.ds(0, size_four), :] = hidden[:, half * 128 : (half + 1) * 128]
        rows = []
        for k in range(ROWS_FOUR):
            rows.append(
                jnp.concatenate(
                    [
                        spread_three[
                            half,
                            pl.ds(k * PIX + e * PAIRS + g, WIDE_FOUR, stride=2),
                            :,
                        ]
                        for e in range(2)
                        for g in range(2)
                        for half in range(2)
                    ],
                    axis=1,
                )
            )
        hidden = jnp.concatenate(rows, axis=0).astype(jnp.bfloat16)
        down = jnp.maximum(dot(hidden, reduce_four[...]), 0.0)
        for k in range(ROWS_FOUR):
            value = down[k * WIDE_FOUR : (k + 1) * WIDE_FOUR]
            value = on_map(value, first + k - 1, col_four, limits_four)
            taps_four[first + k] = jnp.concatenate(
                [value[:16], following(value, 1)[:16], following(value, 2)[:16]], axis=1
            ).astype(jnp.bfloat16)

    fetches[4].wait()
    for half in range(2):
        lanes = slice(half * 256, (half + 1) * 256)
        hidden = sum(
            dot(taps_four[u : u + 32].reshape(512, 1536), weight_four[u, :, lanes])
            for u in range(3)
        )
        out[:, lanes] = jnp.maximum(hidden, 0.0).astype(jnp.bfloat16)


def encode(tile, rims, edges, one, two, reduce_three, three, reduce_four, four, reduce_two):
    hbm = pl.BlockSpec(memory_space=pltpu.HBM)
    vmem = pl.BlockSpec(memory_space=pltpu.VMEM)
    big = (two, reduce_three, three, reduce_four, four)
    return pl.pallas_call(
        encoder_kernel,
        in_specs=[pl.BlockSpec(memory_space=pltpu.SMEM)]
        + [hbm] * 3
        + [vmem] * 2
        + [hbm] * len(big),
        out_specs=vmem,
        out_shape=jax.ShapeDtypeStruct((512, 512), jnp.bfloat16),
        scratch_shapes=[
            pltpu.VMEM((WIDE_WIN, WIDE_COL, 128), jnp.bfloat16),
            pltpu.VMEM((HALVES, 168, 128), jnp.float32),
            pltpu.VMEM((HALVES, PIX, 512), jnp.bfloat16),
            pltpu.VMEM((ROWS_TWO, PIX, 512), jnp.bfloat16),
            pltpu.VMEM((ROWS_TWO, PIX, 512), jnp.bfloat16),
            pltpu.VMEM((PAIRS, 512), jnp.float32),
            pltpu.VMEM((STEPS_FOUR * ROWS_FOUR + 1, PIX, 768), jnp.bfloat16),
            pltpu.VMEM((STEPS_FOUR * ROWS_FOUR + 1, PIX, 768), jnp.bfloat16),
            pltpu.VMEM((PAIRS, 768), jnp.float32),
            pltpu.VMEM((2, ROWS_FOUR * PIX + 16, 128), jnp.float32),
            pltpu.VMEM((STEPS_FOUR * ROWS_FOUR, 16, 1536), jnp.bfloat16),
        ]
        + [pltpu.VMEM(w.shape, jnp.bfloat16) for w in big]
        + [pltpu.SemaphoreType.DMA((len(big),)), pltpu.SemaphoreType.DMA((STEPS_ONE, 4))],
        compiler_params=pltpu.CompilerParams(vmem_limit_bytes=BIG_VMEM),
        name="encoder",
    )(edges, tile, *rims, one, reduce_two, *big)


def patch_weights(kernel):
    rows = np.zeros((8, 4, 3), np.float32)
    for r in range(8):
        for y in range(4):
            u = r - (2 + y) + 1
            if 0 <= u < 3:
                rows[r, y, u] = 1
    cols = np.zeros((4, 2, 3), np.float32)
    for q in range(4):
        for g in range(2):
            v = q - g
            if 0 <= v < 3:
                cols[q, g, v] = 1
    spread = jnp.einsum("ryu,uvbo->rybvo", jnp.asarray(rows, jnp.bfloat16), kernel)
    spread = jnp.einsum("qgv,rybvo->qbrygo", jnp.asarray(cols, jnp.bfloat16), spread)
    spread = spread.reshape(4, BR, 512).astype(jnp.bfloat16)
    return jnp.pad(spread, ((0, 0), (0, 128 - BR), (0, 0))).reshape(512, 512)


def pair_weights(kernel):
    taps = jnp.stack(
        [jnp.pad(kernel, ((0, 0), (g, 1 - g), (0, 0), (0, 0))) for g in range(2)], axis=3
    )
    return taps.reshape(3, 512, 256)


def body(
    granule_blocks,
    row_weights,
    column_bank,
    destination,
    window_index,
    bank_index,
    kernel_one,
    reduce_two,
    kernel_two,
    reduce_three,
    kernel_three,
    reduce_four,
    kernel_four,
):
    nx, ny = lax.axis_size("tx"), lax.axis_size("ty")
    tx, ty = lax.axis_index("tx"), lax.axis_index("ty")
    tiles = nx * ny
    sent = resample(
        granule_blocks, row_weights, column_bank, destination, window_index, bank_index, tiles
    )
    got = lax.all_to_all(sent, ("tx", "ty"), split_axis=0, concat_axis=0, tiled=True)
    gridded, turned = gather_windows(got)
    edges = jnp.stack([ty == 0, ty == ny - 1, tx == 0, tx == nx - 1]).astype(jnp.int32)
    bottleneck = encode(
        turned,
        rim(turned),
        edges,
        patch_weights(kernel_one),
        pair_weights(kernel_two),
        reduce_three.reshape(512, 256),
        kernel_three.reshape(3, 768, 256),
        reduce_four.reshape(1024, 512),
        kernel_four.reshape(3, 1536, 512),
        reduce_two.reshape(256, 128),
    )
    return (gridded, jnp.transpose(bottleneck.reshape(32, 16, 512), (2, 0, 1)))


def solution(mesh):
    in_specs = (
        P(("tx", "ty"), None, None, None),
        P(("tx", "ty"), None, None),
        P(),
        P(("tx", "ty")),
        P(("tx", "ty")),
        P(("tx", "ty")),
        P(),
        P(),
        P(),
        P(),
        P(),
        P(),
        P(),
    )
    out_specs = (P(None, "ty", "tx"), P(None, "ty", "tx"))
    return jax.shard_map(body, mesh=mesh, in_specs=in_specs, out_specs=out_specs, check_vma=False)
```

```python
import functools

import jax
import jax.numpy as jnp
import numpy as np
from jax import lax
from jax.experimental import pallas as pl
from jax.experimental.pallas import tpu as pltpu
from jax.sharding import PartitionSpec as P

MESH = pl.DeviceIdType.MESH
BANDS = 13
CAP = 2
WIN = 8
NWIN = 32
BR = BANDS * WIN
HALO = 16
BIG_VMEM = 58 << 20


def resample_kernel(
    dest,
    window,
    bank_index,
    raw,
    weights,
    bank,
    out,
    tiled_low,
    tiled_high,
    res,
    tags,
    tags_out,
    count,
    rank,
    sem,
    tag_sem,
):
    step = pl.program_id(0)
    per = raw.shape[0]
    held = res.shape[0]
    tiles = out.shape[0]
    lanes = BANDS * 16

    @pl.when(step == 0)
    def _():
        spread = (
            lax.broadcasted_iota(jnp.int32, (16, 256), 1) % 16
            == lax.broadcasted_iota(jnp.int32, (16, 256), 0)
        ).astype(jnp.bfloat16)
        for r in range(WIN):
            both = lax.dot_general(
                weights[r],
                spread,
                (((0,), (0,)), ((), ())),
                preferred_element_type=jnp.float32,
            )
            tiled_low[pl.ds(r, held, stride=WIN), :] = both[:, :128]
            tiled_high[pl.ds(r, held, stride=WIN), :] = both[:, 128:]
        tags[...] = jnp.full_like(tags, float(NWIN))

        @pl.loop(0, tiles // 8)
        def _(t):
            for u in range(8):
                count[t * 8 + u] = 0

        @pl.loop(0, held // 4)
        def _(group):
            for u in range(4):
                n = group * 4 + u
                tile = dest[n]
                place = count[tile]
                rank[n] = place
                count[tile] = place + 1
                tags[tile, pl.ds(place, 1), :] = jnp.full((1, 128), window[n], jnp.int32).astype(
                    jnp.float32
                )

        tags_out[...] = tags[...].astype(jnp.bfloat16)
        pltpu.make_async_copy(tags_out, out.at[:, pl.ds(CAP * BR, 8)], tag_sem).start()

    own_band = (
        lax.broadcasted_iota(jnp.int32, (BANDS, WIN, lanes), 2) // 16
        == lax.broadcasted_iota(jnp.int32, (BANDS, WIN, lanes), 0)
    )
    rowed = []
    for k in range(per):
        n = step * per + k
        rows = pl.ds(pl.multiple_of(n * WIN, WIN), WIN)
        row = jnp.concatenate([tiled_low[rows, :], tiled_high[rows, : lanes - 128]], axis=1)
        block = jnp.where(own_band, row[None], 0.0).reshape(BR, lanes).astype(jnp.bfloat16)
        rowed.append(
            jnp.dot(
                block, raw[k].reshape(lanes, 128), preferred_element_type=jnp.float32
            ).astype(jnp.bfloat16)
        )
    for k in range(per):
        n = step * per + k
        res[n] = jnp.dot(
            rowed[k], bank[bank_index[n]], preferred_element_type=jnp.float32
        ).astype(jnp.bfloat16)
    for k in range(per):
        n = step * per + k
        pltpu.make_async_copy(
            res.at[n], out.at[dest[n], pl.ds(pl.multiple_of(rank[n] * BR, 8), BR)], sem
        ).start()

    @pl.when(step == pl.num_programs(0) - 1)
    def _():
        pltpu.make_async_copy(res, res, sem).wait()
        pltpu.make_async_copy(tags_out, out.at[:, pl.ds(CAP * BR, 8)], tag_sem).wait()


def resample(raw, weights, bank, dest, window, bank_index, tiles):
    held = raw.shape[0]
    per = 32
    return pl.pallas_call(
        resample_kernel,
        grid=(held // per,),
        in_specs=[
            pl.BlockSpec(memory_space=pltpu.SMEM),
            pl.BlockSpec(memory_space=pltpu.SMEM),
            pl.BlockSpec(memory_space=pltpu.SMEM),
            pl.BlockSpec((per, BANDS, 16, 128), lambda i: (i, 0, 0, 0)),
            pl.BlockSpec((WIN, 16, held), lambda i: (0, 0, 0)),
            pl.BlockSpec(bank.shape, lambda i: (0, 0, 0)),
        ],
        out_specs=pl.BlockSpec(memory_space=pltpu.HBM),
        out_shape=jax.ShapeDtypeStruct((tiles, CAP * BR + 8, 128), jnp.bfloat16),
        scratch_shapes=[
            pltpu.VMEM(((held + 1) * WIN, 128), jnp.float32),
            pltpu.VMEM(((held + 1) * WIN, 128), jnp.float32),
            pltpu.VMEM((held, BR, 128), jnp.bfloat16),
            pltpu.VMEM((tiles, 8, 128), jnp.float32),
            pltpu.VMEM((tiles, 8, 128), jnp.bfloat16),
            pltpu.SMEM((tiles,), jnp.int32),
            pltpu.SMEM((held,), jnp.int32),
            pltpu.SemaphoreType.DMA,
            pltpu.SemaphoreType.DMA,
        ],
        compiler_params=pltpu.CompilerParams(vmem_limit_bytes=BIG_VMEM),
        name="resample",
    )(dest, window, bank_index, raw, jnp.transpose(weights, (1, 2, 0)), bank)


CHUNKS = 4
QUARTERS = 4


def gather_kernel(
    got,
    gridded_out,
    turned_out,
    held,
    gridded,
    turned,
    even,
    odd,
    tags,
    dense,
    window,
    inverse,
    tag_sem,
    dense_sem,
    chunk_sem,
    out_sem,
):
    tiles = got.shape[0]
    per = tiles // CHUNKS
    fetch = pltpu.make_async_copy(got.at[:, pl.ds(CAP * BR, 8)], tags, tag_sem)
    fetch.start()
    chunks = [
        pltpu.make_async_copy(
            got.at[pl.ds(i * per, per), pl.ds(0, CAP * BR)],
            held.at[pl.ds(i * per, per)],
            chunk_sem.at[i],
        )
        for i in range(CHUNKS)
    ]
    for chunk in chunks:
        chunk.start()
    even[...] = jnp.zeros_like(even)
    odd[...] = jnp.zeros_like(odd)
    fetch.wait()
    lane = lax.broadcasted_iota(jnp.int32, (8, 128), 1)
    total = jnp.zeros((8, 128), jnp.float32)
    for t in range(tiles):
        total = total + jnp.where(lane == t, tags[t].astype(jnp.float32), 0.0)
    dense[...] = total.astype(jnp.int32)
    scalars = pltpu.make_async_copy(dense, window, dense_sem)
    scalars.start()
    which = lax.broadcasted_iota(jnp.int32, (NWIN, 128), 0).astype(jnp.float32)
    hits = jnp.zeros((NWIN, 128), jnp.float32)
    for k in range(CAP):
        hits = hits + jnp.where(which == total[k : k + 1, :], 1.0, 0.0)
    counts = jnp.sum(hits, axis=1, keepdims=True)
    inverse[...] = jnp.broadcast_to(1.0 / jnp.maximum(counts, 1.0), (NWIN, 128))
    scalars.wait()

    for i in range(CHUNKS):
        chunks[i].wait()

        @pl.loop(0, per // 4)
        def _(group):
            for u in range(4):
                t = i * per + group * 4 + u
                for k, sums in ((0, even), (1, odd)):
                    sums[window[k, t]] += held[t, k * BR : (k + 1) * BR, :].astype(jnp.float32)

    pad = jnp.zeros((128 - BR, 128), jnp.float32)
    outs = []
    pairs = NWIN // 2 // QUARTERS
    for q in range(QUARTERS):
        for p in range(q * pairs, (q + 1) * pairs):
            pair = []
            for w in (2 * p, 2 * p + 1):
                mean = (even[w] + odd[w]) * inverse[w : w + 1, :]
                pair.append(mean)
                turned[w] = jnp.concatenate([mean, pad], axis=0).astype(jnp.bfloat16).T
            for b in range(BANDS):
                rows = slice(b * WIN, (b + 1) * WIN)
                gridded[b, p * 16 : (p + 1) * 16, :] = jnp.concatenate(
                    [pair[0][rows], pair[1][rows]], axis=0
                ).astype(jnp.bfloat16)
        wins = pl.ds(q * 2 * pairs, 2 * pairs)
        rows = pl.ds(q * 16 * pairs, 16 * pairs)
        outs.append(pltpu.make_async_copy(turned.at[wins], turned_out.at[wins], out_sem.at[q, 0]))
        outs.append(
            pltpu.make_async_copy(gridded.at[:, rows], gridded_out.at[:, rows], out_sem.at[q, 1])
        )
        outs[-2].start()
        outs[-1].start()
    for copy in outs:
        copy.wait()


def gather_windows(got):
    tiles = got.shape[0]
    hbm = pl.BlockSpec(memory_space=pltpu.HBM)
    grid_shape = (BANDS, NWIN * WIN, 128)
    turned_shape = (NWIN, 128, 128)
    return pl.pallas_call(
        gather_kernel,
        in_specs=[hbm],
        out_specs=[hbm, hbm],
        out_shape=[
            jax.ShapeDtypeStruct(grid_shape, jnp.bfloat16),
            jax.ShapeDtypeStruct(turned_shape, jnp.bfloat16),
        ],
        scratch_shapes=[
            pltpu.VMEM((tiles, CAP * BR, 128), jnp.bfloat16),
            pltpu.VMEM(grid_shape, jnp.bfloat16),
            pltpu.VMEM(turned_shape, jnp.bfloat16),
            pltpu.VMEM((NWIN + 1, BR, 128), jnp.float32),
            pltpu.VMEM((NWIN + 1, BR, 128), jnp.float32),
            pltpu.VMEM((tiles, 8, 128), jnp.bfloat16),
            pltpu.VMEM((8, 128), jnp.int32),
            pltpu.SMEM((8, 128), jnp.int32),
            pltpu.VMEM((NWIN, 128), jnp.float32),
            pltpu.SemaphoreType.DMA,
            pltpu.SemaphoreType.DMA,
            pltpu.SemaphoreType.DMA((CHUNKS,)),
            pltpu.SemaphoreType.DMA((QUARTERS, 2)),
        ],
        compiler_params=pltpu.CompilerParams(vmem_limit_bytes=BIG_VMEM),
        name="gather_windows",
    )(got)


HALO_WIN = HALO // WIN
WIDE_WIN = NWIN + 2 * HALO_WIN
WIDE_COL = 128 + 2 * HALO
MOVES = [(1, 0), (-1, 0), (0, 1), (0, -1), (1, 1), (1, -1), (-1, 1), (-1, -1)]


def rim_kernel(
    tile,
    rim_rows,
    rim_cols,
    edge_rows,
    edge_cols,
    zero_rows,
    zero_cols,
    edge_sem,
    zero_sem,
    send_sem,
    recv_sem,
):
    tx, ty = lax.axis_index("tx"), lax.axis_index("ty")
    nx, ny = lax.axis_size("tx"), lax.axis_size("ty")

    def inside(dx, dy):
        ok = None
        for d, at, n in ((dx, tx, nx), (dy, ty, ny)):
            if d:
                here = at + d >= 0 if d < 0 else at + d < n
                ok = here if ok is None else jnp.logical_and(ok, here)
        return ok

    def source(dx, dy):
        if dy == 0:
            return edge_cols.at[:, pl.ds(HALO if dx > 0 else 0, HALO)]
        c, cn = {-1: (0, HALO), 0: (0, 128), 1: (128 - HALO, HALO)}[dx]
        return edge_rows.at[pl.ds(HALO_WIN if dy > 0 else 0, HALO_WIN), pl.ds(c, cn)]

    def target(dx, dy):
        if dy == 0:
            return rim_cols.at[:, pl.ds(0 if dx > 0 else HALO, HALO)]
        c, cn = {-1: (HALO + 128, HALO), 0: (HALO, 128), 1: (0, HALO)}[dx]
        return rim_rows.at[pl.ds(0 if dy > 0 else HALO_WIN, HALO_WIN), pl.ds(c, cn)]

    barrier = pltpu.get_barrier_semaphore()
    for dx, dy in MOVES:

        @pl.when(inside(dx, dy))
        def _():
            pl.semaphore_signal(
                barrier, inc=1, device_id=(tx + dx, ty + dy), device_id_type=MESH
            )

    edges = [
        pltpu.make_async_copy(src, dst, edge_sem.at[i])
        for i, (src, dst) in enumerate(
            (
                (tile.at[pl.ds(0, HALO_WIN)], edge_rows.at[pl.ds(0, HALO_WIN)]),
                (
                    tile.at[pl.ds(NWIN - HALO_WIN, HALO_WIN)],
                    edge_rows.at[pl.ds(HALO_WIN, HALO_WIN)],
                ),
                (tile.at[:, pl.ds(0, HALO)], edge_cols.at[:, pl.ds(0, HALO)]),
                (tile.at[:, pl.ds(128 - HALO, HALO)], edge_cols.at[:, pl.ds(HALO, HALO)]),
            )
        )
    ]
    for edge in edges:
        edge.start()
    zero_rows[...] = jnp.zeros_like(zero_rows)
    zero_cols[...] = jnp.zeros_like(zero_cols)
    for edge in edges:
        edge.wait()
    peers = sum(inside(dx, dy).astype(jnp.int32) for dx, dy in MOVES)
    pl.semaphore_wait(barrier, peers)

    copies = []
    for i, (dx, dy) in enumerate(MOVES):
        send = pltpu.make_async_remote_copy(
            src_ref=source(dx, dy),
            dst_ref=target(dx, dy),
            send_sem=send_sem.at[i],
            recv_sem=recv_sem.at[i],
            device_id=(tx + dx, ty + dy),
            device_id_type=MESH,
        )
        zeros = zero_rows.at[:, pl.ds(0, HALO if dx else 128)] if dy else zero_cols
        blank = pltpu.make_async_copy(zeros, target(dx, dy), zero_sem.at[i])
        copies.append((send, blank, inside(dx, dy), inside(-dx, -dy)))
    for send, blank, goes, comes in copies:

        @pl.when(goes)
        def _():
            send.start()

        @pl.when(jnp.logical_not(comes))
        def _():
            blank.start()

    for send, blank, goes, comes in copies:

        @pl.when(goes)
        def _():
            send.wait_send()

        @pl.when(comes)
        def _():
            send.wait_recv()

        @pl.when(jnp.logical_not(comes))
        def _():
            blank.wait()


def rim(turned):
    moves = len(MOVES)
    return pl.pallas_call(
        rim_kernel,
        in_specs=[pl.BlockSpec(memory_space=pl.ANY)],
        out_specs=[pl.BlockSpec(memory_space=pl.ANY)] * 2,
        out_shape=[
            jax.ShapeDtypeStruct((2 * HALO_WIN, WIDE_COL, 128), jnp.bfloat16),
            jax.ShapeDtypeStruct((NWIN, 2 * HALO, 128), jnp.bfloat16),
        ],
        scratch_shapes=[
            pltpu.VMEM((2 * HALO_WIN, 128, 128), jnp.bfloat16),
            pltpu.VMEM((NWIN, 2 * HALO, 128), jnp.bfloat16),
            pltpu.VMEM((HALO_WIN, 128, 128), jnp.bfloat16),
            pltpu.VMEM((NWIN, HALO, 128), jnp.bfloat16),
            pltpu.SemaphoreType.DMA((4,)),
            pltpu.SemaphoreType.DMA((moves,)),
            pltpu.SemaphoreType.DMA((moves,)),
            pltpu.SemaphoreType.DMA((moves,)),
        ],
        compiler_params=pltpu.CompilerParams(
            collective_id=0, has_side_effects=True, vmem_limit_bytes=BIG_VMEM
        ),
        name="rim",
    )(turned)


FAR = 1 << 20
HALVES = 18
STEPS_ONE = 4
PAIRS = 40
PIX = 2 * PAIRS
ROWS_TWO = STEPS_ONE * HALVES
ROWS_THREE = 14
STEPS_THREE = 5
ROWS_FOUR = 17
STEPS_FOUR = 2
WIDE_FOUR = 24


def encoder_kernel(
    edges,
    tile,
    rim_rows,
    rim_cols,
    hbm_one,
    hbm_reduce_two,
    hbm_two,
    hbm_reduce_three,
    hbm_three,
    hbm_reduce_four,
    hbm_four,
    out,
    wide,
    slab,
    patch,
    even_two,
    odd_two,
    carry_two,
    even_three,
    odd_three,
    carry_three,
    spread_three,
    taps_four,
    weight_one,
    reduce_two,
    weight_two,
    reduce_three,
    weight_three,
    reduce_four,
    weight_four,
    sems,
    wide_sems,
):
    per = HALVES // 2
    parts = []
    for i in range(STEPS_ONE):
        low_win, high_win = max(i * per, HALO_WIN), min((i + 1) * per, HALO_WIN + NWIN)
        inner = pl.ds(low_win - HALO_WIN, high_win - low_win)
        outer = pl.ds(low_win, high_win - low_win)
        moves = [
            (tile.at[inner], wide.at[outer, pl.ds(HALO, 128)]),
            (rim_cols.at[inner, pl.ds(0, HALO)], wide.at[outer, pl.ds(0, HALO)]),
            (rim_cols.at[inner, pl.ds(HALO, HALO)], wide.at[outer, pl.ds(HALO + 128, HALO)]),
        ]
        if i == 0:
            moves.append((rim_rows.at[pl.ds(0, HALO_WIN)], wide.at[pl.ds(0, HALO_WIN)]))
        if i == STEPS_ONE - 1:
            moves.append(
                (rim_rows.at[pl.ds(HALO_WIN, HALO_WIN)], wide.at[pl.ds(WIDE_WIN - HALO_WIN, HALO_WIN)])
            )
        parts.append(
            [
                pltpu.make_async_copy(src, dst, wide_sems.at[i, j])
                for j, (src, dst) in enumerate(moves)
            ]
        )
    fetches = [
        pltpu.make_async_copy(source, target, sems.at[i])
        for i, (source, target) in enumerate(
            (
                (hbm_one, weight_one),
                (hbm_reduce_two, reduce_two),
                (hbm_two, weight_two),
                (hbm_reduce_three, reduce_three),
                (hbm_three, weight_three),
                (hbm_reduce_four, reduce_four),
                (hbm_four, weight_four),
            )
        )
    ]
    for copy in parts[0] + fetches[:2] + sum(parts[1:], []) + fetches[2:]:
        copy.start()

    def dot(a, b):
        return jnp.dot(a, b, preferred_element_type=jnp.float32)

    def bounds(tile_rows, tile_cols):
        return (
            jnp.where(edges[0] == 1, 0, -FAR),
            jnp.where(edges[1] == 1, tile_rows, FAR),
            jnp.where(edges[2] == 1, 0, -FAR),
            jnp.where(edges[3] == 1, tile_cols, FAR),
        )

    def on_map(value, row, col, limits):
        top, bottom, left, right = limits
        right = jnp.where(jnp.logical_and(row >= top, row < bottom), right, -FAR)
        return jnp.where(jnp.logical_and(col >= left, col < right), value, 0.0)

    def following(value, by):
        return pltpu.roll(value, value.shape[0] - by, 0)

    last = wide.shape[0] - 1
    cols = wide.shape[1]
    low = lax.broadcasted_iota(jnp.int32, (cols, 128), 1) % 8 < 4
    at = lax.broadcasted_iota(jnp.int32, (PIX, 128), 0)
    col_two = jnp.where(at < PAIRS, 2 * at, 2 * (at - PAIRS) + 1) - 7
    limits_two = bounds(128, 64)
    carry_two[...] = jnp.zeros_like(carry_two)
    for copy in parts[0] + fetches[:2]:
        copy.wait()

    @pl.loop(0, STEPS_ONE)
    def _(step):
        for i in range(1, STEPS_ONE):

            @pl.when(step == i - 1)
            def _():
                for copy in parts[i]:
                    copy.wait()

        for k in range(HALVES):
            w = step * (HALVES // 2) + k // 2
            here = wide[jnp.minimum(w, last)].astype(jnp.float32)
            if k % 2:
                after = wide[jnp.minimum(w + 1, last)].astype(jnp.float32)
                here = jnp.where(low, pltpu.roll(here, 124, 1), pltpu.roll(after, 4, 1))
            slab[k, pl.ds(0, cols), :] = here
            for q in range(4):
                both = [slab[k, pl.ds(first + q, PAIRS, stride=4), :] for first in (1, 3)]
                patch[k, :, q * 128 : (q + 1) * 128] = jnp.concatenate(both, axis=0).astype(
                    jnp.bfloat16
                )
        hidden = dot(patch[...].reshape(HALVES * PIX, 512), weight_one[...])
        hidden = jnp.maximum(hidden, 0.0).astype(jnp.bfloat16)
        down = [
            jnp.maximum(dot(hidden[:, e * 256 : (e + 1) * 256], reduce_two[...]), 0.0).reshape(
                HALVES, PIX, 128
            )
            for e in range(2)
        ]
        before = carry_two[...]
        for k in range(HALVES):
            h = step * HALVES + k
            lines = []
            for e in range(2):
                value = on_map(down[e][k], 2 * h + e - 7, col_two, limits_two)
                first, second = value[:PAIRS], value[PAIRS:]
                lines.append(
                    jnp.concatenate(
                        [first, second, following(first, 1), following(second, 1)], axis=1
                    )
                )
            even_two[h] = jnp.concatenate(lines, axis=0).astype(jnp.bfloat16)
            odd_two[h] = jnp.concatenate([before, lines[0]], axis=0).astype(jnp.bfloat16)
            before = lines[1]
        carry_two[...] = before

    fetches[2].wait()
    fetches[3].wait()
    col_three = lax.broadcasted_iota(jnp.int32, (PAIRS, 256), 0) - 3
    limits_three = bounds(64, 32)
    carry_three[...] = jnp.zeros_like(carry_three)
    size = ROWS_THREE * PIX

    @pl.loop(0, STEPS_THREE)
    def _(step):
        first = step * ROWS_THREE
        hidden = (
            dot(even_two[pl.ds(first, ROWS_THREE)].reshape(size, 512), weight_two[0])
            + dot(odd_two[pl.ds(first + 1, ROWS_THREE)].reshape(size, 512), weight_two[1])
            + dot(even_two[pl.ds(first + 1, ROWS_THREE)].reshape(size, 512), weight_two[2])
        )
        hidden = jnp.maximum(hidden, 0.0).reshape(ROWS_THREE, 2, PAIRS, 256)
        hidden = jnp.concatenate([hidden[:, 0], hidden[:, 1]], axis=-1)
        hidden = hidden.reshape(ROWS_THREE * PAIRS, 512).astype(jnp.bfloat16)
        down = jnp.maximum(dot(hidden, reduce_three[...]), 0.0).reshape(ROWS_THREE, PAIRS, 256)
        before = carry_three[...]
        for k in range(0, ROWS_THREE, 2):
            lines = []
            for e in range(2):
                value = on_map(down[k + e], first + k + e - 3, col_three, limits_three)
                lines.append(
                    jnp.concatenate([value, following(value, 1), following(value, 2)], axis=1)
                )
            i = step * (ROWS_THREE // 2) + k // 2
            even_three[i] = jnp.concatenate(lines, axis=0).astype(jnp.bfloat16)
            odd_three[i] = jnp.concatenate([before, lines[0]], axis=0).astype(jnp.bfloat16)
            before = lines[1]
        carry_three[...] = before

    fetches[4].wait()
    fetches[5].wait()
    col_four = lax.broadcasted_iota(jnp.int32, (WIDE_FOUR, 512), 0) - 1
    limits_four = bounds(32, 16)
    size_four = ROWS_FOUR * PIX

    @pl.loop(0, STEPS_FOUR)
    def _(step):
        first = step * ROWS_FOUR
        hidden = (
            dot(even_three[pl.ds(first, ROWS_FOUR)].reshape(size_four, 768), weight_three[0])
            + dot(odd_three[pl.ds(first + 1, ROWS_FOUR)].reshape(size_four, 768), weight_three[1])
            + dot(even_three[pl.ds(first + 1, ROWS_FOUR)].reshape(size_four, 768), weight_three[2])
        )
        hidden = jnp.maximum(hidden, 0.0)
        for half in range(2):
            spread_three[half, pl.ds(0, size_four), :] = hidden[:, half * 128 : (half + 1) * 128]
        rows = []
        for k in range(ROWS_FOUR):
            rows.append(
                jnp.concatenate(
                    [
                        spread_three[
                            half,
                            pl.ds(k * PIX + e * PAIRS + g, WIDE_FOUR, stride=2),
                            :,
                        ]
                        for e in range(2)
                        for g in range(2)
                        for half in range(2)
                    ],
                    axis=1,
                )
            )
        hidden = jnp.concatenate(rows, axis=0).astype(jnp.bfloat16)
        down = jnp.maximum(dot(hidden, reduce_four[...]), 0.0)
        for k in range(ROWS_FOUR):
            value = down[k * WIDE_FOUR : (k + 1) * WIDE_FOUR]
            value = on_map(value, first + k - 1, col_four, limits_four)
            taps_four[first + k] = jnp.concatenate(
                [value[:16], following(value, 1)[:16], following(value, 2)[:16]], axis=1
            ).astype(jnp.bfloat16)

    fetches[6].wait()
    for half in range(2):
        lanes = slice(half * 256, (half + 1) * 256)
        hidden = sum(
            dot(taps_four[u : u + 32].reshape(512, 1536), weight_four[u, :, lanes])
            for u in range(3)
        )
        out[:, lanes] = jnp.maximum(hidden, 0.0).astype(jnp.bfloat16)


def encode(tile, rims, edges, one, two, reduce_three, three, reduce_four, four, reduce_two):
    hbm = pl.BlockSpec(memory_space=pltpu.HBM)
    big = (one, reduce_two, two, reduce_three, three, reduce_four, four)
    return pl.pallas_call(
        encoder_kernel,
        in_specs=[pl.BlockSpec(memory_space=pltpu.SMEM)] + [hbm] * (3 + len(big)),
        out_specs=pl.BlockSpec(memory_space=pltpu.VMEM),
        out_shape=jax.ShapeDtypeStruct((512, 512), jnp.bfloat16),
        scratch_shapes=[
            pltpu.VMEM((WIDE_WIN, WIDE_COL, 128), jnp.bfloat16),
            pltpu.VMEM((HALVES, 168, 128), jnp.float32),
            pltpu.VMEM((HALVES, PIX, 512), jnp.bfloat16),
            pltpu.VMEM((ROWS_TWO, PIX, 512), jnp.bfloat16),
            pltpu.VMEM((ROWS_TWO, PIX, 512), jnp.bfloat16),
            pltpu.VMEM((PAIRS, 512), jnp.float32),
            pltpu.VMEM((STEPS_FOUR * ROWS_FOUR + 1, PIX, 768), jnp.bfloat16),
            pltpu.VMEM((STEPS_FOUR * ROWS_FOUR + 1, PIX, 768), jnp.bfloat16),
            pltpu.VMEM((PAIRS, 768), jnp.float32),
            pltpu.VMEM((2, ROWS_FOUR * PIX + 16, 128), jnp.float32),
            pltpu.VMEM((STEPS_FOUR * ROWS_FOUR, 16, 1536), jnp.bfloat16),
        ]
        + [pltpu.VMEM(w.shape, jnp.bfloat16) for w in big]
        + [pltpu.SemaphoreType.DMA((len(big),)), pltpu.SemaphoreType.DMA((STEPS_ONE, 4))],
        compiler_params=pltpu.CompilerParams(vmem_limit_bytes=BIG_VMEM),
        name="encoder",
    )(edges, tile, *rims, *big)


def patch_weights(kernel):
    rows = np.zeros((8, 4, 3), np.float32)
    for r in range(8):
        for y in range(4):
            u = r - (2 + y) + 1
            if 0 <= u < 3:
                rows[r, y, u] = 1
    cols = np.zeros((4, 2, 3), np.float32)
    for q in range(4):
        for g in range(2):
            v = q - g
            if 0 <= v < 3:
                cols[q, g, v] = 1
    spread = jnp.einsum("ryu,uvbo->rybvo", jnp.asarray(rows, jnp.bfloat16), kernel)
    spread = jnp.einsum("qgv,rybvo->qbrygo", jnp.asarray(cols, jnp.bfloat16), spread)
    spread = spread.reshape(4, BR, 512).astype(jnp.bfloat16)
    return jnp.pad(spread, ((0, 0), (0, 128 - BR), (0, 0))).reshape(512, 512)


def pair_weights(kernel):
    taps = jnp.stack(
        [jnp.pad(kernel, ((0, 0), (g, 1 - g), (0, 0), (0, 0))) for g in range(2)], axis=3
    )
    return taps.reshape(3, 512, 256)


def body(
    granule_blocks,
    row_weights,
    column_bank,
    destination,
    window_index,
    bank_index,
    kernel_one,
    reduce_two,
    kernel_two,
    reduce_three,
    kernel_three,
    reduce_four,
    kernel_four,
):
    nx, ny = lax.axis_size("tx"), lax.axis_size("ty")
    tx, ty = lax.axis_index("tx"), lax.axis_index("ty")
    tiles = nx * ny
    sent = resample(
        granule_blocks, row_weights, column_bank, destination, window_index, bank_index, tiles
    )
    got = lax.all_to_all(sent, ("tx", "ty"), split_axis=0, concat_axis=0, tiled=True)
    gridded, turned = gather_windows(got)
    edges = jnp.stack([ty == 0, ty == ny - 1, tx == 0, tx == nx - 1]).astype(jnp.int32)
    bottleneck = encode(
        turned,
        rim(turned),
        edges,
        patch_weights(kernel_one),
        pair_weights(kernel_two),
        reduce_three.reshape(512, 256),
        kernel_three.reshape(3, 768, 256),
        reduce_four.reshape(1024, 512),
        kernel_four.reshape(3, 1536, 512),
        reduce_two.reshape(256, 128),
    )
    return (gridded, jnp.transpose(bottleneck.reshape(32, 16, 512), (2, 0, 1)))


def solution(mesh):
    in_specs = (
        P(("tx", "ty"), None, None, None),
        P(("tx", "ty"), None, None),
        P(),
        P(("tx", "ty")),
        P(("tx", "ty")),
        P(("tx", "ty")),
        P(),
        P(),
        P(),
        P(),
        P(),
        P(),
        P(),
    )
    out_specs = (P(None, "ty", "tx"), P(None, "ty", "tx"))
    return jax.shard_map(body, mesh=mesh, in_specs=in_specs, out_specs=out_specs, check_vma=False)
```

```python
import functools

import jax
import jax.numpy as jnp
import numpy as np
from jax import lax
from jax.experimental import pallas as pl
from jax.experimental.pallas import tpu as pltpu
from jax.sharding import PartitionSpec as P

MESH = pl.DeviceIdType.MESH
BANDS = 13
CAP = 2
WIN = 8
NWIN = 32
BR = BANDS * WIN
HALO = 16
BIG_VMEM = 58 << 20


def resample_kernel(
    dest,
    window,
    bank_index,
    raw,
    weights,
    bank,
    out,
    tiled_low,
    tiled_high,
    res,
    tags,
    tags_out,
    count,
    rank,
    sem,
    tag_sem,
):
    step = pl.program_id(0)
    per = raw.shape[0]
    held = res.shape[0]
    tiles = out.shape[0]
    lanes = BANDS * 16

    @pl.when(step == 0)
    def _():
        spread = (
            lax.broadcasted_iota(jnp.int32, (16, 256), 1) % 16
            == lax.broadcasted_iota(jnp.int32, (16, 256), 0)
        ).astype(jnp.bfloat16)
        for r in range(WIN):
            both = lax.dot_general(
                weights[r],
                spread,
                (((0,), (0,)), ((), ())),
                preferred_element_type=jnp.float32,
            )
            tiled_low[pl.ds(r, held, stride=WIN), :] = both[:, :128]
            tiled_high[pl.ds(r, held, stride=WIN), :] = both[:, 128:]
        tags[...] = jnp.full_like(tags, float(NWIN))

        @pl.loop(0, tiles // 8)
        def _(t):
            for u in range(8):
                count[t * 8 + u] = 0

        @pl.loop(0, held // 4)
        def _(group):
            for u in range(4):
                n = group * 4 + u
                tile = dest[n]
                place = count[tile]
                rank[n] = place
                count[tile] = place + 1
                tags[tile, pl.ds(place, 1), :] = jnp.full((1, 128), window[n], jnp.int32).astype(
                    jnp.float32
                )

        tags_out[...] = tags[...].astype(jnp.bfloat16)
        pltpu.make_async_copy(tags_out, out.at[:, pl.ds(CAP * BR, 8)], tag_sem).start()

    own_band = (
        lax.broadcasted_iota(jnp.int32, (BANDS, WIN, lanes), 2) // 16
        == lax.broadcasted_iota(jnp.int32, (BANDS, WIN, lanes), 0)
    )
    rowed = []
    for k in range(0, per, 2):
        pair = []
        for m in (k, k + 1):
            rows = pl.ds(pl.multiple_of((step * per + m) * WIN, WIN), WIN)
            row = jnp.concatenate([tiled_low[rows, :], tiled_high[rows, : lanes - 128]], axis=1)
            pair.append(jnp.where(own_band, row[None], 0.0))
        left = jnp.concatenate(pair, axis=0).reshape(2 * BR, lanes).astype(jnp.bfloat16)
        right = jnp.concatenate([raw[m].reshape(lanes, 128) for m in (k, k + 1)], axis=1)
        both = jnp.dot(left, right, preferred_element_type=jnp.float32)
        rowed.append(
            jnp.concatenate([both[:BR, :128], both[BR:, 128:]], axis=0).astype(jnp.bfloat16)
        )
    for k in range(0, per, 2):
        n = step * per + k
        right = jnp.concatenate([bank[bank_index[n]], bank[bank_index[n + 1]]], axis=1)
        both = jnp.dot(rowed[k // 2], right, preferred_element_type=jnp.float32)
        res[n] = both[:BR, :128].astype(jnp.bfloat16)
        res[n + 1] = both[BR:, 128:].astype(jnp.bfloat16)
    for k in range(per):
        n = step * per + k
        pltpu.make_async_copy(
            res.at[n], out.at[dest[n], pl.ds(pl.multiple_of(rank[n] * BR, 8), BR)], sem
        ).start()

    @pl.when(step == pl.num_programs(0) - 1)
    def _():
        pltpu.make_async_copy(res, res, sem).wait()
        pltpu.make_async_copy(tags_out, out.at[:, pl.ds(CAP * BR, 8)], tag_sem).wait()


def resample(raw, weights, bank, dest, window, bank_index, tiles):
    held = raw.shape[0]
    per = 32
    return pl.pallas_call(
        resample_kernel,
        grid=(held // per,),
        in_specs=[
            pl.BlockSpec(memory_space=pltpu.SMEM),
            pl.BlockSpec(memory_space=pltpu.SMEM),
            pl.BlockSpec(memory_space=pltpu.SMEM),
            pl.BlockSpec((per, BANDS, 16, 128), lambda i: (i, 0, 0, 0)),
            pl.BlockSpec((WIN, 16, held), lambda i: (0, 0, 0)),
            pl.BlockSpec(bank.shape, lambda i: (0, 0, 0)),
        ],
        out_specs=pl.BlockSpec(memory_space=pltpu.HBM),
        out_shape=jax.ShapeDtypeStruct((tiles, CAP * BR + 8, 128), jnp.bfloat16),
        scratch_shapes=[
            pltpu.VMEM(((held + 1) * WIN, 128), jnp.float32),
            pltpu.VMEM(((held + 1) * WIN, 128), jnp.float32),
            pltpu.VMEM((held, BR, 128), jnp.bfloat16),
            pltpu.VMEM((tiles, 8, 128), jnp.float32),
            pltpu.VMEM((tiles, 8, 128), jnp.bfloat16),
            pltpu.SMEM((tiles,), jnp.int32),
            pltpu.SMEM((held,), jnp.int32),
            pltpu.SemaphoreType.DMA,
            pltpu.SemaphoreType.DMA,
        ],
        compiler_params=pltpu.CompilerParams(vmem_limit_bytes=BIG_VMEM),
        name="resample",
    )(dest, window, bank_index, raw, jnp.transpose(weights, (1, 2, 0)), bank)


CHUNKS = 4
QUARTERS = 4


def gather_kernel(
    got,
    gridded_out,
    turned_out,
    held,
    gridded,
    turned,
    even,
    odd,
    tags,
    dense,
    window,
    inverse,
    tag_sem,
    dense_sem,
    chunk_sem,
    out_sem,
):
    tiles = got.shape[0]
    per = tiles // CHUNKS
    fetch = pltpu.make_async_copy(got.at[:, pl.ds(CAP * BR, 8)], tags, tag_sem)
    fetch.start()
    chunks = [
        pltpu.make_async_copy(
            got.at[pl.ds(i * per, per), pl.ds(0, CAP * BR)],
            held.at[pl.ds(i * per, per)],
            chunk_sem.at[i],
        )
        for i in range(CHUNKS)
    ]
    for chunk in chunks:
        chunk.start()
    even[...] = jnp.zeros_like(even)
    odd[...] = jnp.zeros_like(odd)
    fetch.wait()
    lane = lax.broadcasted_iota(jnp.int32, (8, 128), 1)
    total = jnp.zeros((8, 128), jnp.float32)
    for t in range(tiles):
        total = total + jnp.where(lane == t, tags[t].astype(jnp.float32), 0.0)
    dense[...] = total.astype(jnp.int32)
    scalars = pltpu.make_async_copy(dense, window, dense_sem)
    scalars.start()
    which = lax.broadcasted_iota(jnp.int32, (NWIN, 128), 0).astype(jnp.float32)
    hits = jnp.zeros((NWIN, 128), jnp.float32)
    for k in range(CAP):
        hits = hits + jnp.where(which == total[k : k + 1, :], 1.0, 0.0)
    counts = jnp.sum(hits, axis=1, keepdims=True)
    inverse[...] = jnp.broadcast_to(1.0 / jnp.maximum(counts, 1.0), (NWIN, 128))
    scalars.wait()

    for i in range(CHUNKS):
        chunks[i].wait()

        @pl.loop(0, per // 4)
        def _(group):
            for u in range(4):
                t = i * per + group * 4 + u
                for k, sums in ((0, even), (1, odd)):
                    sums[window[k, t]] += held[t, k * BR : (k + 1) * BR, :].astype(jnp.float32)

    pad = jnp.zeros((128 - BR, 128), jnp.float32)
    outs = []
    pairs = NWIN // 2 // QUARTERS
    for q in range(QUARTERS):
        for p in range(q * pairs, (q + 1) * pairs):
            pair = []
            for w in (2 * p, 2 * p + 1):
                mean = (even[w] + odd[w]) * inverse[w : w + 1, :]
                pair.append(mean)
                turned[w] = jnp.concatenate([mean, pad], axis=0).astype(jnp.bfloat16).T
            for b in range(BANDS):
                rows = slice(b * WIN, (b + 1) * WIN)
                gridded[b, p * 16 : (p + 1) * 16, :] = jnp.concatenate(
                    [pair[0][rows], pair[1][rows]], axis=0
                ).astype(jnp.bfloat16)
        wins = pl.ds(q * 2 * pairs, 2 * pairs)
        rows = pl.ds(q * 16 * pairs, 16 * pairs)
        outs.append(pltpu.make_async_copy(turned.at[wins], turned_out.at[wins], out_sem.at[q, 0]))
        outs.append(
            pltpu.make_async_copy(gridded.at[:, rows], gridded_out.at[:, rows], out_sem.at[q, 1])
        )
        outs[-2].start()
        outs[-1].start()
    for copy in outs:
        copy.wait()


def gather_windows(got):
    tiles = got.shape[0]
    hbm = pl.BlockSpec(memory_space=pltpu.HBM)
    grid_shape = (BANDS, NWIN * WIN, 128)
    turned_shape = (NWIN, 128, 128)
    return pl.pallas_call(
        gather_kernel,
        in_specs=[hbm],
        out_specs=[hbm, hbm],
        out_shape=[
            jax.ShapeDtypeStruct(grid_shape, jnp.bfloat16),
            jax.ShapeDtypeStruct(turned_shape, jnp.bfloat16),
        ],
        scratch_shapes=[
            pltpu.VMEM((tiles, CAP * BR, 128), jnp.bfloat16),
            pltpu.VMEM(grid_shape, jnp.bfloat16),
            pltpu.VMEM(turned_shape, jnp.bfloat16),
            pltpu.VMEM((NWIN + 1, BR, 128), jnp.float32),
            pltpu.VMEM((NWIN + 1, BR, 128), jnp.float32),
            pltpu.VMEM((tiles, 8, 128), jnp.bfloat16),
            pltpu.VMEM((8, 128), jnp.int32),
            pltpu.SMEM((8, 128), jnp.int32),
            pltpu.VMEM((NWIN, 128), jnp.float32),
            pltpu.SemaphoreType.DMA,
            pltpu.SemaphoreType.DMA,
            pltpu.SemaphoreType.DMA((CHUNKS,)),
            pltpu.SemaphoreType.DMA((QUARTERS, 2)),
        ],
        compiler_params=pltpu.CompilerParams(vmem_limit_bytes=BIG_VMEM),
        name="gather_windows",
    )(got)


HALO_WIN = HALO // WIN
WIDE_WIN = NWIN + 2 * HALO_WIN
WIDE_COL = 128 + 2 * HALO
MOVES = [(1, 0), (-1, 0), (0, 1), (0, -1), (1, 1), (1, -1), (-1, 1), (-1, -1)]


def rim_kernel(
    tile,
    rim_rows,
    rim_cols,
    edge_rows,
    edge_cols,
    zero_rows,
    zero_cols,
    edge_sem,
    zero_sem,
    send_sem,
    recv_sem,
):
    tx, ty = lax.axis_index("tx"), lax.axis_index("ty")
    nx, ny = lax.axis_size("tx"), lax.axis_size("ty")

    def inside(dx, dy):
        ok = None
        for d, at, n in ((dx, tx, nx), (dy, ty, ny)):
            if d:
                here = at + d >= 0 if d < 0 else at + d < n
                ok = here if ok is None else jnp.logical_and(ok, here)
        return ok

    def source(dx, dy):
        if dy == 0:
            return edge_cols.at[:, pl.ds(HALO if dx > 0 else 0, HALO)]
        c, cn = {-1: (0, HALO), 0: (0, 128), 1: (128 - HALO, HALO)}[dx]
        return edge_rows.at[pl.ds(HALO_WIN if dy > 0 else 0, HALO_WIN), pl.ds(c, cn)]

    def target(dx, dy):
        if dy == 0:
            return rim_cols.at[:, pl.ds(0 if dx > 0 else HALO, HALO)]
        c, cn = {-1: (HALO + 128, HALO), 0: (HALO, 128), 1: (0, HALO)}[dx]
        return rim_rows.at[pl.ds(0 if dy > 0 else HALO_WIN, HALO_WIN), pl.ds(c, cn)]

    barrier = pltpu.get_barrier_semaphore()
    for dx, dy in MOVES:

        @pl.when(inside(dx, dy))
        def _():
            pl.semaphore_signal(
                barrier, inc=1, device_id=(tx + dx, ty + dy), device_id_type=MESH
            )

    edges = [
        pltpu.make_async_copy(src, dst, edge_sem.at[i])
        for i, (src, dst) in enumerate(
            (
                (tile.at[pl.ds(0, HALO_WIN)], edge_rows.at[pl.ds(0, HALO_WIN)]),
                (
                    tile.at[pl.ds(NWIN - HALO_WIN, HALO_WIN)],
                    edge_rows.at[pl.ds(HALO_WIN, HALO_WIN)],
                ),
                (tile.at[:, pl.ds(0, HALO)], edge_cols.at[:, pl.ds(0, HALO)]),
                (tile.at[:, pl.ds(128 - HALO, HALO)], edge_cols.at[:, pl.ds(HALO, HALO)]),
            )
        )
    ]
    for edge in edges:
        edge.start()
    zero_rows[...] = jnp.zeros_like(zero_rows)
    zero_cols[...] = jnp.zeros_like(zero_cols)
    for edge in edges:
        edge.wait()
    peers = sum(inside(dx, dy).astype(jnp.int32) for dx, dy in MOVES)
    pl.semaphore_wait(barrier, peers)

    copies = []
    for i, (dx, dy) in enumerate(MOVES):
        send = pltpu.make_async_remote_copy(
            src_ref=source(dx, dy),
            dst_ref=target(dx, dy),
            send_sem=send_sem.at[i],
            recv_sem=recv_sem.at[i],
            device_id=(tx + dx, ty + dy),
            device_id_type=MESH,
        )
        zeros = zero_rows.at[:, pl.ds(0, HALO if dx else 128)] if dy else zero_cols
        blank = pltpu.make_async_copy(zeros, target(dx, dy), zero_sem.at[i])
        copies.append((send, blank, inside(dx, dy), inside(-dx, -dy)))
    for send, blank, goes, comes in copies:

        @pl.when(goes)
        def _():
            send.start()

        @pl.when(jnp.logical_not(comes))
        def _():
            blank.start()

    for send, blank, goes, comes in copies:

        @pl.when(goes)
        def _():
            send.wait_send()

        @pl.when(comes)
        def _():
            send.wait_recv()

        @pl.when(jnp.logical_not(comes))
        def _():
            blank.wait()


def rim(turned):
    moves = len(MOVES)
    return pl.pallas_call(
        rim_kernel,
        in_specs=[pl.BlockSpec(memory_space=pl.ANY)],
        out_specs=[pl.BlockSpec(memory_space=pl.ANY)] * 2,
        out_shape=[
            jax.ShapeDtypeStruct((2 * HALO_WIN, WIDE_COL, 128), jnp.bfloat16),
            jax.ShapeDtypeStruct((NWIN, 2 * HALO, 128), jnp.bfloat16),
        ],
        scratch_shapes=[
            pltpu.VMEM((2 * HALO_WIN, 128, 128), jnp.bfloat16),
            pltpu.VMEM((NWIN, 2 * HALO, 128), jnp.bfloat16),
            pltpu.VMEM((HALO_WIN, 128, 128), jnp.bfloat16),
            pltpu.VMEM((NWIN, HALO, 128), jnp.bfloat16),
            pltpu.SemaphoreType.DMA((4,)),
            pltpu.SemaphoreType.DMA((moves,)),
            pltpu.SemaphoreType.DMA((moves,)),
            pltpu.SemaphoreType.DMA((moves,)),
        ],
        compiler_params=pltpu.CompilerParams(
            collective_id=0, has_side_effects=True, vmem_limit_bytes=BIG_VMEM
        ),
        name="rim",
    )(turned)


FAR = 1 << 20
HALVES = 24
STEPS_ONE = 3
PAIRS = 40
PIX = 2 * PAIRS
ROWS_TWO = STEPS_ONE * HALVES
ROWS_THREE = 14
STEPS_THREE = 5
ROWS_FOUR = 17
STEPS_FOUR = 2
WIDE_FOUR = 24


def encoder_kernel(
    edges,
    tile,
    rim_rows,
    rim_cols,
    hbm_one,
    hbm_reduce_two,
    hbm_two,
    hbm_reduce_three,
    hbm_three,
    hbm_reduce_four,
    hbm_four,
    out,
    wide,
    slab,
    patch,
    even_two,
    odd_two,
    carry_two,
    even_three,
    odd_three,
    carry_three,
    spread_three,
    taps_four,
    weight_one,
    reduce_two,
    weight_two,
    reduce_three,
    weight_three,
    reduce_four,
    weight_four,
    sems,
    wide_sems,
):
    per = HALVES // 2
    parts = []
    for i in range(STEPS_ONE):
        low_win, high_win = max(i * per, HALO_WIN), min((i + 1) * per, HALO_WIN + NWIN)
        inner = pl.ds(low_win - HALO_WIN, high_win - low_win)
        outer = pl.ds(low_win, high_win - low_win)
        moves = [
            (tile.at[inner], wide.at[outer, pl.ds(HALO, 128)]),
            (rim_cols.at[inner, pl.ds(0, HALO)], wide.at[outer, pl.ds(0, HALO)]),
            (rim_cols.at[inner, pl.ds(HALO, HALO)], wide.at[outer, pl.ds(HALO + 128, HALO)]),
        ]
        if i == 0:
            moves.append((rim_rows.at[pl.ds(0, HALO_WIN)], wide.at[pl.ds(0, HALO_WIN)]))
        if i == STEPS_ONE - 1:
            moves.append(
                (rim_rows.at[pl.ds(HALO_WIN, HALO_WIN)], wide.at[pl.ds(WIDE_WIN - HALO_WIN, HALO_WIN)])
            )
        parts.append(
            [
                pltpu.make_async_copy(src, dst, wide_sems.at[i, j])
                for j, (src, dst) in enumerate(moves)
            ]
        )
    fetches = [
        pltpu.make_async_copy(source, target, sems.at[i])
        for i, (source, target) in enumerate(
            (
                (hbm_one, weight_one),
                (hbm_reduce_two, reduce_two),
                (hbm_two, weight_two),
                (hbm_reduce_three, reduce_three),
                (hbm_three, weight_three),
                (hbm_reduce_four, reduce_four),
                (hbm_four, weight_four),
            )
        )
    ]
    for copy in parts[0] + fetches[:2] + sum(parts[1:], []) + fetches[2:]:
        copy.start()

    def dot(a, b):
        return jnp.dot(a, b, preferred_element_type=jnp.float32)

    def bounds(tile_rows, tile_cols):
        return (
            jnp.where(edges[0] == 1, 0, -FAR),
            jnp.where(edges[1] == 1, tile_rows, FAR),
            jnp.where(edges[2] == 1, 0, -FAR),
            jnp.where(edges[3] == 1, tile_cols, FAR),
        )

    def on_map(value, row, col, limits):
        top, bottom, left, right = limits
        right = jnp.where(jnp.logical_and(row >= top, row < bottom), right, -FAR)
        return jnp.where(jnp.logical_and(col >= left, col < right), value, 0.0)

    def following(value, by):
        return pltpu.roll(value, value.shape[0] - by, 0)

    last = wide.shape[0] - 1
    cols = wide.shape[1]
    low = lax.broadcasted_iota(jnp.int32, (cols, 128), 1) % 8 < 4
    at = lax.broadcasted_iota(jnp.int32, (PIX, 128), 0)
    col_two = jnp.where(at < PAIRS, 2 * at, 2 * (at - PAIRS) + 1) - 7
    limits_two = bounds(128, 64)
    carry_two[...] = jnp.zeros_like(carry_two)
    for copy in parts[0] + fetches[:2]:
        copy.wait()

    @pl.loop(0, STEPS_ONE)
    def _(step):
        for i in range(1, STEPS_ONE):

            @pl.when(step == i - 1)
            def _():
                for copy in parts[i]:
                    copy.wait()

        for k in range(HALVES):
            w = step * (HALVES // 2) + k // 2
            here = wide[jnp.minimum(w, last)].astype(jnp.float32)
            if k % 2:
                after = wide[jnp.minimum(w + 1, last)].astype(jnp.float32)
                here = jnp.where(low, pltpu.roll(here, 124, 1), pltpu.roll(after, 4, 1))
            slab[k, pl.ds(0, cols), :] = here
            for q in range(4):
                both = [slab[k, pl.ds(first + q, PAIRS, stride=4), :] for first in (1, 3)]
                patch[k, :, q * 128 : (q + 1) * 128] = jnp.concatenate(both, axis=0).astype(
                    jnp.bfloat16
                )
        hidden = dot(patch[...].reshape(HALVES * PIX, 512), weight_one[...])
        hidden = jnp.maximum(hidden, 0.0).astype(jnp.bfloat16)
        down = [
            jnp.maximum(dot(hidden[:, e * 256 : (e + 1) * 256], reduce_two[...]), 0.0).reshape(
                HALVES, PIX, 128
            )
            for e in range(2)
        ]
        before = carry_two[...]
        for k in range(HALVES):
            h = step * HALVES + k
            lines = []
            for e in range(2):
                value = on_map(down[e][k], 2 * h + e - 7, col_two, limits_two)
                first, second = value[:PAIRS], value[PAIRS:]
                lines.append(
                    jnp.concatenate(
                        [first, second, following(first, 1), following(second, 1)], axis=1
                    )
                )
            even_two[h] = jnp.concatenate(lines, axis=0).astype(jnp.bfloat16)
            odd_two[h] = jnp.concatenate([before, lines[0]], axis=0).astype(jnp.bfloat16)
            before = lines[1]
        carry_two[...] = before

    fetches[2].wait()
    fetches[3].wait()
    col_three = lax.broadcasted_iota(jnp.int32, (PAIRS, 256), 0) - 3
    limits_three = bounds(64, 32)
    carry_three[...] = jnp.zeros_like(carry_three)
    size = ROWS_THREE * PIX

    @pl.loop(0, STEPS_THREE)
    def _(step):
        first = step * ROWS_THREE
        hidden = (
            dot(even_two[pl.ds(first, ROWS_THREE)].reshape(size, 512), weight_two[0])
            + dot(odd_two[pl.ds(first + 1, ROWS_THREE)].reshape(size, 512), weight_two[1])
            + dot(even_two[pl.ds(first + 1, ROWS_THREE)].reshape(size, 512), weight_two[2])
        )
        hidden = jnp.maximum(hidden, 0.0).reshape(ROWS_THREE, 2, PAIRS, 256)
        hidden = jnp.concatenate([hidden[:, 0], hidden[:, 1]], axis=-1)
        hidden = hidden.reshape(ROWS_THREE * PAIRS, 512).astype(jnp.bfloat16)
        down = jnp.maximum(dot(hidden, reduce_three[...]), 0.0).reshape(ROWS_THREE, PAIRS, 256)
        before = carry_three[...]
        for k in range(0, ROWS_THREE, 2):
            lines = []
            for e in range(2):
                value = on_map(down[k + e], first + k + e - 3, col_three, limits_three)
                lines.append(
                    jnp.concatenate([value, following(value, 1), following(value, 2)], axis=1)
                )
            i = step * (ROWS_THREE // 2) + k // 2
            even_three[i] = jnp.concatenate(lines, axis=0).astype(jnp.bfloat16)
            odd_three[i] = jnp.concatenate([before, lines[0]], axis=0).astype(jnp.bfloat16)
            before = lines[1]
        carry_three[...] = before

    fetches[4].wait()
    fetches[5].wait()
    col_four = lax.broadcasted_iota(jnp.int32, (WIDE_FOUR, 512), 0) - 1
    limits_four = bounds(32, 16)
    size_four = ROWS_FOUR * PIX

    @pl.loop(0, STEPS_FOUR)
    def _(step):
        first = step * ROWS_FOUR
        hidden = (
            dot(even_three[pl.ds(first, ROWS_FOUR)].reshape(size_four, 768), weight_three[0])
            + dot(odd_three[pl.ds(first + 1, ROWS_FOUR)].reshape(size_four, 768), weight_three[1])
            + dot(even_three[pl.ds(first + 1, ROWS_FOUR)].reshape(size_four, 768), weight_three[2])
        )
        hidden = jnp.maximum(hidden, 0.0)
        for half in range(2):
            spread_three[half, pl.ds(0, size_four), :] = hidden[:, half * 128 : (half + 1) * 128]
        rows = []
        for k in range(ROWS_FOUR):
            rows.append(
                jnp.concatenate(
                    [
                        spread_three[
                            half,
                            pl.ds(k * PIX + e * PAIRS + g, WIDE_FOUR, stride=2),
                            :,
                        ]
                        for e in range(2)
                        for g in range(2)
                        for half in range(2)
                    ],
                    axis=1,
                )
            )
        hidden = jnp.concatenate(rows, axis=0).astype(jnp.bfloat16)
        down = jnp.maximum(dot(hidden, reduce_four[...]), 0.0)
        for k in range(ROWS_FOUR):
            value = down[k * WIDE_FOUR : (k + 1) * WIDE_FOUR]
            value = on_map(value, first + k - 1, col_four, limits_four)
            taps_four[first + k] = jnp.concatenate(
                [value[:16], following(value, 1)[:16], following(value, 2)[:16]], axis=1
            ).astype(jnp.bfloat16)

    fetches[6].wait()
    for half in range(2):
        lanes = slice(half * 256, (half + 1) * 256)
        hidden = sum(
            dot(taps_four[u : u + 32].reshape(512, 1536), weight_four[u, :, lanes])
            for u in range(3)
        )
        out[:, lanes] = jnp.maximum(hidden, 0.0).astype(jnp.bfloat16)


def encode(tile, rims, edges, one, two, reduce_three, three, reduce_four, four, reduce_two):
    hbm = pl.BlockSpec(memory_space=pltpu.HBM)
    big = (one, reduce_two, two, reduce_three, three, reduce_four, four)
    return pl.pallas_call(
        encoder_kernel,
        in_specs=[pl.BlockSpec(memory_space=pltpu.SMEM)] + [hbm] * (3 + len(big)),
        out_specs=pl.BlockSpec(memory_space=pltpu.VMEM),
        out_shape=jax.ShapeDtypeStruct((512, 512), jnp.bfloat16),
        scratch_shapes=[
            pltpu.VMEM((WIDE_WIN, WIDE_COL, 128), jnp.bfloat16),
            pltpu.VMEM((HALVES, 168, 128), jnp.float32),
            pltpu.VMEM((HALVES, PIX, 512), jnp.bfloat16),
            pltpu.VMEM((ROWS_TWO, PIX, 512), jnp.bfloat16),
            pltpu.VMEM((ROWS_TWO, PIX, 512), jnp.bfloat16),
            pltpu.VMEM((PAIRS, 512), jnp.float32),
            pltpu.VMEM((STEPS_FOUR * ROWS_FOUR + 1, PIX, 768), jnp.bfloat16),
            pltpu.VMEM((STEPS_FOUR * ROWS_FOUR + 1, PIX, 768), jnp.bfloat16),
            pltpu.VMEM((PAIRS, 768), jnp.float32),
            pltpu.VMEM((2, ROWS_FOUR * PIX + 16, 128), jnp.float32),
            pltpu.VMEM((STEPS_FOUR * ROWS_FOUR, 16, 1536), jnp.bfloat16),
        ]
        + [pltpu.VMEM(w.shape, jnp.bfloat16) for w in big]
        + [pltpu.SemaphoreType.DMA((len(big),)), pltpu.SemaphoreType.DMA((STEPS_ONE, 4))],
        compiler_params=pltpu.CompilerParams(vmem_limit_bytes=BIG_VMEM),
        name="encoder",
    )(edges, tile, *rims, *big)


def patch_weights(kernel):
    rows = np.zeros((8, 4, 3), np.float32)
    for r in range(8):
        for y in range(4):
            u = r - (2 + y) + 1
            if 0 <= u < 3:
                rows[r, y, u] = 1
    cols = np.zeros((4, 2, 3), np.float32)
    for q in range(4):
        for g in range(2):
            v = q - g
            if 0 <= v < 3:
                cols[q, g, v] = 1
    spread = jnp.einsum("ryu,uvbo->rybvo", jnp.asarray(rows, jnp.bfloat16), kernel)
    spread = jnp.einsum("qgv,rybvo->qbrygo", jnp.asarray(cols, jnp.bfloat16), spread)
    spread = spread.reshape(4, BR, 512).astype(jnp.bfloat16)
    return jnp.pad(spread, ((0, 0), (0, 128 - BR), (0, 0))).reshape(512, 512)


def pair_weights(kernel):
    taps = jnp.stack(
        [jnp.pad(kernel, ((0, 0), (g, 1 - g), (0, 0), (0, 0))) for g in range(2)], axis=3
    )
    return taps.reshape(3, 512, 256)


def body(
    granule_blocks,
    row_weights,
    column_bank,
    destination,
    window_index,
    bank_index,
    kernel_one,
    reduce_two,
    kernel_two,
    reduce_three,
    kernel_three,
    reduce_four,
    kernel_four,
):
    nx, ny = lax.axis_size("tx"), lax.axis_size("ty")
    tx, ty = lax.axis_index("tx"), lax.axis_index("ty")
    tiles = nx * ny
    sent = resample(
        granule_blocks, row_weights, column_bank, destination, window_index, bank_index, tiles
    )
    got = lax.all_to_all(sent, ("tx", "ty"), split_axis=0, concat_axis=0, tiled=True)
    gridded, turned = gather_windows(got)
    edges = jnp.stack([ty == 0, ty == ny - 1, tx == 0, tx == nx - 1]).astype(jnp.int32)
    bottleneck = encode(
        turned,
        rim(turned),
        edges,
        patch_weights(kernel_one),
        pair_weights(kernel_two),
        reduce_three.reshape(512, 256),
        kernel_three.reshape(3, 768, 256),
        reduce_four.reshape(1024, 512),
        kernel_four.reshape(3, 1536, 512),
        reduce_two.reshape(256, 128),
    )
    return (gridded, jnp.transpose(bottleneck.reshape(32, 16, 512), (2, 0, 1)))


def solution(mesh):
    in_specs = (
        P(("tx", "ty"), None, None, None),
        P(("tx", "ty"), None, None),
        P(),
        P(("tx", "ty")),
        P(("tx", "ty")),
        P(("tx", "ty")),
        P(),
        P(),
        P(),
        P(),
        P(),
        P(),
        P(),
    )
    out_specs = (P(None, "ty", "tx"), P(None, "ty", "tx"))
    return jax.shard_map(body, mesh=mesh, in_specs=in_specs, out_specs=out_specs, check_vma=False)
```

```python
import functools

import jax
import jax.numpy as jnp
import numpy as np
from jax import lax
from jax.experimental import pallas as pl
from jax.experimental.pallas import tpu as pltpu
from jax.sharding import PartitionSpec as P

MESH = pl.DeviceIdType.MESH
BANDS = 13
CAP = 2
WIN = 8
NWIN = 32
BR = BANDS * WIN
HALO = 16
BIG_VMEM = 58 << 20


def resample_kernel(
    dest,
    window,
    bank_index,
    raw,
    weights,
    bank,
    out,
    tiled_low,
    tiled_high,
    res,
    tags,
    tags_out,
    count,
    rank,
    sem,
    tag_sem,
):
    step = pl.program_id(0)
    per = raw.shape[0]
    held = res.shape[0]
    tiles = out.shape[0]
    lanes = BANDS * 16

    @pl.when(step == 0)
    def _():
        spread = (
            lax.broadcasted_iota(jnp.int32, (16, 256), 1) % 16
            == lax.broadcasted_iota(jnp.int32, (16, 256), 0)
        ).astype(jnp.bfloat16)
        for r in range(WIN):
            both = lax.dot_general(
                weights[r],
                spread,
                (((0,), (0,)), ((), ())),
                preferred_element_type=jnp.float32,
            )
            tiled_low[pl.ds(r, held, stride=WIN), :] = both[:, :128]
            tiled_high[pl.ds(r, held, stride=WIN), :] = both[:, 128:]
        tags[...] = jnp.full_like(tags, float(NWIN))

        @pl.loop(0, tiles // 8)
        def _(t):
            for u in range(8):
                count[t * 8 + u] = 0

        @pl.loop(0, held // 4)
        def _(group):
            for u in range(4):
                n = group * 4 + u
                tile = dest[n]
                place = count[tile]
                rank[n] = place
                count[tile] = place + 1
                tags[tile, pl.ds(place, 1), :] = jnp.full((1, 128), window[n], jnp.int32).astype(
                    jnp.float32
                )

        tags_out[...] = tags[...].astype(jnp.bfloat16)
        pltpu.make_async_copy(tags_out, out.at[:, pl.ds(CAP * BR, 8)], tag_sem).start()

    own_band = (
        lax.broadcasted_iota(jnp.int32, (BANDS, WIN, lanes), 2) // 16
        == lax.broadcasted_iota(jnp.int32, (BANDS, WIN, lanes), 0)
    )
    rowed = []
    for k in range(0, per, 2):
        pair = []
        for m in (k, k + 1):
            rows = pl.ds(pl.multiple_of((step * per + m) * WIN, WIN), WIN)
            row = jnp.concatenate([tiled_low[rows, :], tiled_high[rows, : lanes - 128]], axis=1)
            pair.append(jnp.where(own_band, row[None], 0.0))
        left = jnp.concatenate(pair, axis=0).reshape(2 * BR, lanes).astype(jnp.bfloat16)
        right = jnp.concatenate([raw[m].reshape(lanes, 128) for m in (k, k + 1)], axis=1)
        both = jnp.dot(left, right, preferred_element_type=jnp.float32)
        rowed.append(
            jnp.concatenate([both[:BR, :128], both[BR:, 128:]], axis=0).astype(jnp.bfloat16)
        )
    for k in range(0, per, 2):
        n = step * per + k
        right = jnp.concatenate([bank[bank_index[n]], bank[bank_index[n + 1]]], axis=1)
        both = jnp.dot(rowed[k // 2], right, preferred_element_type=jnp.float32)
        res[n] = both[:BR, :128].astype(jnp.bfloat16)
        res[n + 1] = both[BR:, 128:].astype(jnp.bfloat16)
    for k in range(per):
        n = step * per + k
        pltpu.make_async_copy(
            res.at[n], out.at[dest[n], pl.ds(pl.multiple_of(rank[n] * BR, 8), BR)], sem
        ).start()

    @pl.when(step == pl.num_programs(0) - 1)
    def _():
        pltpu.make_async_copy(res, res, sem).wait()
        pltpu.make_async_copy(tags_out, out.at[:, pl.ds(CAP * BR, 8)], tag_sem).wait()


def resample(raw, weights, bank, dest, window, bank_index, tiles):
    held = raw.shape[0]
    per = 32
    return pl.pallas_call(
        resample_kernel,
        grid=(held // per,),
        in_specs=[
            pl.BlockSpec(memory_space=pltpu.SMEM),
            pl.BlockSpec(memory_space=pltpu.SMEM),
            pl.BlockSpec(memory_space=pltpu.SMEM),
            pl.BlockSpec((per, BANDS, 16, 128), lambda i: (i, 0, 0, 0)),
            pl.BlockSpec((WIN, 16, held), lambda i: (0, 0, 0)),
            pl.BlockSpec(bank.shape, lambda i: (0, 0, 0)),
        ],
        out_specs=pl.BlockSpec(memory_space=pltpu.HBM),
        out_shape=jax.ShapeDtypeStruct((tiles, CAP * BR + 8, 128), jnp.bfloat16),
        scratch_shapes=[
            pltpu.VMEM(((held + 1) * WIN, 128), jnp.float32),
            pltpu.VMEM(((held + 1) * WIN, 128), jnp.float32),
            pltpu.VMEM((held, BR, 128), jnp.bfloat16),
            pltpu.VMEM((tiles, 8, 128), jnp.float32),
            pltpu.VMEM((tiles, 8, 128), jnp.bfloat16),
            pltpu.SMEM((tiles,), jnp.int32),
            pltpu.SMEM((held,), jnp.int32),
            pltpu.SemaphoreType.DMA,
            pltpu.SemaphoreType.DMA,
        ],
        compiler_params=pltpu.CompilerParams(vmem_limit_bytes=BIG_VMEM),
        name="resample",
    )(dest, window, bank_index, raw, jnp.transpose(weights, (1, 2, 0)), bank)


CHUNKS = 4
QUARTERS = 2


def gather_kernel(
    got,
    gridded_out,
    turned_out,
    held,
    gridded,
    turned,
    even,
    odd,
    tags,
    dense,
    window,
    inverse,
    tag_sem,
    dense_sem,
    chunk_sem,
    out_sem,
):
    tiles = got.shape[0]
    per = tiles // CHUNKS
    fetch = pltpu.make_async_copy(got.at[:, pl.ds(CAP * BR, 8)], tags, tag_sem)
    fetch.start()
    chunks = [
        pltpu.make_async_copy(
            got.at[pl.ds(i * per, per), pl.ds(0, CAP * BR)],
            held.at[pl.ds(i * per, per)],
            chunk_sem.at[i],
        )
        for i in range(CHUNKS)
    ]
    for chunk in chunks:
        chunk.start()
    even[...] = jnp.zeros_like(even)
    odd[...] = jnp.zeros_like(odd)
    fetch.wait()
    lane = lax.broadcasted_iota(jnp.int32, (8, 128), 1)
    total = jnp.zeros((8, 128), jnp.float32)
    for t in range(tiles):
        total = total + jnp.where(lane == t, tags[t].astype(jnp.float32), 0.0)
    dense[...] = total.astype(jnp.int32)
    scalars = pltpu.make_async_copy(dense, window, dense_sem)
    scalars.start()
    which = lax.broadcasted_iota(jnp.int32, (NWIN, 128), 0).astype(jnp.float32)
    hits = jnp.zeros((NWIN, 128), jnp.float32)
    for k in range(CAP):
        hits = hits + jnp.where(which == total[k : k + 1, :], 1.0, 0.0)
    counts = jnp.sum(hits, axis=1, keepdims=True)
    inverse[...] = jnp.broadcast_to(1.0 / jnp.maximum(counts, 1.0), (NWIN, 128))
    scalars.wait()

    for i in range(CHUNKS):
        chunks[i].wait()

        @pl.loop(0, per // 4)
        def _(group):
            for u in range(4):
                t = i * per + group * 4 + u
                for k, sums in ((0, even), (1, odd)):
                    sums[window[k, t]] += held[t, k * BR : (k + 1) * BR, :].astype(jnp.float32)

    pad = jnp.zeros((128 - BR, 128), jnp.float32)
    outs = []
    pairs = NWIN // 2 // QUARTERS
    for q in range(QUARTERS):
        for p in range(q * pairs, (q + 1) * pairs):
            pair = []
            for w in (2 * p, 2 * p + 1):
                mean = (even[w] + odd[w]) * inverse[w : w + 1, :]
                pair.append(mean)
                turned[w] = jnp.concatenate([mean, pad], axis=0).astype(jnp.bfloat16).T
            for b in range(BANDS):
                rows = slice(b * WIN, (b + 1) * WIN)
                gridded[b, p * 16 : (p + 1) * 16, :] = jnp.concatenate(
                    [pair[0][rows], pair[1][rows]], axis=0
                ).astype(jnp.bfloat16)
        wins = pl.ds(q * 2 * pairs, 2 * pairs)
        rows = pl.ds(q * 16 * pairs, 16 * pairs)
        outs.append(pltpu.make_async_copy(turned.at[wins], turned_out.at[wins], out_sem.at[q, 0]))
        outs.append(
            pltpu.make_async_copy(gridded.at[:, rows], gridded_out.at[:, rows], out_sem.at[q, 1])
        )
        outs[-2].start()
        outs[-1].start()
    for copy in outs:
        copy.wait()


def gather_windows(got):
    tiles = got.shape[0]
    hbm = pl.BlockSpec(memory_space=pltpu.HBM)
    grid_shape = (BANDS, NWIN * WIN, 128)
    turned_shape = (NWIN, 128, 128)
    return pl.pallas_call(
        gather_kernel,
        in_specs=[hbm],
        out_specs=[hbm, hbm],
        out_shape=[
            jax.ShapeDtypeStruct(grid_shape, jnp.bfloat16),
            jax.ShapeDtypeStruct(turned_shape, jnp.bfloat16),
        ],
        scratch_shapes=[
            pltpu.VMEM((tiles, CAP * BR, 128), jnp.bfloat16),
            pltpu.VMEM(grid_shape, jnp.bfloat16),
            pltpu.VMEM(turned_shape, jnp.bfloat16),
            pltpu.VMEM((NWIN + 1, BR, 128), jnp.float32),
            pltpu.VMEM((NWIN + 1, BR, 128), jnp.float32),
            pltpu.VMEM((tiles, 8, 128), jnp.bfloat16),
            pltpu.VMEM((8, 128), jnp.int32),
            pltpu.SMEM((8, 128), jnp.int32),
            pltpu.VMEM((NWIN, 128), jnp.float32),
            pltpu.SemaphoreType.DMA,
            pltpu.SemaphoreType.DMA,
            pltpu.SemaphoreType.DMA((CHUNKS,)),
            pltpu.SemaphoreType.DMA((QUARTERS, 2)),
        ],
        compiler_params=pltpu.CompilerParams(vmem_limit_bytes=BIG_VMEM),
        name="gather_windows",
    )(got)


HALO_WIN = HALO // WIN
WIDE_WIN = NWIN + 2 * HALO_WIN
WIDE_COL = 128 + 2 * HALO
MOVES = [(1, 0), (-1, 0), (0, 1), (0, -1), (1, 1), (1, -1), (-1, 1), (-1, -1)]


def rim_kernel(
    tile,
    rim_rows,
    rim_cols,
    edge_rows,
    edge_cols,
    zero_rows,
    zero_cols,
    edge_sem,
    zero_sem,
    send_sem,
    recv_sem,
):
    tx, ty = lax.axis_index("tx"), lax.axis_index("ty")
    nx, ny = lax.axis_size("tx"), lax.axis_size("ty")

    def inside(dx, dy):
        ok = None
        for d, at, n in ((dx, tx, nx), (dy, ty, ny)):
            if d:
                here = at + d >= 0 if d < 0 else at + d < n
                ok = here if ok is None else jnp.logical_and(ok, here)
        return ok

    def source(dx, dy):
        if dy == 0:
            return edge_cols.at[:, pl.ds(HALO if dx > 0 else 0, HALO)]
        c, cn = {-1: (0, HALO), 0: (0, 128), 1: (128 - HALO, HALO)}[dx]
        return edge_rows.at[pl.ds(HALO_WIN if dy > 0 else 0, HALO_WIN), pl.ds(c, cn)]

    def target(dx, dy):
        if dy == 0:
            return rim_cols.at[:, pl.ds(0 if dx > 0 else HALO, HALO)]
        c, cn = {-1: (HALO + 128, HALO), 0: (HALO, 128), 1: (0, HALO)}[dx]
        return rim_rows.at[pl.ds(0 if dy > 0 else HALO_WIN, HALO_WIN), pl.ds(c, cn)]

    barrier = pltpu.get_barrier_semaphore()
    for dx, dy in MOVES:

        @pl.when(inside(dx, dy))
        def _():
            pl.semaphore_signal(
                barrier, inc=1, device_id=(tx + dx, ty + dy), device_id_type=MESH
            )

    edges = [
        pltpu.make_async_copy(src, dst, edge_sem.at[i])
        for i, (src, dst) in enumerate(
            (
                (tile.at[pl.ds(0, HALO_WIN)], edge_rows.at[pl.ds(0, HALO_WIN)]),
                (
                    tile.at[pl.ds(NWIN - HALO_WIN, HALO_WIN)],
                    edge_rows.at[pl.ds(HALO_WIN, HALO_WIN)],
                ),
                (tile.at[:, pl.ds(0, HALO)], edge_cols.at[:, pl.ds(0, HALO)]),
                (tile.at[:, pl.ds(128 - HALO, HALO)], edge_cols.at[:, pl.ds(HALO, HALO)]),
            )
        )
    ]
    for edge in edges:
        edge.start()
    zero_rows[...] = jnp.zeros_like(zero_rows)
    zero_cols[...] = jnp.zeros_like(zero_cols)
    for edge in edges:
        edge.wait()
    peers = sum(inside(dx, dy).astype(jnp.int32) for dx, dy in MOVES)
    pl.semaphore_wait(barrier, peers)

    copies = []
    for i, (dx, dy) in enumerate(MOVES):
        send = pltpu.make_async_remote_copy(
            src_ref=source(dx, dy),
            dst_ref=target(dx, dy),
            send_sem=send_sem.at[i],
            recv_sem=recv_sem.at[i],
            device_id=(tx + dx, ty + dy),
            device_id_type=MESH,
        )
        zeros = zero_rows.at[:, pl.ds(0, HALO if dx else 128)] if dy else zero_cols
        blank = pltpu.make_async_copy(zeros, target(dx, dy), zero_sem.at[i])
        copies.append((send, blank, inside(dx, dy), inside(-dx, -dy)))
    for send, blank, goes, comes in copies:

        @pl.when(goes)
        def _():
            send.start()

        @pl.when(jnp.logical_not(comes))
        def _():
            blank.start()

    for send, blank, goes, comes in copies:

        @pl.when(goes)
        def _():
            send.wait_send()

        @pl.when(comes)
        def _():
            send.wait_recv()

        @pl.when(jnp.logical_not(comes))
        def _():
            blank.wait()


def rim(turned):
    moves = len(MOVES)
    return pl.pallas_call(
        rim_kernel,
        in_specs=[pl.BlockSpec(memory_space=pl.ANY)],
        out_specs=[pl.BlockSpec(memory_space=pl.ANY)] * 2,
        out_shape=[
            jax.ShapeDtypeStruct((2 * HALO_WIN, WIDE_COL, 128), jnp.bfloat16),
            jax.ShapeDtypeStruct((NWIN, 2 * HALO, 128), jnp.bfloat16),
        ],
        scratch_shapes=[
            pltpu.VMEM((2 * HALO_WIN, 128, 128), jnp.bfloat16),
            pltpu.VMEM((NWIN, 2 * HALO, 128), jnp.bfloat16),
            pltpu.VMEM((HALO_WIN, 128, 128), jnp.bfloat16),
            pltpu.VMEM((NWIN, HALO, 128), jnp.bfloat16),
            pltpu.SemaphoreType.DMA((4,)),
            pltpu.SemaphoreType.DMA((moves,)),
            pltpu.SemaphoreType.DMA((moves,)),
            pltpu.SemaphoreType.DMA((moves,)),
        ],
        compiler_params=pltpu.CompilerParams(
            collective_id=0, has_side_effects=True, vmem_limit_bytes=BIG_VMEM
        ),
        name="rim",
    )(turned)


FAR = 1 << 20
HALVES = 24
STEPS_ONE = 3
PAIRS = 40
PIX = 2 * PAIRS
ROWS_TWO = STEPS_ONE * HALVES
ROWS_THREE = 14
STEPS_THREE = 5
ROWS_FOUR = 17
STEPS_FOUR = 2
WIDE_FOUR = 24


def encoder_kernel(
    edges,
    tile,
    rim_rows,
    rim_cols,
    hbm_one,
    hbm_reduce_two,
    hbm_two,
    hbm_reduce_three,
    hbm_three,
    hbm_reduce_four,
    hbm_four,
    out,
    wide,
    slab,
    patch,
    even_two,
    odd_two,
    carry_two,
    even_three,
    odd_three,
    carry_three,
    spread_three,
    taps_four,
    weight_one,
    reduce_two,
    weight_two,
    reduce_three,
    weight_three,
    reduce_four,
    weight_four,
    sems,
    wide_sems,
):
    per = HALVES // 2
    parts = []
    for i in range(STEPS_ONE):
        low_win, high_win = max(i * per, HALO_WIN), min((i + 1) * per, HALO_WIN + NWIN)
        inner = pl.ds(low_win - HALO_WIN, high_win - low_win)
        outer = pl.ds(low_win, high_win - low_win)
        moves = [
            (tile.at[inner], wide.at[outer, pl.ds(HALO, 128)]),
            (rim_cols.at[inner, pl.ds(0, HALO)], wide.at[outer, pl.ds(0, HALO)]),
            (rim_cols.at[inner, pl.ds(HALO, HALO)], wide.at[outer, pl.ds(HALO + 128, HALO)]),
        ]
        if i == 0:
            moves.append((rim_rows.at[pl.ds(0, HALO_WIN)], wide.at[pl.ds(0, HALO_WIN)]))
        if i == STEPS_ONE - 1:
            moves.append(
                (rim_rows.at[pl.ds(HALO_WIN, HALO_WIN)], wide.at[pl.ds(WIDE_WIN - HALO_WIN, HALO_WIN)])
            )
        parts.append(
            [
                pltpu.make_async_copy(src, dst, wide_sems.at[i, j])
                for j, (src, dst) in enumerate(moves)
            ]
        )
    fetches = [
        pltpu.make_async_copy(source, target, sems.at[i])
        for i, (source, target) in enumerate(
            (
                (hbm_one, weight_one),
                (hbm_reduce_two, reduce_two),
                (hbm_two, weight_two),
                (hbm_reduce_three, reduce_three),
                (hbm_three, weight_three),
                (hbm_reduce_four, reduce_four),
                (hbm_four, weight_four),
            )
        )
    ]
    for copy in parts[0] + fetches[:2] + sum(parts[1:], []) + fetches[2:]:
        copy.start()

    def dot(a, b):
        return jnp.dot(a, b, preferred_element_type=jnp.float32)

    def bounds(tile_rows, tile_cols):
        return (
            jnp.where(edges[0] == 1, 0, -FAR),
            jnp.where(edges[1] == 1, tile_rows, FAR),
            jnp.where(edges[2] == 1, 0, -FAR),
            jnp.where(edges[3] == 1, tile_cols, FAR),
        )

    def on_map(value, row, col, limits):
        top, bottom, left, right = limits
        right = jnp.where(jnp.logical_and(row >= top, row < bottom), right, -FAR)
        return jnp.where(jnp.logical_and(col >= left, col < right), value, 0.0)

    def following(value, by):
        return pltpu.roll(value, value.shape[0] - by, 0)

    last = wide.shape[0] - 1
    cols = wide.shape[1]
    low = lax.broadcasted_iota(jnp.int32, (cols, 128), 1) % 8 < 4
    at = lax.broadcasted_iota(jnp.int32, (PIX, 128), 0)
    col_two = jnp.where(at < PAIRS, 2 * at, 2 * (at - PAIRS) + 1) - 7
    limits_two = bounds(128, 64)
    carry_two[...] = jnp.zeros_like(carry_two)
    for copy in parts[0] + fetches[:2]:
        copy.wait()

    @pl.loop(0, STEPS_ONE)
    def _(step):
        for i in range(1, STEPS_ONE):

            @pl.when(step == i - 1)
            def _():
                for copy in parts[i]:
                    copy.wait()

        for k in range(HALVES):
            w = step * (HALVES // 2) + k // 2
            here = wide[jnp.minimum(w, last)].astype(jnp.float32)
            if k % 2:
                after = wide[jnp.minimum(w + 1, last)].astype(jnp.float32)
                here = jnp.where(low, pltpu.roll(here, 124, 1), pltpu.roll(after, 4, 1))
            slab[k, pl.ds(0, cols), :] = here
            for q in range(4):
                both = [slab[k, pl.ds(first + q, PAIRS, stride=4), :] for first in (1, 3)]
                patch[k, :, q * 128 : (q + 1) * 128] = jnp.concatenate(both, axis=0).astype(
                    jnp.bfloat16
                )
        hidden = dot(patch[...].reshape(HALVES * PIX, 512), weight_one[...])
        hidden = jnp.maximum(hidden, 0.0).astype(jnp.bfloat16)
        down = [
            jnp.maximum(dot(hidden[:, e * 256 : (e + 1) * 256], reduce_two[...]), 0.0).reshape(
                HALVES, PIX, 128
            )
            for e in range(2)
        ]
        before = carry_two[...]
        for k in range(HALVES):
            h = step * HALVES + k
            lines = []
            for e in range(2):
                value = on_map(down[e][k], 2 * h + e - 7, col_two, limits_two)
                first, second = value[:PAIRS], value[PAIRS:]
                lines.append(
                    jnp.concatenate(
                        [first, second, following(first, 1), following(second, 1)], axis=1
                    )
                )
            even_two[h] = jnp.concatenate(lines, axis=0).astype(jnp.bfloat16)
            odd_two[h] = jnp.concatenate([before, lines[0]], axis=0).astype(jnp.bfloat16)
            before = lines[1]
        carry_two[...] = before

    fetches[2].wait()
    fetches[3].wait()
    col_three = lax.broadcasted_iota(jnp.int32, (PAIRS, 256), 0) - 3
    limits_three = bounds(64, 32)
    carry_three[...] = jnp.zeros_like(carry_three)
    size = ROWS_THREE * PIX

    @pl.loop(0, STEPS_THREE)
    def _(step):
        first = step * ROWS_THREE
        hidden = (
            dot(even_two[pl.ds(first, ROWS_THREE)].reshape(size, 512), weight_two[0])
            + dot(odd_two[pl.ds(first + 1, ROWS_THREE)].reshape(size, 512), weight_two[1])
            + dot(even_two[pl.ds(first + 1, ROWS_THREE)].reshape(size, 512), weight_two[2])
        )
        hidden = jnp.maximum(hidden, 0.0).reshape(ROWS_THREE, 2, PAIRS, 256)
        hidden = jnp.concatenate([hidden[:, 0], hidden[:, 1]], axis=-1)
        hidden = hidden.reshape(ROWS_THREE * PAIRS, 512).astype(jnp.bfloat16)
        down = jnp.maximum(dot(hidden, reduce_three[...]), 0.0).reshape(ROWS_THREE, PAIRS, 256)
        before = carry_three[...]
        for k in range(0, ROWS_THREE, 2):
            lines = []
            for e in range(2):
                value = on_map(down[k + e], first + k + e - 3, col_three, limits_three)
                lines.append(
                    jnp.concatenate([value, following(value, 1), following(value, 2)], axis=1)
                )
            i = step * (ROWS_THREE // 2) + k // 2
            even_three[i] = jnp.concatenate(lines, axis=0).astype(jnp.bfloat16)
            odd_three[i] = jnp.concatenate([before, lines[0]], axis=0).astype(jnp.bfloat16)
            before = lines[1]
        carry_three[...] = before

    fetches[4].wait()
    fetches[5].wait()
    col_four = lax.broadcasted_iota(jnp.int32, (WIDE_FOUR, 512), 0) - 1
    limits_four = bounds(32, 16)
    size_four = ROWS_FOUR * PIX

    @pl.loop(0, STEPS_FOUR)
    def _(step):
        first = step * ROWS_FOUR
        hidden = (
            dot(even_three[pl.ds(first, ROWS_FOUR)].reshape(size_four, 768), weight_three[0])
            + dot(odd_three[pl.ds(first + 1, ROWS_FOUR)].reshape(size_four, 768), weight_three[1])
            + dot(even_three[pl.ds(first + 1, ROWS_FOUR)].reshape(size_four, 768), weight_three[2])
        )
        hidden = jnp.maximum(hidden, 0.0)
        for half in range(2):
            spread_three[half, pl.ds(0, size_four), :] = hidden[:, half * 128 : (half + 1) * 128]
        rows = []
        for k in range(ROWS_FOUR):
            rows.append(
                jnp.concatenate(
                    [
                        spread_three[
                            half,
                            pl.ds(k * PIX + e * PAIRS + g, WIDE_FOUR, stride=2),
                            :,
                        ]
                        for e in range(2)
                        for g in range(2)
                        for half in range(2)
                    ],
                    axis=1,
                )
            )
        hidden = jnp.concatenate(rows, axis=0).astype(jnp.bfloat16)
        down = jnp.maximum(dot(hidden, reduce_four[...]), 0.0)
        for k in range(ROWS_FOUR):
            value = down[k * WIDE_FOUR : (k + 1) * WIDE_FOUR]
            value = on_map(value, first + k - 1, col_four, limits_four)
            taps_four[first + k] = jnp.concatenate(
                [value[:16], following(value, 1)[:16], following(value, 2)[:16]], axis=1
            ).astype(jnp.bfloat16)

    fetches[6].wait()
    for half in range(2):
        lanes = slice(half * 256, (half + 1) * 256)
        hidden = sum(
            dot(taps_four[u : u + 32].reshape(512, 1536), weight_four[u, :, lanes])
            for u in range(3)
        )
        out[:, lanes] = jnp.maximum(hidden, 0.0).astype(jnp.bfloat16)


def encode(tile, rims, edges, one, two, reduce_three, three, reduce_four, four, reduce_two):
    hbm = pl.BlockSpec(memory_space=pltpu.HBM)
    big = (one, reduce_two, two, reduce_three, three, reduce_four, four)
    return pl.pallas_call(
        encoder_kernel,
        in_specs=[pl.BlockSpec(memory_space=pltpu.SMEM)] + [hbm] * (3 + len(big)),
        out_specs=pl.BlockSpec(memory_space=pltpu.VMEM),
        out_shape=jax.ShapeDtypeStruct((512, 512), jnp.bfloat16),
        scratch_shapes=[
            pltpu.VMEM((WIDE_WIN, WIDE_COL, 128), jnp.bfloat16),
            pltpu.VMEM((HALVES, 168, 128), jnp.float32),
            pltpu.VMEM((HALVES, PIX, 512), jnp.bfloat16),
            pltpu.VMEM((ROWS_TWO, PIX, 512), jnp.bfloat16),
            pltpu.VMEM((ROWS_TWO, PIX, 512), jnp.bfloat16),
            pltpu.VMEM((PAIRS, 512), jnp.float32),
            pltpu.VMEM((STEPS_FOUR * ROWS_FOUR + 1, PIX, 768), jnp.bfloat16),
            pltpu.VMEM((STEPS_FOUR * ROWS_FOUR + 1, PIX, 768), jnp.bfloat16),
            pltpu.VMEM((PAIRS, 768), jnp.float32),
            pltpu.VMEM((2, ROWS_FOUR * PIX + 16, 128), jnp.float32),
            pltpu.VMEM((STEPS_FOUR * ROWS_FOUR, 16, 1536), jnp.bfloat16),
        ]
        + [pltpu.VMEM(w.shape, jnp.bfloat16) for w in big]
        + [pltpu.SemaphoreType.DMA((len(big),)), pltpu.SemaphoreType.DMA((STEPS_ONE, 4))],
        compiler_params=pltpu.CompilerParams(vmem_limit_bytes=BIG_VMEM),
        name="encoder",
    )(edges, tile, *rims, *big)


def patch_weights(kernel):
    rows = np.zeros((8, 4, 3), np.float32)
    for r in range(8):
        for y in range(4):
            u = r - (2 + y) + 1
            if 0 <= u < 3:
                rows[r, y, u] = 1
    cols = np.zeros((4, 2, 3), np.float32)
    for q in range(4):
        for g in range(2):
            v = q - g
            if 0 <= v < 3:
                cols[q, g, v] = 1
    spread = jnp.einsum("ryu,uvbo->rybvo", jnp.asarray(rows, jnp.bfloat16), kernel)
    spread = jnp.einsum("qgv,rybvo->qbrygo", jnp.asarray(cols, jnp.bfloat16), spread)
    spread = spread.reshape(4, BR, 512).astype(jnp.bfloat16)
    return jnp.pad(spread, ((0, 0), (0, 128 - BR), (0, 0))).reshape(512, 512)


def pair_weights(kernel):
    taps = jnp.stack(
        [jnp.pad(kernel, ((0, 0), (g, 1 - g), (0, 0), (0, 0))) for g in range(2)], axis=3
    )
    return taps.reshape(3, 512, 256)


def body(
    granule_blocks,
    row_weights,
    column_bank,
    destination,
    window_index,
    bank_index,
    kernel_one,
    reduce_two,
    kernel_two,
    reduce_three,
    kernel_three,
    reduce_four,
    kernel_four,
):
    nx, ny = lax.axis_size("tx"), lax.axis_size("ty")
    tx, ty = lax.axis_index("tx"), lax.axis_index("ty")
    tiles = nx * ny
    sent = resample(
        granule_blocks, row_weights, column_bank, destination, window_index, bank_index, tiles
    )
    got = lax.all_to_all(sent, ("tx", "ty"), split_axis=0, concat_axis=0, tiled=True)
    gridded, turned = gather_windows(got)
    edges = jnp.stack([ty == 0, ty == ny - 1, tx == 0, tx == nx - 1]).astype(jnp.int32)
    bottleneck = encode(
        turned,
        rim(turned),
        edges,
        patch_weights(kernel_one),
        pair_weights(kernel_two),
        reduce_three.reshape(512, 256),
        kernel_three.reshape(3, 768, 256),
        reduce_four.reshape(1024, 512),
        kernel_four.reshape(3, 1536, 512),
        reduce_two.reshape(256, 128),
    )
    return (gridded, jnp.transpose(bottleneck.reshape(32, 16, 512), (2, 0, 1)))


def solution(mesh):
    in_specs = (
        P(("tx", "ty"), None, None, None),
        P(("tx", "ty"), None, None),
        P(),
        P(("tx", "ty")),
        P(("tx", "ty")),
        P(("tx", "ty")),
        P(),
        P(),
        P(),
        P(),
        P(),
        P(),
        P(),
    )
    out_specs = (P(None, "ty", "tx"), P(None, "ty", "tx"))
    return jax.shard_map(body, mesh=mesh, in_specs=in_specs, out_specs=out_specs, check_vma=False)
```
